32 devices in a mesh: ctx: 8 (over z, y), uly: 4 (over x, core).
Axes of the slice: x: 2, y: 2, z: 4, core: 2. Of those that a mesh axis runs over, the one named last changes fastest.
Arguments:
- byte_embed: bfloat16 [24576, 768], P(('ctx', 'uly')), may hold values from -6 to 6
- query_weight: bfloat16 [768, 768], P(('ctx', 'uly')), may hold values from -0.109375 to 0.109375
- key_weight: bfloat16 [768, 768], P(('ctx', 'uly')), may hold values from -0.109375 to 0.109375
- value_weight: bfloat16 [768, 768], P(('ctx', 'uly')), may hold values from -0.21875 to 0.21875
- merge_weight: bfloat16 [768, 768], P(('ctx', 'uly')), may hold values from -0.625 to 0.625
- gate_weight: bfloat16 [768, 2048], P(('ctx', 'uly')), may hold values from -0.21875 to 0.21875
- up_weight: bfloat16 [768, 2048], P(('ctx', 'uly')), may hold values from -0.21875 to 0.21875
- down_weight: bfloat16 [2048, 768], P(('ctx', 'uly')), may hold values from -0.25 to 0.25
- conv_weight: float32 [5, 768], replicated, may hold values from -3 to 3
- score_weight: float32 [768], replicated, may hold values from -0.4375 to 0.4375
- attn_gain: float32 [768], replicated, may hold values from 0.1 to 1.9
- ffn_gain: float32 [768], replicated, may hold values from 0.1 to 1.9
- bias_table: float32 [32, 12], replicated, may hold values from -4 to 4
- doc_lengths: int32 [23], replicated, may hold values from 1 to 2048, as said below
- rel_bucket: int32 [2047], replicated, may hold values from 0 to 31
- out_grad: bfloat16 [12288, 768], P(('ctx', 'uly')), may hold values from -6 to 6
Outputs:
- layer_out: bfloat16 [12288, 768], P(('ctx', 'uly'))
- embed_grad: float32 [24576, 768], P(('ctx', 'uly'))
- query_grad: float32 [768, 768], P(('ctx', 'uly'))
- key_grad: float32 [768, 768], P(('ctx', 'uly'))
- value_grad: float32 [768, 768], P(('ctx', 'uly'))
- merge_grad: float32 [768, 768], P(('ctx', 'uly'))
- gate_grad: float32 [768, 2048], P(('ctx', 'uly'))
- up_grad: float32 [768, 2048], P(('ctx', 'uly'))
- down_grad: float32 [2048, 768], P(('ctx', 'uly'))
- conv_grad: float32 [5, 768], replicated
- score_grad: float32 [768], replicated
- attn_gain_grad: float32 [768], replicated
- ffn_gain_grad: float32 [768], replicated
- table_grad: float32 [32, 12], replicated
The draws below stay inside these ranges and needn't reach their ends.
Inputs may be any that keep to these rules, and one draw needn't show every extreme that they name: `doc_lengths`: the documents lie end to end over the 24576 bytes in this order; the longest has exactly 2048 bytes; at every multiple of 3072 inside the stream a document of exactly 2048 bytes begins between 768 and 1280 bytes before it. `rel_bucket`: entry r is the bucket of the key-minus-query offset r - 1023.
All inputs are finite; a program needn't handle non-finite values.
Results may differ from the reference program's by a relative error of at most 0.02.
Values may be sent and summed in bfloat16 or wider, within the bound.
No kernel may reach another device: no remote copies, remote signals or barrier semaphores. Data moves between devices by JAX's collectives and lax.ppermute only.
A program may use at most 448 MiB of HBM per device.

```python
import jax
import jax.numpy as jnp
from jax import lax

D = 768
HEADS = 12
HEAD_DIM = 64
FF = 2048
NBUCK = 32
CONV = 5
QBLK = 768
DOC_BYTES = 2048
TOK_DEV = 384
DOC_TOK = 1024
BYTES = 24576
TOKENS = 12288
GRP_BYTES = 3072
DOCS_FREE = 2
NDOCS = 23
N_CTX = 8
N_ULY = 4


def draw_doc_lengths(key, part):
    groups = BYTES // GRP_BYTES
    reach_lo = 3 * DOC_BYTES // 8
    reach_hi = 5 * DOC_BYTES // 8
    reach = jax.random.randint(key, (groups - 1,), reach_lo, reach_hi + 1).astype(jnp.int32)
    bounds = GRP_BYTES * jnp.arange(1, groups, dtype=jnp.int32)
    cross_start = bounds - reach
    cross_end = cross_start + DOC_BYTES
    free_lo = jnp.concatenate([jnp.zeros((1,), jnp.int32), cross_end])
    free_hi = jnp.concatenate([cross_start, jnp.full((1,), BYTES, jnp.int32)])
    free_len = free_hi - free_lo
    places = jnp.arange(DOCS_FREE, dtype=jnp.int32)
    pieces = free_len[:, None] // DOCS_FREE + (places[None, :] < (free_len % DOCS_FREE)[:, None]).astype(jnp.int32)
    crossing = jnp.full((groups, 1), DOC_BYTES, jnp.int32)
    table = jnp.concatenate([pieces, crossing], axis=1).reshape(-1)
    return table[:NDOCS].astype(jnp.int32)


def with_ends(result, own_key, smallest, top_value):
    shape = result.shape
    index_at = [jax.random.randint(jax.random.fold_in(own_key, axis), (), 0, shape[axis]) for axis in range(len(shape))]
    result = result.at[tuple(index_at)].set(smallest)
    longest = shape.index(max(shape))
    index_at[longest] = (index_at[longest] + 1) % shape[longest]
    return result.at[tuple(index_at)].set(top_value)


def levels(key, dims, shards, smallest, largest):
    level = 1.0
    for axis_at, blocks in shards:
        heights = jax.random.uniform(jax.random.fold_in(jax.random.fold_in(key, 6), axis_at), (blocks,), jnp.float32, smallest / len(shards), largest / len(shards))
        level = level * jnp.repeat(jnp.exp(heights), dims[axis_at] // blocks).reshape((-1,) + (1,) * (len(dims) - 1 - axis_at))
    return level


def noise(stream_key, shape, deviation, most, shards=(), held_as=jnp.bfloat16):
    level = levels(stream_key, shape, shards, -0.22, 0.18) if shards else 1.0
    drawn = jax.random.normal(stream_key, shape, jnp.float32) * deviation * level
    return jnp.minimum(jnp.maximum(drawn, -most), most).astype(held_as)


def setup_inputs(seed: int = 0) -> dict:
    key_list = jax.random.split(jax.random.key(seed), 17)
    return {
        "byte_embed": noise(key_list[0], (BYTES, D), 1.0, 6.0, ((0, 32),)),
        "query_weight": noise(key_list[1], (D, D), (4 * D) ** -0.5, 0.109375, ((0, 32),)),
        "key_weight": noise(key_list[2], (D, D), (4 * D) ** -0.5, 0.109375, ((0, 32),)),
        "value_weight": noise(key_list[3], (D, D), D ** -0.5, 0.21875, ((0, 32),)),
        "merge_weight": noise(key_list[4], (D, D), (D // 8) ** -0.5, 0.625, ((0, 32),)),
        "gate_weight": noise(key_list[5], (D, FF), D ** -0.5, 0.21875, ((0, 32),)),
        "up_weight": noise(key_list[6], (D, FF), D ** -0.5, 0.21875, ((0, 32),)),
        "down_weight": noise(key_list[7], (FF, D), (FF // 4) ** -0.5, 0.25, ((0, 32),)),
        "conv_weight": noise(key_list[8], (CONV, D), 0.5, 3.0, (), jnp.float32),
        "score_weight": noise(key_list[9], (D,), (D // 4) ** -0.5, 0.4375, (), jnp.float32),
        "attn_gain": jnp.clip(1.0 + 0.18 * jax.random.normal(key_list[10], (D,), jnp.float32), 0.1, 1.9),
        "ffn_gain": jnp.clip(1.0 + 0.18 * jax.random.normal(key_list[11], (D,), jnp.float32), 0.1, 1.9),
        "bias_table": noise(key_list[12], (NBUCK, HEADS), 1.0, 4.0, (), jnp.float32),
        "doc_lengths": draw_doc_lengths(jax.random.fold_in(key_list[16], 71), 0),
        "rel_bucket": with_ends(jax.random.randint(key_list[14], (2 * DOC_TOK - 1,), 0, NBUCK), jax.random.fold_in(key_list[14], 1), 0, NBUCK - 1).astype(jnp.int32),
        "out_grad": noise(key_list[15], (TOKENS, D), 1.0, 6.0, ((0, 32),)),
    }


epsilon = 1e-06
highest = lax.Precision.HIGHEST
masked_score = -1e+30

@jax.custom_vjp
def low(v):
    return lax.optimization_barrier(v.astype(jnp.bfloat16)).astype(jnp.float32)

@jax.custom_vjp
def low_back(v):
    return v

def low_keep(v):
    return (low(v), None)

def low_pass(kept, grad):
    return (grad,)

def back_keep(v):
    return (v, None)

def back_low(kept, grad):
    return (low(grad),)
low.defvjp(low_keep, low_pass)
low_back.defvjp(back_keep, back_low)

def matmul(left, right):
    return jnp.dot(left, right, precision=highest, preferred_element_type=jnp.float32)

def rms_scale(activity, gain_vec):
    return activity * lax.rsqrt(lax.optimization_barrier(jnp.mean(activity * activity, axis=-1, keepdims=True)) + epsilon) * gain_vec

def gelu_mix(gate_rows, up_rows):
    return jax.nn.gelu(gate_rows, approximate=True) * up_rows

def doc_index(lengths, places):
    starts = jnp.cumsum(lengths, dtype=jnp.int32) - lengths
    limit = jnp.sum(lengths, dtype=jnp.int32)
    doc_found = jnp.searchsorted(starts, places, side='right').astype(jnp.int32) - 1
    inside = (places >= 0) & (places < limit)
    return jnp.where(inside, doc_found, -1).astype(jnp.int32)

def gbst_local(byte_ext, conv_weight, score_weight, doc_ext):
    tap_count = conv_weight.shape[0]
    half_taps = tap_count // 2
    byte_count = byte_ext.shape[0] - 2 * half_taps
    feature_count = byte_ext.shape[1]
    centre = doc_ext[half_taps:half_taps + byte_count]
    convolved = jnp.zeros((byte_count, feature_count), jnp.float32)
    for offset in range(tap_count):
        same_doc = (doc_ext[offset:offset + byte_count] == centre)[:, None]
        convolved = convolved + jnp.where(same_doc, byte_ext[offset:offset + byte_count], 0.0) * conv_weight[offset]
    pooled_all = []
    scores_all = []
    for block_size in range(1, 5):
        block_means = lax.optimization_barrier(jnp.mean(convolved.reshape(byte_count // block_size, block_size, feature_count), axis=1))
        scores_all.append(jnp.repeat(jnp.dot(block_means, score_weight, precision=highest), block_size))
        pooled_all.append(jnp.repeat(block_means, block_size, axis=0))
    weights = jax.nn.softmax(jnp.stack(scores_all), axis=0)
    mixture = weights[0][:, None] * pooled_all[0]
    for block_size in range(1, 4):
        mixture = mixture + weights[block_size][:, None] * pooled_all[block_size]
    return lax.optimization_barrier(jnp.mean(mixture.reshape(byte_count // 2, 2, feature_count), axis=1))

def reference(byte_embed, query_weight, key_weight, value_weight, merge_weight, gate_weight, up_weight, down_weight, conv_weight, score_weight, attn_gain, ffn_gain, bias_table, doc_lengths, rel_bucket, out_grad):
    half_taps = CONV // 2
    group_len = TOK_DEV * N_ULY
    window_len = QBLK + 2 * DOC_TOK
    byte_doc = doc_index(doc_lengths, jnp.arange(BYTES + 2 * half_taps, dtype=jnp.int32) - half_taps)
    tok_doc = doc_index(doc_lengths, 2 * (jnp.arange(TOKENS + 2 * DOC_TOK, dtype=jnp.int32) - DOC_TOK))
    rel_at = jnp.clip(jnp.arange(window_len, dtype=jnp.int32)[None, :] - jnp.arange(QBLK, dtype=jnp.int32)[:, None] - 1, 0, 2 * DOC_TOK - 2)
    buckets = jnp.take(rel_bucket, rel_at)

    def forward(emb_in, query_in, key_in, value_in, merge_in, gate_in, up_in, down_in, conv_in, score_in, gain_one, gain_two, table_in):
        emb_pad = jnp.pad(emb_in, ((half_taps, half_taps), (0, 0)))

        def gbst_block(block_at):
            begin_at = block_at * 2 * group_len
            piece_len = 2 * group_len + 2 * half_taps
            return gbst_local(lax.dynamic_slice_in_dim(emb_pad, begin_at, piece_len, 0), conv_in, score_in, lax.dynamic_slice_in_dim(byte_doc, begin_at, piece_len, 0))
        gbst_out = lax.map(jax.checkpoint(gbst_block), jnp.arange(N_CTX, dtype=jnp.int32)).reshape(TOKENS, D)

        def project(rows_in):
            normed = low(rms_scale(rows_in, gain_one))
            return (low(low_back(matmul(normed, query_in))), low(low_back(matmul(normed, key_in))), low(low_back(matmul(normed, value_in))))
        query_all, key_all, value_all = lax.map(jax.checkpoint(project), gbst_out.reshape(N_CTX, group_len, D))
        queries = query_all.reshape(TOKENS, D)
        key_pad = jnp.pad(key_all.reshape(TOKENS, D), ((DOC_TOK, DOC_TOK), (0, 0)))
        value_pad = jnp.pad(value_all.reshape(TOKENS, D), ((DOC_TOK, DOC_TOK), (0, 0)))
        bias_all = jnp.transpose(jnp.take(table_in, buckets, axis=0), (2, 0, 1))

        def attend_block(block_at):
            begin_at = block_at * QBLK
            query_here = lax.dynamic_slice_in_dim(queries, begin_at, QBLK, 0).reshape(QBLK, HEADS, HEAD_DIM)
            key_here = lax.dynamic_slice_in_dim(key_pad, begin_at, window_len, 0).reshape(window_len, HEADS, HEAD_DIM)
            value_here = lax.dynamic_slice_in_dim(value_pad, begin_at, window_len, 0).reshape(window_len, HEADS, HEAD_DIM)
            query_doc = lax.dynamic_slice_in_dim(tok_doc, begin_at + DOC_TOK, QBLK, 0)
            key_doc = lax.dynamic_slice_in_dim(tok_doc, begin_at, window_len, 0)
            scores = low_back(jnp.einsum('qhd,khd->hqk', query_here, key_here, precision=highest) + bias_all)
            scores = jnp.where((query_doc[:, None] == key_doc[None, :])[None], scores, masked_score)
            weights = low(jax.nn.softmax(scores, axis=-1))
            return jnp.einsum('hqk,khd->qhd', weights, value_here, precision=highest).reshape(QBLK, D)
        attended = lax.map(jax.checkpoint(attend_block), jnp.arange(TOKENS // QBLK, dtype=jnp.int32)).reshape(TOKENS, D)
        attended = low(low_back(attended))

        def finish(pair_in):
            attended_rows, gbst_rows = pair_in
            mid_rows = gbst_rows + low_back(matmul(attended_rows, merge_in))
            normed = low(rms_scale(mid_rows, gain_two))
            hidden = low(gelu_mix(low_back(matmul(normed, gate_in)), low_back(matmul(normed, up_in))))
            return mid_rows + low_back(matmul(hidden, down_in))
        return lax.map(jax.checkpoint(finish), (attended.reshape(N_CTX, group_len, D), gbst_out.reshape(N_CTX, group_len, D))).reshape(TOKENS, D)
    layer_full, pullback = jax.vjp(forward, byte_embed.astype(jnp.float32), query_weight.astype(jnp.float32), key_weight.astype(jnp.float32), value_weight.astype(jnp.float32), merge_weight.astype(jnp.float32), gate_weight.astype(jnp.float32), up_weight.astype(jnp.float32), down_weight.astype(jnp.float32), conv_weight, score_weight, attn_gain, ffn_gain, bias_table)
    grads = pullback(out_grad.astype(jnp.float32))
    return (layer_full.astype(jnp.bfloat16), grads[0], grads[1], grads[2], grads[3], grads[4], grads[5], grads[6], grads[7], grads[8], grads[9], grads[10], grads[11], grads[12])
```

```python
from functools import partial

import jax
import jax.numpy as jnp
from jax import lax
from jax.experimental import pallas as pl
from jax.experimental.pallas import tpu as pltpu
from jax.sharding import Mesh, PartitionSpec as P

HEADS = 12
HEAD_DIM = 64
NBUCK = 32
CONV = 5
DOC_TOK = 1024
TILE = 256
FORM = 16
PHASES = 12
EPS = 1e-06
BIG = 1e30
GELU_C = 0.7978845608028654
GELU_A = 0.044715

bf16 = jnp.bfloat16
f32 = jnp.float32
RING = ("ctx", "ux", "uc")
ULY = ("ux", "uc")
highest = lax.Precision.HIGHEST


def dot(left, right, dims=((1,), (0,))):
    return lax.dot_general(left, right, (dims, ((), ())), preferred_element_type=f32)


def kernel_call(body, outs, *, grid=(1,), ins, scratch=(), prefetch=0, out_specs=None, flops=0, moved=0, name=None):
    params = pltpu.CompilerParams(
        dimension_semantics=("arbitrary",) * len(grid), vmem_limit_bytes=56 << 20
    )
    return pl.pallas_call(
        body,
        out_shape=outs,
        grid_spec=pltpu.PrefetchScalarGridSpec(
            num_scalar_prefetch=prefetch,
            grid=grid,
            in_specs=ins,
            out_specs=out_specs,
            scratch_shapes=list(scratch),
        ),
        compiler_params=params,
        cost_estimate=pl.CostEstimate(flops=int(flops), bytes_accessed=int(moved), transcendentals=0),
        name=name,
    )


def whole(shape, once=True):
    zeros = (0,) * len(shape)
    if once:
        return pl.BlockSpec(shape, lambda *a: zeros, pipeline_mode=pl.Buffered(1))
    return pl.BlockSpec(shape, lambda *a: zeros)


def struct(shape, dtype):
    return jax.ShapeDtypeStruct(shape, dtype)


def block_of(size, at):
    first = size * (at // size)
    return range(first, first + size)


def token_pairs(tok):
    found = set()
    for byte in (2 * tok, 2 * tok + 1):
        for size in range(1, 5):
            found |= set(block_of(size, byte))
    return sorted(found)


def mix_coefs(weights):
    coefs = {}
    for tok in range(PHASES // 2):
        for at in token_pairs(tok):
            total = None
            for byte in (2 * tok, 2 * tok + 1):
                for size in range(1, 5):
                    if at in block_of(size, byte):
                        term = weights[size - 1][byte] * (0.5 / size)
                        total = term if total is None else total + term
            coefs[tok, at] = total
    return coefs


def lane_chunks(feats):
    return [slice(128 * c, 128 * (c + 1)) for c in range(feats // 128)]


def fill_bytes(pad, lo, emb, hi):
    byte_count, feats = emb.shape
    chunks = lane_chunks(feats)
    for c, cols in enumerate(chunks):
        pad[c, 0:8, :] = lo[:, cols].astype(f32)
        pad[c, 8 + byte_count : 16 + byte_count, :] = hi[:, cols].astype(f32)

    def fill(t, _):
        at = pl.multiple_of(t * 32, 32)
        for c, cols in enumerate(chunks):
            pad[c, pl.ds(at + 8, 32), :] = emb[pl.ds(at, 32), cols].astype(f32)
        return 0

    lax.fori_loop(0, byte_count // 32, fill, 0)


def gbst_forward_kernel(lo, emb, hi, msk, cw, sw, gain, gb, nrm, conv, aw, pad, mix):
    byte_count, feats = emb.shape
    chunks = lane_chunks(feats)
    fill_bytes(pad, lo, emb, hi)
    lanes = lax.broadcasted_iota(jnp.int32, (8, 128), 1)

    def step(g, _):
        base = g * 8 * PHASES + 8
        rows = pl.ds(pl.multiple_of(8 * g, 8), 8)
        first = []
        for p in range(PHASES):
            mask = msk[pl.ds(base + p, 8, stride=PHASES), :]
            same = {k: mask[:, k : k + 1] for k in (0, 1, 3, 4)}
            dots = None
            for c, cols in enumerate(chunks):
                x = pad[c, pl.ds(base + p, 8, stride=PHASES), :] * cw[2:3, cols]
                for k in (0, 1, 3, 4):
                    x = x + pad[c, pl.ds(base + p + k - 2, 8, stride=PHASES), :] * same[k] * cw[k : k + 1, cols]
                conv[p, rows, cols] = x
                term = x * sw[:, cols]
                dots = term if dots is None else dots + term
            first.append(jnp.sum(dots, axis=1, keepdims=True))
        weights = [[None] * PHASES for _ in range(4)]
        packed = jnp.zeros((8, 128), f32)
        for p in range(PHASES):
            scores = []
            for size in range(1, 5):
                total = None
                for at in block_of(size, p):
                    total = first[at] if total is None else total + first[at]
                scores.append(total * (1.0 / size))
            top = jnp.maximum(jnp.maximum(scores[0], scores[1]), jnp.maximum(scores[2], scores[3]))
            exps = [jnp.exp(s - top) for s in scores]
            inv = 1.0 / (exps[0] + exps[1] + exps[2] + exps[3])
            for size in range(4):
                weights[size][p] = exps[size] * inv
                packed = jnp.where(lanes == 4 * p + size, weights[size][p], packed)
        aw[rows, :] = packed
        coefs = mix_coefs(weights)
        for tok in range(PHASES // 2):
            for c, cols in enumerate(chunks):
                out = None
                for at in token_pairs(tok):
                    term = coefs[tok, at] * conv[at, rows, cols]
                    out = term if out is None else out + term
                mix[c, pl.ds(g * 4 * PHASES + tok, 8, stride=PHASES // 2), :] = out
        return 0

    lax.fori_loop(0, byte_count // (8 * PHASES), step, 0)

    def norm(t, _):
        at = pl.multiple_of(t * 16, 16)
        v = jnp.concatenate([mix[c, pl.ds(at, 16), :] for c in range(len(chunks))], axis=1)
        r = lax.rsqrt(jnp.mean(v * v, axis=1, keepdims=True) + EPS)
        gb[pl.ds(at, 16), :] = v
        nrm[pl.ds(at, 16), :] = (v * r * gain[...]).astype(bf16)
        return 0

    lax.fori_loop(0, byte_count // 32, norm, 0)


def gbst_forward(lo, emb, hi, msk, cw, sw, gain):
    nb, d = emb.shape
    return kernel_call(
        gbst_forward_kernel,
        (
            struct((nb // 2, d), f32),
            struct((nb // 2, d), bf16),
            struct((PHASES, nb // PHASES, d), f32),
            struct((nb // PHASES, 128), f32),
        ),
        ins=[whole(x.shape) for x in (lo, emb, hi, msk, cw, sw, gain)],
        out_specs=(
            whole((nb // 2, d), False),
            whole((nb // 2, d), False),
            whole((PHASES, nb // PHASES, d), False),
            whole((nb // PHASES, 128), False),
        ),
        scratch=[pltpu.VMEM((d // 128, nb + 16, 128), f32), pltpu.VMEM((d // 128, nb // 2, 128), f32)],
        flops=60 * nb * d,
        moved=20 * nb * d,
        name="gbst_forward",
    )(lo, emb, hi, msk, cw, sw, gain)


def gbst_backward_kernel(keep, recv, gb, dmid, gain, conv, aw, lo, emb, hi, msk, cw, sw, eg, small, dtok, dconv, pad, acc):
    byte_count, feats = emb.shape
    chunks = lane_chunks(feats)
    acc[...] = jnp.zeros_like(acc)
    fill_bytes(pad, lo, emb, hi)
    for c in range(len(chunks)):
        dconv[c, 0:16, :] = jnp.zeros((16, 128), f32)
        dconv[c, 16 + byte_count : 32 + byte_count, :] = jnp.zeros((16, 128), f32)

    def norm(t, _):
        at = pl.multiple_of(t * 16, 16)
        e = keep[pl.ds(at, 16), :] + recv[pl.ds(at, 16), :].astype(f32)
        v = gb[pl.ds(at, 16), :]
        r = lax.rsqrt(jnp.mean(v * v, axis=1, keepdims=True) + EPS)
        ge = gain[...] * e
        m = jnp.mean(ge * v, axis=1, keepdims=True)
        out = dmid[pl.ds(at, 16), :] + r * ge - v * (r * r * r * m)
        for c, cols in enumerate(chunks):
            dtok[c, pl.ds(at, 16), :] = out[:, cols]
        part = e * v * r
        acc[48:56, :] = acc[48:56, :] + part[0:8] + part[8:16]
        return 0

    lax.fori_loop(0, byte_count // 32, norm, 0)

    def step(g, _):
        rows = pl.ds(pl.multiple_of(8 * g, 8), 8)
        half = PHASES // 2

        def tok_rows(tok, c):
            return dtok[c, pl.ds(g * 8 * half + tok, 8, stride=half), :]

        inner = {}
        for tok in range(half):
            toks = [tok_rows(tok, c) for c in range(len(chunks))]
            for at in token_pairs(tok):
                dots = None
                for c, cols in enumerate(chunks):
                    term = toks[c] * conv[at, rows, cols]
                    dots = term if dots is None else dots + term
                inner[tok, at] = jnp.sum(dots, axis=1, keepdims=True)
        tile = aw[rows, :]
        weights = [[tile[:, 4 * p + size : 4 * p + size + 1] for p in range(PHASES)] for size in range(4)]
        coefs = mix_coefs(weights)
        dsize = [[None] * PHASES for _ in range(4)]
        for p in range(PHASES):
            cs = []
            for size in range(1, 5):
                total = None
                for at in block_of(size, p):
                    total = inner[p // 2, at] if total is None else total + inner[p // 2, at]
                cs.append(total * (0.5 / size))
            mean = sum(weights[s][p] * cs[s] for s in range(4))
            for s in range(4):
                dsize[s][p] = weights[s][p] * (cs[s] - mean)
        slopes = []
        for at in range(PHASES):
            e = None
            for size in range(1, 5):
                for p in block_of(size, at):
                    term = dsize[size - 1][p] * (1.0 / size)
                    e = term if e is None else e + term
            slopes.append(e)
        for c, cols in enumerate(chunks):
            toks = [tok_rows(tok, c) for tok in range(half)]
            score = acc[40:48, cols]
            for at in range(PHASES):
                out = slopes[at] * sw[:, cols]
                for tok in range(half):
                    if (tok, at) in coefs:
                        out = out + coefs[tok, at] * toks[tok]
                dconv[c, pl.ds(g * 8 * PHASES + 16 + at, 8, stride=PHASES), :] = out
                score = score + slopes[at] * conv[at, rows, cols]
            acc[40:48, cols] = score
        return 0

    lax.fori_loop(0, byte_count // (8 * PHASES), step, 0)

    def taps(t, _):
        at = pl.multiple_of(t * 8, 8)
        mask = msk[pl.ds(at, 8), :]
        same = {k: mask[:, 4 - k : 5 - k] for k in (0, 1, 3, 4)}
        for c, cols in enumerate(chunks):
            x = pad[c, pl.ds(at, 8), :]
            out = None
            for k in range(CONV):
                z = dconv[c, pl.ds(at + 8 + 2 - k, 8), :]
                if k != 2:
                    z = z * same[k]
                term = z * cw[k : k + 1, cols]
                out = term if out is None else out + term
                acc[8 * k : 8 * k + 8, cols] = acc[8 * k : 8 * k + 8, cols] + z * x
            eg[pl.ds(at, 8), cols] = out
        return 0

    lax.fori_loop(0, (byte_count + 16) // 8, taps, 0)
    small[...] = jnp.zeros_like(small)
    for k in range(7):
        small[k : k + 1, :] = jnp.sum(acc[8 * k : 8 * k + 8, :], axis=0, keepdims=True)


def gbst_backward(keep, recv, gb, dmid, gain, conv, aw, lo, emb, hi, msk, cw, sw):
    nb, d = emb.shape
    args = (keep, recv, gb, dmid, gain, conv, aw, lo, emb, hi, msk, cw, sw)
    return kernel_call(
        gbst_backward_kernel,
        (struct((nb + 16, d), f32), struct((8, d), f32)),
        ins=[whole(x.shape) for x in args],
        out_specs=(whole((nb + 16, d), False), whole((8, d), False)),
        scratch=[
            pltpu.VMEM((d // 128, nb // 2, 128), f32),
            pltpu.VMEM((d // 128, nb + 32, 128), f32),
            pltpu.VMEM((d // 128, nb + 16, 128), f32),
            pltpu.VMEM((56, d), f32),
        ],
        flops=120 * nb * d,
        moved=24 * nb * d,
        name="gbst_backward",
    )(*args)


def halo_row(who, tok_dev, ext):
    return jnp.where(who >= 2, (who - 2) * tok_dev, ext - 2 * tok_dev + who * tok_dev)


def project_kernel(me, *refs):
    own, far, w, (q, k, v, wp) = refs[:4], refs[4:8], refs[8], refs[9:13]
    tok, _ = own[0].shape
    wide = TILE
    part = w.shape[1] // 3
    wp[...] = jnp.zeros_like(wp)
    for j in range(3):
        wp[:, wide * j : wide * j + part] = w[:, part * j : part * (j + 1)]
    ext = k.shape[0]
    left = (ext - q.shape[0]) // 2
    for rel in range(4):
        who = me[0] ^ rel
        out = dot(own[rel][...], wp[...]).astype(bf16)
        q[pl.ds(pl.multiple_of(who * tok, 128), tok), :] = out[:, :wide]
        at = pl.multiple_of(left + who * tok, 128)
        k[pl.ds(at, tok), :] = out[:, wide : 2 * wide]
        v[pl.ds(at, tok), :] = out[:, 2 * wide :]
        at = pl.multiple_of(halo_row(who, tok, ext), 128)
        out = dot(far[rel][...], wp[:, wide:]).astype(bf16)
        k[pl.ds(at, tok), :] = out[:, :wide]
        v[pl.ds(at, tok), :] = out[:, wide:]


def project(me, own, far, w):
    tok, d = own[0].shape
    rows, ext = 4 * tok, 8 * tok
    args = (*own, *far, w)
    return kernel_call(
        project_kernel,
        (
            struct((rows, TILE), bf16),
            struct((ext, TILE), bf16),
            struct((ext, TILE), bf16),
            struct((d, 3 * TILE), bf16),
        ),
        prefetch=1,
        ins=[whole(x.shape) for x in args],
        out_specs=(
            whole((rows, TILE), False),
            whole((ext, TILE), False),
            whole((ext, TILE), False),
            whole((d, 3 * TILE), False),
        ),
        flops=2 * ext * d * 3 * TILE,
        moved=2 * (ext * d + 2 * ext * TILE + d * d),
        name="project",
    )(me, *args)


def project_back_kernel(is_halo, me, dq, dk, dv, wp, keep0, keep2, send1, send3):
    tok = keep0.shape[0]
    ext = dk.shape[0]
    left = (ext - dq.shape[0]) // 2
    for rel, ref in ((3, send3), (1, send1), (2, keep2), (0, keep0)):
        who = me[0] ^ rel
        if is_halo:
            at = pl.multiple_of(halo_row(who, tok, ext), 128)
            out = dot(dk[pl.ds(at, tok), :], wp[:, TILE : 2 * TILE], ((1,), (1,)))
        else:
            at = pl.multiple_of(left + who * tok, 128)
            out = dot(dk[pl.ds(at, tok), :], wp[:, TILE : 2 * TILE], ((1,), (1,)))
            mine = pl.multiple_of(who * tok, 128)
            out = out + dot(dq[pl.ds(mine, tok), :], wp[:, :TILE], ((1,), (1,)))
        out = out + dot(dv[pl.ds(at, tok), :], wp[:, 2 * TILE :], ((1,), (1,)))
        ref[...] = out.astype(ref.dtype)


def project_back(is_halo, me, dq, dk, dv, wp):
    ext, d = dk.shape[0], wp.shape[0]
    tok = ext // 8
    args = (dq, dk, dv, wp)
    kinds = (f32, f32, bf16, bf16)
    return kernel_call(
        partial(project_back_kernel, is_halo),
        tuple(struct((tok, d), kind) for kind in kinds),
        prefetch=1,
        ins=[whole(x.shape) for x in args],
        out_specs=tuple(whole((tok, d), False) for _ in kinds),
        flops=2 * ext // 2 * d * 3 * TILE,
        moved=4 * ext * d,
        name="project_back",
    )(me, *args)


def project_grad_kernel(me, *refs):
    own, far, (dqt, dkt, dvt), out = refs[:4], refs[4:8], refs[8:11], refs[11]
    tok = own[0].shape[0]
    ext = dkt.shape[1]
    left = (ext - dqt.shape[1]) // 2
    part = dqt.shape[0]
    totals = [None] * 3
    for rel in range(4):
        who = me[0] ^ rel
        mine = pl.multiple_of(who * tok, 128)
        at = pl.multiple_of(left + who * tok, 128)
        edge = pl.multiple_of(halo_row(who, tok, ext), 128)
        terms = [
            dot(dqt[:, pl.ds(mine, tok)], own[rel][...]),
            dot(dkt[:, pl.ds(at, tok)], own[rel][...]) + dot(dkt[:, pl.ds(edge, tok)], far[rel][...]),
            dot(dvt[:, pl.ds(at, tok)], own[rel][...]) + dot(dvt[:, pl.ds(edge, tok)], far[rel][...]),
        ]
        totals = [t if s is None else s + t for s, t in zip(totals, terms)]
    for j in range(3):
        out[:, part * j : part * (j + 1)] = totals[j].T.astype(bf16)


def project_grad(me, own, far, dqt, dkt, dvt):
    tok, d = own[0].shape
    args = (*own, *far, dqt, dkt, dvt)
    return kernel_call(
        project_grad_kernel,
        struct((d, 3 * dqt.shape[0]), bf16),
        prefetch=1,
        ins=[whole(x.shape) for x in args],
        out_specs=whole((d, 3 * dqt.shape[0]), False),
        flops=2 * 8 * tok * d * 3 * dqt.shape[0],
        moved=2 * 12 * tok * d,
        name="project_grad",
    )(me, *args)


def bias_kernel(diag, out):
    at = pl.program_id(0)
    heads = diag.shape[0]
    seg = diag[:, pl.ds(pl.multiple_of(at * TILE, TILE), 2 * TILE)]
    for h in range(heads):
        rows = jnp.broadcast_to(seg[h : h + 1, :], (TILE, 2 * TILE))
        turned = pltpu.roll(rows, TILE + 1, axis=1, stride=1, stride_axis=0)
        out[0, TILE * h : TILE * (h + 1), :] = turned[:, :TILE]


def bias_tiles(diag):
    heads, width = diag.shape
    count = width // TILE - 1
    return kernel_call(
        bias_kernel,
        struct((count, heads * TILE, TILE), f32),
        grid=(count,),
        ins=[whole(diag.shape)],
        out_specs=pl.BlockSpec((1, heads * TILE, TILE), lambda i: (i, 0, 0)),
        moved=4 * count * heads * TILE * TILE,
        name="bias_tiles",
    )(diag)


def table_kernel(tiles, out):
    heads = out.shape[1]
    for h in range(heads):
        part = tiles[0, TILE * h : TILE * (h + 1), :]
        cur = jnp.concatenate([part, jnp.zeros_like(part)], axis=1)
        rows = TILE
        while rows > 8:
            rows //= 2
            cur = cur[:rows] + pltpu.roll(cur[rows:], 2 * TILE - rows, axis=1)
        total = cur[0:1]
        for i in range(1, 8):
            total = total + pltpu.roll(cur[i : i + 1], 2 * TILE - i, axis=1)
        out[0, h : h + 1, :] = pltpu.roll(total, TILE - 1, axis=1)


def table_sums(tiles):
    count, rows, _ = tiles.shape
    heads = rows // TILE
    return kernel_call(
        table_kernel,
        struct((count, heads, 2 * TILE), f32),
        grid=(count,),
        ins=[pl.BlockSpec((1, rows, TILE), lambda i: (i, 0, 0))],
        out_specs=pl.BlockSpec((1, heads, 2 * TILE), lambda i: (i, 0, 0)),
        moved=4 * count * rows * TILE,
        name="table_sums",
    )(tiles)


def lane_head(shape):
    return lax.broadcasted_iota(jnp.int32, shape, 1) // HEAD_DIM


def attend_kernel(heads, info, q, k, v, cq, ck, bias, oa, ob, oloc, lse, kx, q3, sc, mx, ls, ac):
    i = pl.program_id(0)
    grid = pl.num_programs(0)
    me = info[2 * grid]
    ext = k.shape[0]

    @pl.when(i == 0)
    def _():
        kx[...] = k[...] + ck[...]

    lo, hi = info[i], info[grid + i]
    away = (ext // TILE - grid) // 2
    where = lane_head((TILE, TILE))
    for h in range(heads):
        q3[TILE * h : TILE * (h + 1), :] = jnp.where(where == h, q[...], jnp.zeros_like(q[...])) + cq[...]
    mx[...] = jnp.full_like(mx, -jnp.inf)
    ls[...] = jnp.zeros_like(ls)
    ac[...] = jnp.zeros_like(ac)

    def scores(kt, _):
        at = pl.multiple_of(kt * TILE, TILE)
        s = dot(q3[...], kx[pl.ds(at, TILE), :], ((1,), (1,))) + bias[kt - i - away + 4]
        sc[kt - lo] = s
        mx[...] = jnp.maximum(mx[...], jnp.maximum(s[:, :128], s[:, 128:]))
        return 0

    lax.fori_loop(lo, hi, scores, 0)
    top = jnp.max(mx[...], axis=1, keepdims=True)

    def gather(kt, _):
        at = pl.multiple_of(kt * TILE, TILE)
        p = jnp.exp(sc[kt - lo] - top)
        ls[...] = ls[...] + p[:, :128] + p[:, 128:]
        ac[...] = ac[...] + dot(p.astype(bf16), v[pl.ds(at, TILE), :])
        return 0

    lax.fori_loop(lo, hi, gather, 0)
    total = jnp.sum(ls[...], axis=1, keepdims=True)
    inv = 1.0 / total
    logs = top + jnp.log(total)
    out = jnp.zeros((TILE, TILE), f32)
    kept = jnp.zeros((TILE, 128), f32)
    lane = lax.broadcasted_iota(jnp.int32, (TILE, 128), 1)
    for h in range(heads):
        rows = slice(TILE * h, TILE * (h + 1))
        out = jnp.where(where == h, ac[rows, :] * inv[rows], out)
        kept = jnp.where(lane == h, logs[rows], kept)
    lse[...] = kept
    oloc[...] = out.astype(bf16)
    turned = out.T.astype(bf16)
    per = oa.shape[1]
    for j in range(TILE // 128):
        chunk = i * (TILE // 128) + j
        rel = (chunk // per) ^ me
        piece = turned[: heads * HEAD_DIM, 128 * j : 128 * (j + 1)]

        @pl.when(rel < 2)
        def _():
            oa[rel, chunk % per] = piece

        @pl.when(rel >= 2)
        def _():
            ob[rel - 2, chunk % per] = piece


def attend(info, q, k, v, cq, ck, bias, heads, tok):
    rows, ext = q.shape[0], k.shape[0]
    grid = rows // TILE
    width = heads * HEAD_DIM
    sent = (2, tok // 128, width, 128)
    tile = pl.BlockSpec((TILE, TILE), lambda i, *_: (i, 0))
    return kernel_call(
        partial(attend_kernel, heads),
        (
            struct(sent, bf16),
            struct(sent, bf16),
            struct((rows, TILE), bf16),
            struct((rows, 128), f32),
        ),
        grid=(grid,),
        prefetch=1,
        ins=[tile, whole(k.shape), whole(v.shape), tile, whole(ck.shape), whole(bias.shape)],
        out_specs=(
            whole(sent, False),
            whole(sent, False),
            tile,
            pl.BlockSpec((TILE, 128), lambda i, *_: (i, 0)),
        ),
        scratch=[
            pltpu.VMEM((ext, TILE), bf16),
            pltpu.VMEM((heads * TILE, TILE), bf16),
            pltpu.VMEM((9, heads * TILE, TILE), f32),
            pltpu.VMEM((heads * TILE, 128), f32),
            pltpu.VMEM((heads * TILE, 128), f32),
            pltpu.VMEM((heads * TILE, TILE), f32),
        ],
        flops=4 * rows * 1280 * TILE * heads,
        moved=4 * bias.size + 8 * ext * TILE,
        name="attend",
    )(info, q, k, v, cq, ck, bias)


def attend_back_kernel(
    heads, info, q, k, v, cq, ck, bias, oloc, lse, d0, d2, d13,
    dq, dk, dv, dqt, dkt, dvt, tacc,
    kx, q3, g3, gall, dqa, dka, dva, qt, gt,
):
    i = pl.program_id(0)
    grid = pl.num_programs(0)
    me = info[2 * grid]
    ext = k.shape[0]
    per = d0.shape[0]
    width = heads * HEAD_DIM

    @pl.when(i == 0)
    def _():
        kx[...] = k[...] + ck[...]
        dka[...] = jnp.zeros_like(dka)
        dva[...] = jnp.zeros_like(dva)
        tacc[...] = jnp.zeros_like(tacc)
        for rel, piece in ((0, d0[...]), (2, d2[...]), (1, d13[0]), (3, d13[1])):
            gall[pl.ds((me ^ rel) * per, per)] = piece

    lo, hi = info[i], info[grid + i]
    away = (ext // TILE - grid) // 2
    where = lane_head((TILE, TILE))
    for j in range(TILE // 128):
        gt[:width, 128 * j : 128 * (j + 1)] = gall[i * (TILE // 128) + j]
    gt[width:, :] = jnp.zeros((TILE - width, TILE), bf16)
    grad = gt[...].astype(f32).T
    qt[...] = q[...].astype(f32).T.astype(bf16)
    prod = grad * oloc[...].astype(f32)
    deltas, logs = [], []
    for h in range(heads):
        rows = slice(TILE * h, TILE * (h + 1))
        q3[rows, :] = jnp.where(where == h, q[...], jnp.zeros_like(q[...])) + cq[...]
        g3[rows, :] = jnp.where(where == h, grad, 0.0).astype(bf16)
        deltas.append(jnp.sum(jnp.where(where == h, prod, 0.0), axis=1, keepdims=True))
        logs.append(lse[:, h : h + 1])
    delta = jnp.concatenate(deltas, axis=0)
    log = jnp.concatenate(logs, axis=0)
    dqa[...] = jnp.zeros_like(dqa)

    def step(kt, _):
        at = pl.ds(pl.multiple_of(kt * TILE, TILE), TILE)
        rel = kt - i - away + 4
        s = dot(q3[...], kx[at, :], ((1,), (1,))) + bias[rel]
        p = jnp.exp(s - log)
        dp = dot(g3[...], v[at, :], ((1,), (1,)))
        ds = p * (dp - delta)
        tacc[rel] = tacc[rel] + ds
        low = ds.astype(bf16)
        plow = p.astype(bf16)
        dqa[...] = dqa[...] + dot(low, k[at, :])
        for h in range(heads):
            rows = slice(TILE * h, TILE * (h + 1))
            head = slice(HEAD_DIM * h, HEAD_DIM * (h + 1))
            dka[head, at] = dka[head, at] + dot(qt[head, :], low[rows, :])
            dva[head, at] = dva[head, at] + dot(gt[head, :], plow[rows, :])
        return 0

    lax.fori_loop(lo, hi, step, 0)
    out = jnp.zeros((TILE, TILE), f32)
    for h in range(heads):
        out = jnp.where(where == h, dqa[TILE * h : TILE * (h + 1), :], out)
    dq[...] = out.astype(bf16)
    dqt[...] = out.T[:width].astype(bf16)

    @pl.when(i == grid - 1)
    def _():
        fill = jnp.zeros((TILE - width, TILE), f32)

        def turn(t, _):
            at = pl.ds(pl.multiple_of(t * TILE, TILE), TILE)
            for acc, flat, turned in ((dka, dkt, dk), (dva, dvt, dv)):
                part = acc[:, at]
                flat[:, at] = part.astype(bf16)
                turned[at, :] = jnp.concatenate([part, fill], axis=0).T.astype(bf16)
            return 0

        lax.fori_loop(0, ext // TILE, turn, 0)


def attend_back(info, q, k, v, cq, ck, bias, oloc, lse, d0, d2, d13, heads):
    rows, ext = q.shape[0], k.shape[0]
    grid = rows // TILE
    width = heads * HEAD_DIM
    per = d0.shape[0]
    tile = pl.BlockSpec((TILE, TILE), lambda i, *_: (i, 0))
    return kernel_call(
        partial(attend_back_kernel, heads),
        (
            struct((rows, TILE), bf16),
            struct((ext, TILE), bf16),
            struct((ext, TILE), bf16),
            struct((width, rows), bf16),
            struct((width, ext), bf16),
            struct((width, ext), bf16),
            struct(bias.shape, f32),
        ),
        grid=(grid,),
        prefetch=1,
        ins=[
            tile, whole(k.shape), whole(v.shape), tile, whole(ck.shape), whole(bias.shape),
            tile, pl.BlockSpec((TILE, 128), lambda i, *_: (i, 0)),
            whole(d0.shape), whole(d2.shape), whole(d13.shape),
        ],
        out_specs=(
            tile,
            whole((ext, TILE)),
            whole((ext, TILE)),
            pl.BlockSpec((width, TILE), lambda i, *_: (0, i)),
            whole((width, ext)),
            whole((width, ext)),
            whole(bias.shape),
        ),
        scratch=[
            pltpu.VMEM((ext, TILE), bf16),
            pltpu.VMEM((heads * TILE, TILE), bf16),
            pltpu.VMEM((heads * TILE, TILE), bf16),
            pltpu.VMEM((rows // 128, width, 128), bf16),
            pltpu.VMEM((heads * TILE, TILE), f32),
            pltpu.VMEM((width, ext), f32),
            pltpu.VMEM((width, ext), f32),
            pltpu.VMEM((TILE, TILE), bf16),
            pltpu.VMEM((TILE, TILE), bf16),
        ],
        flops=10 * rows * 1280 * TILE * heads,
        moved=8 * bias.size + 16 * ext * TILE,
        name="attend_back",
    )(info, q, k, v, cq, ck, bias, oloc, lse, d0, d2, d13)


def merge_rows(packed, src, part):
    span = FORM // 4
    low = 576 + 48 * part
    return packed[pl.ds(src * span, span), low : low + 48, :].reshape(48 * span, TILE)


def merge_kernel(me, a0, a2, a13, packed, gb, gain, mid, nrm):
    per = a0.shape[0]
    for t in range(per):
        rows = slice(128 * t, 128 * (t + 1))
        total = [gb[rows, TILE * part : TILE * (part + 1)] for part in range(3)]
        for rel, piece in ((0, a0[t]), (2, a2[t]), (1, a13[0, t]), (3, a13[1, t])):
            flat = piece.astype(f32).T.astype(bf16)
            for part in range(3):
                total[part] = total[part] + dot(flat, merge_rows(packed, me[0] ^ rel, part))
        v = jnp.concatenate(total, axis=1)
        mid[rows, :] = v
        r = lax.rsqrt(jnp.mean(v * v, axis=1, keepdims=True) + EPS)
        nrm[rows, :] = (v * r * gain[...]).astype(bf16)


def merge(me, a0, a2, a13, packed, gb, gain):
    tok, d = gb.shape
    args = (a0, a2, a13, packed, gb, gain)
    return kernel_call(
        merge_kernel,
        (struct((tok, d), f32), struct((tok, d), bf16)),
        prefetch=1,
        ins=[whole(x.shape) for x in args],
        out_specs=(whole((tok, d), False), whole((tok, d), False)),
        flops=2 * tok * d * d,
        moved=10 * tok * d + packed.size * 2,
        name="merge",
    )(me, *args)


def feed_kernel(na, nb, ga, gb, packed, oa, ob, da, db, hid, dg, du, nt, gr, osum, dsum):
    j = pl.program_id(0)
    tok = na.shape[0]

    @pl.when(j == 0)
    def _():
        nt[:tok, :] = na[...]
        nt[tok:, :] = nb[...]
        gr[:tok, :] = ga[...]
        gr[tok:, :] = gb[...]
        osum[...] = jnp.zeros_like(osum)
        dsum[...] = jnp.zeros_like(dsum)

    at = pl.multiple_of(48 * j, 16)
    wg = packed[:, pl.ds(at, 48), :].reshape(FORM * 48, TILE)
    wu = packed[:, pl.ds(192 + at, 48), :].reshape(FORM * 48, TILE)
    gate = dot(nt[...], wg)
    up = dot(nt[...], wu)
    dh = None
    wds = []
    for part in range(3):
        wd = packed[pl.ds(4 * j, 4), 384 + 64 * part : 448 + 64 * part, :].reshape(TILE, TILE)
        wds.append(wd)
        term = dot(gr[:, TILE * part : TILE * (part + 1)], wd, ((1,), (1,)))
        dh = term if dh is None else dh + term
    sq = gate * gate
    th = jnp.tanh(GELU_C * gate * (1.0 + GELU_A * sq))
    half = 0.5 * (1.0 + th)
    act = gate * half
    slope = half + 0.5 * gate * (1.0 - th * th) * (GELU_C * (1.0 + 3.0 * GELU_A * sq))
    h = (act * up).astype(bf16)
    g = (dh * up * slope).astype(bf16)
    u = (dh * act).astype(bf16)
    hid[...] = h
    dg[...] = g
    du[...] = u
    for part in range(3):
        cols = slice(TILE * part, TILE * (part + 1))
        osum[:, cols] = osum[:, cols] + dot(h, wds[part])
    dsum[...] = dsum[...] + dot(g, wg, ((1,), (1,))) + dot(u, wu, ((1,), (1,)))

    @pl.when(j == pl.num_programs(0) - 1)
    def _():
        oa[...] = osum[:tok, :]
        ob[...] = osum[tok:, :].astype(bf16)
        da[...] = dsum[:tok, :]
        db[...] = dsum[tok:, :].astype(bf16)


def feed(na, nb, ga, gb, packed, units):
    tok, d = na.shape
    args = (na, nb, ga, gb, packed)
    col = pl.BlockSpec((2 * tok, TILE), lambda j: (0, j))
    full = whole((tok, d))
    return kernel_call(
        feed_kernel,
        (
            struct((tok, d), f32), struct((tok, d), bf16), struct((tok, d), f32), struct((tok, d), bf16),
            struct((2 * tok, units), bf16), struct((2 * tok, units), bf16), struct((2 * tok, units), bf16),
        ),
        grid=(units // TILE,),
        ins=[whole(x.shape) for x in args],
        out_specs=(full, full, full, full, col, col, col),
        scratch=[
            pltpu.VMEM((2 * tok, d), bf16), pltpu.VMEM((2 * tok, d), bf16),
            pltpu.VMEM((2 * tok, d), f32), pltpu.VMEM((2 * tok, d), f32),
        ],
        flops=12 * 2 * tok * d * units,
        moved=2 * packed.size + 20 * tok * d + 12 * tok * units,
        name="feed",
    )(*args)


def middle_kernel(me, mid, da, db, oa, ob, og, gain, packed, layer, dmid, dlow, ga, gb, gsum):
    tok, d = mid.shape
    gsum[...] = jnp.zeros_like(gsum)

    def norm(t, _):
        at = pl.ds(pl.multiple_of(t * 16, 16), 16)
        v = mid[at, :]
        layer[at, :] = (v + oa[at, :] + ob[at, :].astype(f32)).astype(bf16)
        e = da[at, :] + db[at, :].astype(f32)
        r = lax.rsqrt(jnp.mean(v * v, axis=1, keepdims=True) + EPS)
        ge = gain[...] * e
        m = jnp.mean(ge * v, axis=1, keepdims=True)
        out = og[at, :].astype(f32) + r * ge - v * (r * r * r * m)
        dmid[at, :] = out
        dlow[at, :] = out.astype(bf16)
        part = e * v * r
        gsum[...] = gsum[...] + part[0:8] + part[8:16]
        return 0

    lax.fori_loop(0, tok // 16, norm, 0)
    for rel in range(4):
        out = None
        for part in range(3):
            cols = slice(TILE * part, TILE * (part + 1))
            term = dot(merge_rows(packed, me[0] ^ rel, part), dlow[:, cols], ((1,), (1,)))
            out = term if out is None else out + term
        low = out.astype(bf16)
        for t in range(tok // 128):
            ref = ga if rel < 2 else gb
            ref[rel % 2, t] = low[:, 128 * t : 128 * (t + 1)]


def middle(me, mid, da, db, oa, ob, og, gain, packed):
    tok, d = mid.shape
    args = (mid, da, db, oa, ob, og, gain, packed)
    sent = (2, tok // 128, d // 4, 128)
    shapes = [((tok, d), bf16), ((tok, d), f32), ((tok, d), bf16), (sent, bf16), (sent, bf16), ((8, d), f32)]
    return kernel_call(
        middle_kernel,
        tuple(struct(*s) for s in shapes),
        prefetch=1,
        ins=[whole(x.shape) for x in args],
        out_specs=tuple(whole(s[0], False) for s in shapes),
        flops=2 * tok * d * d,
        moved=30 * tok * d + packed.size * 2,
        name="middle",
    )(me, *args)


def merge_grad_kernel(me, a0, a2, a13, dlow, keep, send):
    per = a0.shape[0]
    width = a0.shape[1]
    half = keep.shape[1]
    core = me[0] % 2
    for rel in range(4):
        pieces = [(a0[t], a2[t], a13[0, t], a13[1, t])[(0, 2, 1, 3)[rel]] for t in range(per)]
        left = jnp.concatenate(pieces, axis=1)
        rows = pl.ds(pl.multiple_of((me[0] ^ rel) * width, 64), width)
        mine = dlow[:, pl.ds(pl.multiple_of(core * half, 128), half)]
        other = dlow[:, pl.ds(pl.multiple_of((1 - core) * half, 128), half)]
        keep[rows, :] = dot(left, mine)
        send[rows, :] = dot(left, other).astype(bf16)


def merge_grad(me, a0, a2, a13, dlow):
    tok, d = dlow.shape
    args = (a0, a2, a13, dlow)
    return kernel_call(
        merge_grad_kernel,
        (struct((d, d // 2), f32), struct((d, d // 2), bf16)),
        prefetch=1,
        ins=[whole(x.shape) for x in args],
        out_specs=(whole((d, d // 2), False), whole((d, d // 2), False)),
        flops=2 * tok * d * d,
        moved=4 * tok * d + 3 * d * d,
        name="merge_grad",
    )(me, *args)


def weight_kernel(na, nb, ga, gb, hid, dg, du, keep, recv, out, nt, gr):
    j = pl.program_id(0)
    tok, d = na.shape

    @pl.when(j == 0)
    def _():
        nt[:, :tok] = na[...].astype(f32).T.astype(bf16)
        nt[:, tok:] = nb[...].astype(f32).T.astype(bf16)
        gr[:tok, :] = ga[...]
        gr[tok:, :] = gb[...]
        total = (keep[...] + recv[...].astype(f32)).astype(bf16)
        for part in range(total.shape[1] // 128):
            low = 1152 + 48 * part
            out[:, low : low + 48, :] = total[:, 128 * part : 128 * (part + 1)].reshape(FORM, 48, 128)

    for base, ref in ((0, dg), (384, du)):
        grad = dot(nt[...], ref[...]).astype(bf16)
        for part in range(TILE // 128):
            at = pl.multiple_of(base + 48 * ((TILE // 128) * j + part), 16)
            out[:, pl.ds(at, 48), :] = grad[:, 128 * part : 128 * (part + 1)].reshape(FORM, 48, 128)
    turned = hid[...].astype(f32).T.astype(bf16)
    grad = dot(turned, gr[...]).astype(bf16)
    for part in range(d // 128):
        low = 768 + 64 * part
        out[pl.ds(4 * j, 4), low : low + 64, :] = grad[:, 128 * part : 128 * (part + 1)].reshape(4, 64, 128)


def weight_grads(na, nb, ga, gb, hid, dg, du, keep, recv):
    tok, d = na.shape
    units = hid.shape[1]
    args = (na, nb, ga, gb, hid, dg, du, keep, recv)
    col = pl.BlockSpec((2 * tok, TILE), lambda j: (0, j))
    shape = (FORM, 1296, 128)
    return kernel_call(
        weight_kernel,
        struct(shape, bf16),
        grid=(units // TILE,),
        ins=[whole(x.shape) for x in args[:4]] + [col, col, col] + [whole(keep.shape), whole(recv.shape)],
        out_specs=whole(shape),
        scratch=[pltpu.VMEM((d, 2 * tok), bf16), pltpu.VMEM((2 * tok, d), bf16)],
        flops=6 * 2 * tok * d * units,
        moved=12 * tok * units + 16 * tok * d,
        name="weight_grads",
    )(*args)


def regroup(stacked, parts, groups):
    count, _, width = stacked.shape
    if count == groups:
        return stacked
    pieces, low = [], 0
    for blocks, rows in parts:
        piece = stacked[:, low : low + blocks * rows].reshape(count, blocks, rows, width)
        low += blocks * rows
        piece = jnp.transpose(piece, (1, 0, 2, 3)).reshape(blocks, groups, count * rows // groups, width)
        pieces.append(jnp.transpose(piece, (1, 0, 2, 3)).reshape(groups, blocks * count * rows // groups, width))
    return jnp.concatenate(pieces, axis=1)


def to_blocks(mat, width):
    rows, cols = mat.shape
    return jnp.transpose(mat.reshape(rows, cols // width, width), (1, 0, 2)).reshape(-1, width)


def from_blocks(stacked, rows):
    blocks, width = stacked.shape[0] // rows, stacked.shape[1]
    return jnp.transpose(stacked.reshape(blocks, rows, width), (1, 0, 2)).reshape(rows, blocks * width)


def flip(x, bit):
    return lax.ppermute(x, ULY, [(i, i ^ bit) for i in range(4)])


def ordered(core, mine, theirs, axis):
    first = jnp.where(core == 0, mine, theirs)
    second = jnp.where(core == 0, theirs, mine)
    return jnp.concatenate([first, second], axis=axis)


def local(
    n_ctx,
    byte_embed,
    query_weight,
    key_weight,
    value_weight,
    merge_weight,
    gate_weight,
    up_weight,
    down_weight,
    conv_weight,
    score_weight,
    attn_gain,
    ffn_gain,
    bias_table,
    doc_lengths,
    rel_bucket,
    out_grad,
):
    nb, d = byte_embed.shape
    tok = out_grad.shape[0]
    n_dev = n_ctx * 4
    groups = n_ctx * 2
    rows_dev = query_weight.shape[0]
    down_dev = down_weight.shape[0]
    heads = HEADS // 4
    width = heads * HEAD_DIM
    group_len = tok * 4
    ext = 2 * group_len
    ff = gate_weight.shape[1]
    ctx_at = lax.axis_index("ctx")
    core = lax.axis_index("uc")
    uly_at = lax.axis_index(ULY)
    dev_at = lax.axis_index(RING)
    me = uly_at.astype(jnp.int32).reshape(1)

    up_pairs = [(i, i + 1) for i in range(n_dev - 1)]
    down_pairs = [(i + 1, i) for i in range(n_dev - 1)]
    lo = lax.ppermute(byte_embed[nb - 8 :], RING, up_pairs)
    hi = lax.ppermute(byte_embed[:8], RING, down_pairs)

    qkv_own = jnp.stack(
        [w.reshape(rows_dev, 4, width) for w in (query_weight, key_weight, value_weight)], axis=2
    ).reshape(rows_dev, 4, 3 * width)
    qkv_send = jnp.broadcast_to(
        jnp.transpose(qkv_own, (1, 0, 2))[None], (n_ctx, 4, rows_dev, 3 * width)
    ).reshape(n_dev, rows_dev, 3 * width)
    qkv_w = lax.all_to_all(qkv_send, RING, 0, 0, tiled=True).reshape(d, 3 * width)

    unit = ff // n_dev
    split = lambda w, at: lax.dynamic_index_in_dim(
        w.reshape(rows_dev, groups, 2, unit), at, 2, keepdims=False
    ).reshape(rows_dev, ff // 2)
    mine = jnp.concatenate([split(gate_weight, core), split(up_weight, core), merge_weight], axis=1)
    other = jnp.concatenate([split(gate_weight, 1 - core), split(up_weight, 1 - core), merge_weight], axis=1)
    theirs = flip(other, 1)
    both = ordered(core, mine, theirs, 0)
    packed_own = jnp.concatenate(
        [
            to_blocks(both[:, : ff // 2], TILE),
            to_blocks(both[:, ff // 2 : ff], TILE),
            to_blocks(down_weight, TILE),
            to_blocks(both[:, ff:], TILE),
        ],
        axis=0,
    )
    packed = lax.all_gather(packed_own, ("ctx", "ux"), axis=0, tiled=False)
    packed = packed.reshape(groups, packed_own.shape[0], TILE)
    packed = regroup(
        packed,
        ((4, 2 * rows_dev), (4, 2 * rows_dev), (3, down_dev), (3, 2 * rows_dev)),
        FORM,
    )
    grad_other = flip(out_grad, 1)

    count = doc_lengths.shape[0]
    order = lax.broadcasted_iota(jnp.int32, (count, count), 0)
    before = lax.broadcasted_iota(jnp.int32, (count, count), 1)
    starts = jnp.sum(jnp.where(before < order, doc_lengths[None, :], 0), axis=1)
    limit = jnp.sum(doc_lengths)

    def doc_of(places):
        found = jnp.sum((starts[None, :] <= places[:, None]).astype(jnp.int32), axis=1) - 1
        return jnp.where((places >= 0) & (places < limit), found, -1)

    byte_doc = doc_of(dev_at * nb - 16 + jnp.arange(nb + 32, dtype=jnp.int32))
    center = byte_doc[8 : nb + 24]
    msk = jnp.stack(
        [(byte_doc[8 + k - 2 : 8 + k - 2 + nb + 16] == center).astype(f32) for k in range(CONV)]
        + [jnp.zeros((nb + 16,), f32)] * (128 - CONV),
        axis=1,
    )
    tok_doc = doc_of(2 * (ctx_at * group_len - group_len // 2 + jnp.arange(ext, dtype=jnp.int32)))
    bits = count.bit_length()
    lane = jnp.arange(TILE, dtype=jnp.int32) - width
    bit_on = ((tok_doc[:, None] >> jnp.clip(lane // 2, 0, 31)[None, :]) & 1) == 1
    used = ((lane >= 0) & (lane < 2 * bits))[None, :]
    odd = (lane % 2 == 1)[None, :]
    code_k = jnp.where(used & (bit_on == odd), 1.0, 0.0).astype(bf16)
    code_q = jnp.where(used & (bit_on != odd), -BIG, 0.0).astype(bf16)[group_len // 2 : group_len // 2 + group_len]
    tiles = group_len // TILE
    first = ctx_at * group_len + TILE * jnp.arange(tiles, dtype=jnp.int32)
    begin = jnp.max(jnp.where(starts[None, :] <= 2 * first[:, None], starts[None, :], 0), axis=1)
    last = 2 * (first + TILE - 1)
    end = jnp.min(jnp.where(starts[None, :] > last[:, None], starts[None, :], limit), axis=1)
    shift = group_len // 2 - ctx_at * group_len
    tile_lo = jnp.clip(((begin + 1) // 2 + shift) // TILE, 0, ext // TILE)
    tile_hi = jnp.clip(((end - 1) // 2 + shift) // TILE + 1, 0, ext // TILE)
    info = jnp.concatenate([tile_lo, tile_hi, me]).astype(jnp.int32)

    rel_count = rel_bucket.shape[0]
    diag_len = 2 * DOC_TOK + 2 * TILE
    bucket = jnp.pad(rel_bucket, (TILE, diag_len - TILE - rel_count), constant_values=-1)
    onehot = (bucket[None, :] == jnp.arange(NBUCK, dtype=jnp.int32)[:, None]).astype(f32)
    table_here = lax.dynamic_slice_in_dim(bias_table, uly_at * heads, heads, 1)
    diag = lax.dot_general(table_here, onehot, (((0,), (0,)), ((), ())), precision=highest)
    bias = bias_tiles(diag)

    cw, sw = conv_weight, score_weight[None, :]
    gain_one, gain_two = attn_gain[None, :], ffn_gain[None, :]
    gbst, normed, conv, aw = gbst_forward(lo, byte_embed, hi, msk, cw, sw, gain_one)

    near = [(4 * c + u, 4 * (c + s) + u) for c in range(n_ctx) for u, s in ((0, -1), (1, -1), (2, 1), (3, 1)) if 0 <= c + s < n_ctx]
    far0 = lax.ppermute(normed, RING, near)
    own2 = flip(normed, 2)
    own1 = flip(normed, 1)
    own3 = flip(own2, 1)
    far2 = flip(far0, 2)
    far1 = flip(far0, 1)
    far3 = flip(far2, 1)
    own = (normed, own1, own2, own3)
    far = (far0, far1, far2, far3)
    q, k, v, wp = project(me, own, far, qkv_w)

    oa, ob, oloc, lse = attend(info, q, k, v, code_q, code_k, bias, heads, tok)
    got2 = flip(ob, 2)
    got1 = flip(jnp.stack([oa[1], got2[1]]), 1)
    att = (oa[0], got2[0], got1)
    mid, normed_two = merge(me, *att, packed, gbst, gain_two)

    normed_other = flip(normed_two, 1)
    out_a, out_b, dn_a, dn_b, hid, dgate, dup = feed(
        normed_two, normed_other, out_grad, grad_other, packed, ff // 2
    )
    dn_got = flip(dn_b, 1)
    out_got = flip(out_b, 1)
    layer_out, dmid, dlow, ga, gb2, ffn_sum = middle(
        me, mid, dn_a, dn_got, out_a, out_got, out_grad, gain_two, packed
    )
    back2 = flip(gb2, 2)
    keep_m, send_m = merge_grad(me, *att, dlow)
    recv_m = flip(send_m, 1)
    back1 = flip(jnp.stack([ga[1], back2[1]]), 1)
    grads = weight_grads(normed_two, normed_other, out_grad, grad_other, hid, dgate, dup, keep_m, recv_m)
    parts16 = ((8, 48), (8, 48), (6, 64), (3, 48))
    grads = regroup(grads, parts16, groups)
    summed = lax.psum_scatter(grads, ("ctx", "ux"), scatter_dimension=0, tiled=False)

    dq, dk, dv, dqt, dkt, dvt, tacc = attend_back(
        info, q, k, v, code_q, code_k, bias, oloc, lse, ga[0], back2[0], back1, heads
    )
    hk0, hk2, hs1, hs3 = project_back(True, me, dq, dk, dv, wp)
    h_got3 = flip(hs3, 1)
    h_mid = (hk2 + h_got3.astype(f32)).astype(bf16)
    h_got2 = flip(h_mid, 2)
    h_got1 = flip(hs1, 1)
    ok0, ok2, os1, os3 = project_back(False, me, dq, dk, dv, wp)
    o_got3 = flip(os3, 1)
    o_mid = (ok2 + o_got3.astype(f32)).astype(bf16)
    o_got2 = flip(o_mid, 2)
    o_got1 = flip(os1, 1)
    h_sum = (hk0 + h_got1.astype(f32) + h_got2.astype(f32)).astype(bf16)
    h_back = lax.ppermute(h_sum, RING, [(b, a) for a, b in near])
    o_sum = ok0 + o_got1.astype(f32) + o_got2.astype(f32)

    qkv_grad = project_grad(me, own, far, dqt, dkt, dvt)
    qkv_got = lax.all_to_all(qkv_grad.reshape(n_dev, rows_dev, 3 * width), RING, 0, 0, tiled=True)
    qkv_sum = jnp.sum(qkv_got.reshape(n_ctx, 4, rows_dev, 3, width).astype(f32), axis=0)
    qkv_sum = jnp.transpose(qkv_sum, (2, 1, 0, 3))
    query_grad, key_grad, value_grad = (
        qkv_sum[j].reshape(rows_dev, d) for j in range(3)
    )

    diag_parts = jnp.transpose(table_sums(tacc), (1, 0, 2))
    count_t = diag_parts.shape[1]
    low = diag_parts[:, :, :TILE].reshape(heads, count_t * TILE)
    high = diag_parts[:, :, TILE:].reshape(heads, count_t * TILE)
    diag_grad = jnp.pad(low, ((0, 0), (0, TILE))) + jnp.pad(high, ((0, 0), (TILE, 0)))
    table_local = lax.dot_general(onehot, diag_grad, (((1,), (1,)), ((), ())), precision=highest)
    table_grad = lax.dynamic_update_slice(jnp.zeros((NBUCK, HEADS), f32), table_local, (0, uly_at * heads))

    eg, small = gbst_backward(
        o_sum, h_back, gbst, dmid, gain_one, conv, aw, lo, byte_embed, hi, msk, cw, sw
    )
    from_prev = lax.ppermute(eg[nb + 8 :], RING, up_pairs)
    from_next = lax.ppermute(eg[:8], RING, down_pairs)
    main = eg[8 : nb + 8]
    embed_grad = jnp.concatenate(
        [main[:8] + from_prev, main[8 : nb - 8], main[nb - 8 :] + from_next], axis=0
    )

    rest = jnp.concatenate(
        [jnp.sum(ffn_sum, axis=0, keepdims=True), jnp.pad(table_grad.reshape(1, -1), ((0, 0), (0, d - NBUCK * HEADS)))],
        axis=0,
    )
    total = jnp.concatenate([small, jnp.pad(rest, ((0, 6), (0, 0)))], axis=0)
    for bit in (1, 2):
        total = total + flip(total, bit)
    bit = 1
    while bit < n_ctx:
        total = total + lax.ppermute(total, "ctx", [(i, i ^ bit) for i in range(n_ctx)])
        bit *= 2

    rows2 = 2 * rows_dev
    gate_b = from_blocks(summed[: 8 * rows2], rows2)
    up_b = from_blocks(summed[8 * rows2 : 16 * rows2], rows2)
    down_grad = from_blocks(summed[16 * rows2 : 16 * rows2 + 6 * down_dev], down_dev).astype(f32)
    merge_b = from_blocks(summed[16 * rows2 + 6 * down_dev :], rows2)
    three = jnp.concatenate([gate_b, up_b, merge_b], axis=1).reshape(2, rows_dev, -1)
    kept = lax.dynamic_index_in_dim(three, core, 0, keepdims=False)
    given = flip(lax.dynamic_index_in_dim(three, 1 - core, 0, keepdims=False), 1)
    even = jnp.where(core == 0, kept, given).astype(f32)
    odd_part = jnp.where(core == 0, given, kept).astype(f32)

    def units(low_col, cols):
        return jnp.stack(
            [x[:, low_col : low_col + cols].reshape(rows_dev, groups, unit) for x in (even, odd_part)], axis=2
        ).reshape(rows_dev, 2 * cols)

    gate_grad = units(0, ff // 2)
    up_grad = units(ff // 2, ff // 2)
    merge_g = jnp.concatenate([even[:, ff:], odd_part[:, ff:]], axis=1)
    return (
        layer_out,
        embed_grad,
        query_grad,
        key_grad,
        value_grad,
        merge_g,
        gate_grad,
        up_grad,
        down_grad,
        total[:CONV],
        total[5],
        total[6],
        total[8],
        total[9, : NBUCK * HEADS].reshape(NBUCK, HEADS),
    )


def solution(mesh):
    n_ctx = mesh.shape["ctx"]
    inner = Mesh(mesh.devices.reshape(n_ctx, 2, 2), RING)
    row = P(RING, None)
    return jax.shard_map(
        partial(local, n_ctx),
        mesh=inner,
        in_specs=(row,) * 8 + (P(),) * 7 + (row,),
        out_specs=(row,) * 9 + (P(),) * 5,
        check_vma=False,
    )
```

```python
from functools import partial

import jax
import jax.numpy as jnp
from jax import lax
from jax.experimental import pallas as pl
from jax.experimental.pallas import tpu as pltpu
from jax.sharding import Mesh, PartitionSpec as P

HEADS = 12
HEAD_DIM = 64
NBUCK = 32
CONV = 5
DOC_TOK = 1024
TILE = 256
FORM = 16
PHASES = 12
EPS = 1e-06
BIG = 1e30
GELU_C = 0.7978845608028654
GELU_A = 0.044715

bf16 = jnp.bfloat16
f32 = jnp.float32
RING = ("ctx", "ux", "uc")
ULY = ("ux", "uc")
highest = lax.Precision.HIGHEST


def dot(left, right, dims=((1,), (0,))):
    return lax.dot_general(left, right, (dims, ((), ())), preferred_element_type=f32)


def kernel_call(body, outs, *, grid=(1,), ins, scratch=(), prefetch=0, out_specs=None, flops=0, moved=0, vmem=40, name=None):
    params = pltpu.CompilerParams(
        dimension_semantics=("arbitrary",) * len(grid), vmem_limit_bytes=vmem << 20
    )
    return pl.pallas_call(
        body,
        out_shape=outs,
        grid_spec=pltpu.PrefetchScalarGridSpec(
            num_scalar_prefetch=prefetch,
            grid=grid,
            in_specs=ins,
            out_specs=out_specs,
            scratch_shapes=list(scratch),
        ),
        compiler_params=params,
        cost_estimate=pl.CostEstimate(flops=int(flops), bytes_accessed=int(moved), transcendentals=0),
        name=name,
    )


def whole(shape, once=True):
    zeros = (0,) * len(shape)
    if once:
        return pl.BlockSpec(shape, lambda *a: zeros, pipeline_mode=pl.Buffered(1))
    return pl.BlockSpec(shape, lambda *a: zeros)


def in_hbm(*arrays):
    return tuple(pltpu.with_memory_space_constraint(x, pltpu.HBM) for x in arrays)


def struct(shape, dtype):
    return jax.ShapeDtypeStruct(shape, dtype)


def block_of(size, at):
    first = size * (at // size)
    return range(first, first + size)


def token_pairs(tok):
    found = set()
    for byte in (2 * tok, 2 * tok + 1):
        for size in range(1, 5):
            found |= set(block_of(size, byte))
    return sorted(found)


def mix_coefs(weights):
    coefs = {}
    for tok in range(PHASES // 2):
        for at in token_pairs(tok):
            total = None
            for byte in (2 * tok, 2 * tok + 1):
                for size in range(1, 5):
                    if at in block_of(size, byte):
                        term = weights[size - 1][byte] * (0.5 / size)
                        total = term if total is None else total + term
            coefs[tok, at] = total
    return coefs


def lane_chunks(feats):
    return [slice(128 * c, 128 * (c + 1)) for c in range(feats // 128)]


def fill_bytes(pad, lo, emb, hi):
    byte_count, feats = emb.shape
    chunks = lane_chunks(feats)
    for c, cols in enumerate(chunks):
        pad[c, 0:8, :] = lo[:, cols].astype(f32)
        pad[c, 8 + byte_count : 16 + byte_count, :] = hi[:, cols].astype(f32)

    def fill(t, _):
        at = pl.multiple_of(t * 32, 32)
        for c, cols in enumerate(chunks):
            pad[c, pl.ds(at + 8, 32), :] = emb[pl.ds(at, 32), cols].astype(f32)
        return 0

    lax.fori_loop(0, byte_count // 32, fill, 0)


def gbst_forward_kernel(lo, emb, hi, msk, cw, sw, gain, gb, nrm, conv, aw, pad, mix):
    byte_count, feats = emb.shape
    chunks = lane_chunks(feats)
    fill_bytes(pad, lo, emb, hi)
    lanes = lax.broadcasted_iota(jnp.int32, (8, 128), 1)

    def step(g, _):
        base = g * 8 * PHASES + 8
        rows = pl.ds(pl.multiple_of(8 * g, 8), 8)
        first = []
        for p in range(PHASES):
            mask = msk[pl.ds(base + p, 8, stride=PHASES), :]
            same = {k: jnp.broadcast_to(mask[:, k : k + 1], (8, 128)) for k in (0, 1, 3, 4)}
            dots = None
            for c, cols in enumerate(chunks):
                x = pad[c, pl.ds(base + p, 8, stride=PHASES), :] * cw[2:3, cols]
                for k in (0, 1, 3, 4):
                    x = x + pad[c, pl.ds(base + p + k - 2, 8, stride=PHASES), :] * same[k] * cw[k : k + 1, cols]
                conv[p, rows, cols] = x
                term = x * sw[:, cols]
                dots = term if dots is None else dots + term
            first.append(jnp.broadcast_to(jnp.sum(dots, axis=1, keepdims=True), (8, 128)))
        weights = [[None] * PHASES for _ in range(4)]
        packed = jnp.zeros((8, 128), f32)
        for p in range(PHASES):
            scores = []
            for size in range(1, 5):
                total = None
                for at in block_of(size, p):
                    total = first[at] if total is None else total + first[at]
                scores.append(total * (1.0 / size))
            top = jnp.maximum(jnp.maximum(scores[0], scores[1]), jnp.maximum(scores[2], scores[3]))
            exps = [jnp.exp(s - top) for s in scores]
            inv = 1.0 / (exps[0] + exps[1] + exps[2] + exps[3])
            for size in range(4):
                weights[size][p] = exps[size] * inv
                packed = jnp.where(lanes == 4 * p + size, weights[size][p], packed)
        aw[rows, :] = packed
        coefs = mix_coefs(weights)
        for tok in range(PHASES // 2):
            for c, cols in enumerate(chunks):
                out = None
                for at in token_pairs(tok):
                    term = coefs[tok, at] * conv[at, rows, cols]
                    out = term if out is None else out + term
                mix[c, pl.ds(g * 4 * PHASES + tok, 8, stride=PHASES // 2), :] = out
        return 0

    lax.fori_loop(0, byte_count // (8 * PHASES), step, 0)

    def norm(t, _):
        at = pl.multiple_of(t * 16, 16)
        v = jnp.concatenate([mix[c, pl.ds(at, 16), :] for c in range(len(chunks))], axis=1)
        r = lax.rsqrt(jnp.mean(v * v, axis=1, keepdims=True) + EPS)
        gb[pl.ds(at, 16), :] = v
        nrm[pl.ds(at, 16), :] = (v * r * gain[...]).astype(bf16)
        return 0

    lax.fori_loop(0, byte_count // 32, norm, 0)


def gbst_forward(lo, emb, hi, msk, cw, sw, gain):
    nb, d = emb.shape
    return kernel_call(
        gbst_forward_kernel,
        (
            struct((nb // 2, d), f32),
            struct((nb // 2, d), bf16),
            struct((PHASES, nb // PHASES, d), f32),
            struct((nb // PHASES, 128), f32),
        ),
        ins=[whole(x.shape) for x in (lo, emb, hi, msk, cw, sw, gain)],
        out_specs=(
            whole((nb // 2, d)),
            whole((nb // 2, d)),
            whole((PHASES, nb // PHASES, d)),
            whole((nb // PHASES, 128)),
        ),
        scratch=[pltpu.VMEM((d // 128, nb + 16, 128), f32), pltpu.VMEM((d // 128, nb // 2, 128), f32)],
        flops=60 * nb * d,
        moved=20 * nb * d,
        vmem=20,
        name="gbst_forward",
    )(lo, emb, hi, msk, cw, sw, gain)


def gbst_backward_kernel(keep, recv, gb, dmid, gain, conv, aw, lo, emb, hi, msk, cw, sw, eg, small, dtok, dconv, pad, acc):
    byte_count, feats = emb.shape
    chunks = lane_chunks(feats)
    acc[...] = jnp.zeros_like(acc)
    fill_bytes(pad, lo, emb, hi)
    for c in range(len(chunks)):
        dconv[c, 0:16, :] = jnp.zeros((16, 128), f32)
        dconv[c, 16 + byte_count : 32 + byte_count, :] = jnp.zeros((16, 128), f32)

    def norm(t, _):
        at = pl.multiple_of(t * 16, 16)
        e = keep[pl.ds(at, 16), :] + recv[pl.ds(at, 16), :].astype(f32)
        v = gb[pl.ds(at, 16), :]
        r = lax.rsqrt(jnp.mean(v * v, axis=1, keepdims=True) + EPS)
        ge = gain[...] * e
        m = jnp.mean(ge * v, axis=1, keepdims=True)
        out = dmid[pl.ds(at, 16), :] + r * ge - v * (r * r * r * m)
        for c, cols in enumerate(chunks):
            dtok[c, pl.ds(at, 16), :] = out[:, cols]
        part = e * v * r
        acc[48:56, :] = acc[48:56, :] + part[0:8] + part[8:16]
        return 0

    lax.fori_loop(0, byte_count // 32, norm, 0)

    def step(g, _):
        rows = pl.ds(pl.multiple_of(8 * g, 8), 8)
        half = PHASES // 2

        def tok_rows(tok, c):
            return dtok[c, pl.ds(g * 8 * half + tok, 8, stride=half), :]

        inner = {}
        for tok in range(half):
            toks = [tok_rows(tok, c) for c in range(len(chunks))]
            for at in token_pairs(tok):
                dots = None
                for c, cols in enumerate(chunks):
                    term = toks[c] * conv[at, rows, cols]
                    dots = term if dots is None else dots + term
                inner[tok, at] = jnp.broadcast_to(jnp.sum(dots, axis=1, keepdims=True), (8, 128))
        tile = aw[rows, :]
        weights = [
            [jnp.broadcast_to(tile[:, 4 * p + size : 4 * p + size + 1], (8, 128)) for p in range(PHASES)]
            for size in range(4)
        ]
        coefs = mix_coefs(weights)
        dsize = [[None] * PHASES for _ in range(4)]
        for p in range(PHASES):
            cs = []
            for size in range(1, 5):
                total = None
                for at in block_of(size, p):
                    total = inner[p // 2, at] if total is None else total + inner[p // 2, at]
                cs.append(total * (0.5 / size))
            mean = sum(weights[s][p] * cs[s] for s in range(4))
            for s in range(4):
                dsize[s][p] = weights[s][p] * (cs[s] - mean)
        slopes = []
        for at in range(PHASES):
            e = None
            for size in range(1, 5):
                for p in block_of(size, at):
                    term = dsize[size - 1][p] * (1.0 / size)
                    e = term if e is None else e + term
            slopes.append(e)
        for c, cols in enumerate(chunks):
            toks = [tok_rows(tok, c) for tok in range(half)]
            score = acc[40:48, cols]
            for at in range(PHASES):
                out = slopes[at] * sw[:, cols]
                for tok in range(half):
                    if (tok, at) in coefs:
                        out = out + coefs[tok, at] * toks[tok]
                dconv[c, pl.ds(g * 8 * PHASES + 16 + at, 8, stride=PHASES), :] = out
                score = score + slopes[at] * conv[at, rows, cols]
            acc[40:48, cols] = score
        return 0

    lax.fori_loop(0, byte_count // (8 * PHASES), step, 0)

    def taps(t, _):
        masks = []
        for u in range(2):
            mask = msk[pl.ds(pl.multiple_of(t * 16 + 8 * u, 8), 8), :]
            masks.append({k: jnp.broadcast_to(mask[:, 4 - k : 5 - k], (8, 128)) for k in (0, 1, 3, 4)})
        for c, cols in enumerate(chunks):
            sums = [None] * CONV
            for u in range(2):
                at = pl.multiple_of(t * 16 + 8 * u, 8)
                x = pad[c, pl.ds(at, 8), :]
                out = None
                for k in range(CONV):
                    z = dconv[c, pl.ds(at + 8 + 2 - k, 8), :]
                    if k != 2:
                        z = z * masks[u][k]
                    term = z * cw[k : k + 1, cols]
                    out = term if out is None else out + term
                    sums[k] = z * x if sums[k] is None else sums[k] + z * x
                eg[pl.ds(at, 8), cols] = out
            for k in range(CONV):
                acc[8 * k : 8 * k + 8, cols] = acc[8 * k : 8 * k + 8, cols] + sums[k]
        return 0

    lax.fori_loop(0, (byte_count + 16) // 16, taps, 0)
    small[...] = jnp.zeros_like(small)
    for k in range(7):
        small[k : k + 1, :] = jnp.sum(acc[8 * k : 8 * k + 8, :], axis=0, keepdims=True)


def gbst_backward(keep, recv, gb, dmid, gain, conv, aw, lo, emb, hi, msk, cw, sw):
    nb, d = emb.shape
    args = (keep, recv, *in_hbm(gb, dmid, gain, conv, aw, lo, emb, hi, msk, cw, sw))
    return kernel_call(
        gbst_backward_kernel,
        (struct((nb + 16, d), f32), struct((8, d), f32)),
        ins=[whole(x.shape) for x in args],
        out_specs=(whole((nb + 16, d)), whole((8, d))),
        scratch=[
            pltpu.VMEM((d // 128, nb // 2, 128), f32),
            pltpu.VMEM((d // 128, nb + 32, 128), f32),
            pltpu.VMEM((d // 128, nb + 16, 128), f32),
            pltpu.VMEM((56, d), f32),
        ],
        flops=120 * nb * d,
        moved=24 * nb * d,
        vmem=28,
        name="gbst_backward",
    )(*args)


def halo_row(who, tok_dev, ext):
    return jnp.where(who >= 2, (who - 2) * tok_dev, ext - 2 * tok_dev + who * tok_dev)


def project_kernel(n_heads, info, *refs):
    own, far, w, cq, ck, (q, k, v, vt, wp) = refs[:4], refs[4:8], refs[8], refs[9], refs[10], refs[11:16]
    tok, _ = own[0].shape
    me = info[0]
    part = w.shape[2] // 3
    rows = w.shape[1]
    wp[...] = jnp.zeros_like(wp)
    for b in range(w.shape[0]):
        at = pl.ds(pl.multiple_of(info[1 + b] * rows, 16), rows)
        block = w[b]
        for j in range(3):
            wp[at, TILE * j : TILE * j + part] = block[:, part * j : part * (j + 1)]
    ext = k.shape[0]
    left = (ext - q.shape[0]) // 2
    for rel in range(4):
        who = me ^ rel
        out = dot(own[rel][...], wp[...])
        at = pl.ds(pl.multiple_of(who * tok, 128), tok)
        q[at, :] = out[:, :TILE].astype(bf16) + cq[at, :]
        edge = dot(far[rel][...], wp[:, TILE:])
        for at, ks, vs in (
            (left + who * tok, out[:, TILE : 2 * TILE], out[:, 2 * TILE :]),
            (halo_row(who, tok, ext), edge[:, :TILE], edge[:, TILE:]),
        ):
            at = pl.ds(pl.multiple_of(at, 128), tok)
            k[at, :] = ks.astype(bf16) + ck[at, :]
            v[at, :] = vs.astype(bf16)
            vt[:, at] = vs.T.astype(bf16)


def project(info, own, far, w, cq, ck, n_heads):
    tok, d = own[0].shape
    rows, ext = 4 * tok, 8 * tok
    args = (*own, *far, w, cq, ck)
    shapes = [(rows, TILE), (ext, TILE), (ext, TILE), (TILE, ext), (d, 3 * TILE)]
    return kernel_call(
        partial(project_kernel, n_heads),
        tuple(struct(x, bf16) for x in shapes),
        prefetch=1,
        ins=[whole(x.shape) for x in args],
        out_specs=tuple(whole(x) for x in shapes),
        flops=2 * ext * d * 3 * TILE,
        moved=2 * (ext * d + 2 * ext * TILE + d * d),
        vmem=30,
        name="project",
    )(info, *args)


def project_back_kernel(is_halo, me, dq, dk, dv, wp, keep0, keep2, send1, send3):
    tok = keep0.shape[0]
    ext = dk.shape[0]
    left = (ext - dq.shape[0]) // 2
    for rel, ref in ((3, send3), (1, send1), (2, keep2), (0, keep0)):
        who = me[0] ^ rel
        if is_halo:
            at = pl.multiple_of(halo_row(who, tok, ext), 128)
            out = dot(dk[pl.ds(at, tok), :], wp[:, TILE : 2 * TILE], ((1,), (1,)))
        else:
            at = pl.multiple_of(left + who * tok, 128)
            out = dot(dk[pl.ds(at, tok), :], wp[:, TILE : 2 * TILE], ((1,), (1,)))
            mine = pl.multiple_of(who * tok, 128)
            out = out + dot(dq[pl.ds(mine, tok), :], wp[:, :TILE], ((1,), (1,)))
        out = out + dot(dv[pl.ds(at, tok), :], wp[:, 2 * TILE :], ((1,), (1,)))
        ref[...] = out.astype(ref.dtype)


def project_back(is_halo, me, dq, dk, dv, wp):
    ext, d = dk.shape[0], wp.shape[0]
    tok = ext // 8
    args = (dq, dk, dv, wp)
    kinds = (f32, f32, bf16, bf16)
    return kernel_call(
        partial(project_back_kernel, is_halo),
        tuple(struct((tok, d), kind) for kind in kinds),
        prefetch=1,
        ins=[whole(x.shape) for x in args],
        out_specs=tuple(whole((tok, d)) for _ in kinds),
        flops=2 * ext // 2 * d * 3 * TILE,
        moved=4 * ext * d,
        vmem=20,
        name="project_back",
    )(me, *args)


def project_grad_kernel(info, *refs):
    own, far, (dq, dk, dv, mkeep, mrecv, mgot), out, flat = refs[:4], refs[4:8], refs[8:14], refs[14], refs[15]
    tok = own[0].shape[0]
    ext = dk.shape[0]
    me = info[0]
    left = (ext - dq.shape[0]) // 2
    part = mgot.shape[1]
    totals = [None] * 3

    def turned(ref, at):
        return ref[pl.ds(pl.multiple_of(at, 128), tok), :].astype(f32).T[:part].astype(bf16)

    for rel in range(4):
        who = me ^ rel
        at = left + who * tok
        edge = halo_row(who, tok, ext)
        terms = [
            dot(turned(dq, who * tok), own[rel][...]),
            dot(turned(dk, at), own[rel][...]) + dot(turned(dk, edge), far[rel][...]),
            dot(turned(dv, at), own[rel][...]) + dot(turned(dv, edge), far[rel][...]),
        ]
        totals = [t if x is None else x + t for x, t in zip(totals, terms)]
    for j in range(3):
        flat[:, part * j : part * (j + 1)] = totals[j].T.astype(bf16)
    merged = mkeep[0] + mrecv[0].astype(f32) + mgot[...].astype(f32)
    flat[:, 3 * part :] = merged.astype(bf16)
    rows = out.shape[1]
    for b in range(out.shape[0]):
        out[b] = flat[pl.ds(pl.multiple_of(info[1 + b] * rows, 16), rows), :]


def project_grad(info, own, far, dq, dk, dv, mkeep, mrecv, mgot, blocks):
    tok, d = own[0].shape
    args = (*in_hbm(*own, *far), dq, dk, dv, *in_hbm(mkeep, mrecv, mgot))
    shape = (blocks, d // blocks, 4 * mgot.shape[1])
    return kernel_call(
        project_grad_kernel,
        struct(shape, bf16),
        prefetch=1,
        ins=[whole(x.shape) for x in args],
        out_specs=whole(shape),
        scratch=[pltpu.VMEM((d, shape[2]), bf16)],
        flops=2 * 8 * tok * d * 3 * mgot.shape[1],
        moved=2 * 12 * tok * d,
        vmem=28,
        name="project_grad",
    )(info, *args)


def fill_bias(diag, bias):
    count = bias.shape[0]
    heads = diag.shape[0]

    def tile(t, _):
        seg = diag[:, pl.ds(pl.multiple_of((count - 1 - t) * TILE, TILE), 2 * TILE)]
        for h in range(heads):
            rows = jnp.broadcast_to(seg[h : h + 1, :], (TILE, 2 * TILE))
            turned = pltpu.roll(rows, TILE, axis=1, stride=1, stride_axis=0)
            bias[t, :, TILE * h : TILE * (h + 1)] = turned[:, :TILE]
        return 0

    lax.fori_loop(0, count, tile, 0)


def sum_diagonals(tiles, out):
    count, heads, _ = out.shape

    def tile(t, _):
        for h in range(heads):
            part = tiles[t, :, TILE * h : TILE * (h + 1)]
            cur = jnp.concatenate([part, jnp.zeros_like(part)], axis=1)
            rows = TILE
            while rows > 8:
                rows //= 2
                cur = cur[:rows] + pltpu.roll(cur[rows:], 2 * TILE - rows, axis=1)
            total = cur[0:1]
            for i in range(1, 8):
                total = total + pltpu.roll(cur[i : i + 1], 2 * TILE - i, axis=1)
            out[count - 1 - t, h : h + 1, :] = pltpu.roll(total, TILE, axis=1)
        return 0

    lax.fori_loop(0, count, tile, 0)


def lane_head(shape):
    return lax.broadcasted_iota(jnp.int32, shape, 1) // HEAD_DIM


def fill_queries(heads, q, q3):
    turned = q[...].astype(f32).T
    row = lax.broadcasted_iota(jnp.int32, (TILE, TILE), 0) // HEAD_DIM
    for h in range(heads):
        q3[:, TILE * h : TILE * (h + 1)] = jnp.where((row == h) | (row >= heads), turned, 0.0).astype(bf16)


def attend_kernel(heads, info, q, k, vt, diag, oa, ob, oloc, lse, bias, q3, sc, ac):
    i = pl.program_id(0)
    grid = pl.num_programs(0)
    me = info[2 * grid]
    ext = k.shape[0]
    wide = heads * TILE

    @pl.when(i == 0)
    def _():
        fill_bias(diag, bias)

    lo, hi = info[i], info[grid + i]
    away = (ext // TILE - grid) // 2
    fill_queries(heads, q, q3)
    ac[...] = jnp.zeros_like(ac)

    def scores(kt, top):
        at = pl.multiple_of(kt * TILE, TILE)
        s = dot(k[pl.ds(at, TILE), :], q3[...]) + bias[kt - i - away + 4]
        sc[kt - lo] = s
        return jnp.maximum(top, jnp.max(s.reshape(TILE // 8, 8, wide), axis=0))

    top = lax.fori_loop(lo, hi, scores, jnp.full((8, wide), -jnp.inf, f32))
    top = jnp.max(top, axis=0, keepdims=True)

    def gather(kt, total):
        at = pl.multiple_of(kt * TILE, TILE)
        p = jnp.exp(sc[kt - lo] - top)
        low = p.astype(bf16)
        for h in range(heads):
            cols = slice(TILE * h, TILE * (h + 1))
            head = slice(HEAD_DIM * h, HEAD_DIM * (h + 1))
            ac[head, :] = ac[head, :] + dot(vt[head, pl.ds(at, TILE)], low[:, cols])
        return total + jnp.sum(p.reshape(TILE // 8, 8, wide), axis=0)

    total = lax.fori_loop(lo, hi, gather, jnp.zeros((8, wide), f32))
    total = jnp.sum(total, axis=0, keepdims=True)
    inv = 1.0 / total
    lse[0] = jnp.broadcast_to(top + jnp.log(total), (8, wide))
    parts = []
    for h in range(heads):
        parts.append(ac[HEAD_DIM * h : HEAD_DIM * (h + 1), :] * inv[:, TILE * h : TILE * (h + 1)])
    turned = jnp.concatenate(parts, axis=0).astype(bf16)
    oloc[...] = turned
    per = oa.shape[1]
    for j in range(TILE // 128):
        chunk = i * (TILE // 128) + j
        rel = (chunk // per) ^ me
        piece = turned[:, 128 * j : 128 * (j + 1)]

        @pl.when(rel < 2)
        def _():
            oa[rel, chunk % per] = piece

        @pl.when(rel >= 2)
        def _():
            ob[rel - 2, chunk % per] = piece


def attend(info, q, k, vt, diag, heads, tok):
    rows, ext = q.shape[0], k.shape[0]
    grid = rows // TILE
    width = heads * HEAD_DIM
    sent = (2, tok // 128, width, 128)
    tile = pl.BlockSpec((TILE, TILE), lambda i, *_: (i, 0))
    return kernel_call(
        partial(attend_kernel, heads),
        (
            struct(sent, bf16),
            struct(sent, bf16),
            struct((width, rows), bf16),
            struct((grid, 8, heads * TILE), f32),
        ),
        grid=(grid,),
        prefetch=1,
        ins=[tile, whole(k.shape), whole(vt.shape), whole(diag.shape)],
        out_specs=(
            whole(sent),
            whole(sent),
            pl.BlockSpec((width, TILE), lambda i, *_: (0, i)),
            pl.BlockSpec((1, 8, heads * TILE), lambda i, *_: (i, 0, 0)),
        ),
        scratch=[
            pltpu.VMEM((9, TILE, heads * TILE), f32),
            pltpu.VMEM((TILE, heads * TILE), bf16),
            pltpu.VMEM((9, TILE, heads * TILE), f32),
            pltpu.VMEM((width, TILE), f32),
        ],
        flops=4 * rows * 1280 * TILE * heads,
        moved=8 * ext * TILE,
        vmem=30,
        name="attend",
    )(info, q, k, vt, diag)


def attend_back_kernel(
    heads, info, q, k, v, diag, oloc, lse, d0, d1, d2, d3,
    dq, dk, dv, sums,
    bias, tacc, kt_all, q3, g3, q3n, g3n, gall, dqa, dka, dva,
):
    i = pl.program_id(0)
    grid = pl.num_programs(0)
    me = info[2 * grid]
    ext = k.shape[0]
    per = d0.shape[0]
    width = heads * HEAD_DIM

    @pl.when(i == 0)
    def _():
        fill_bias(diag, bias)

        def turn(t, _):
            at = pl.ds(pl.multiple_of(t * TILE, TILE), TILE)
            kt_all[:, at] = k[at, :].astype(f32).T[:width].astype(bf16)
            return 0

        lax.fori_loop(0, ext // TILE, turn, 0)
        dka[...] = jnp.zeros_like(dka)
        dva[...] = jnp.zeros_like(dva)
        tacc[...] = jnp.zeros_like(tacc)
        for rel, piece in ((0, d0[...]), (2, d2[...]), (1, d1[...]), (3, d3[...])):
            gall[pl.ds((me ^ rel) * per, per)] = piece

    lo, hi = info[i], info[grid + i]
    away = (ext // TILE - grid) // 2
    where = lane_head((TILE, TILE))
    fill = jnp.zeros((TILE - width, TILE), f32)
    pieces = [gall[i * (TILE // 128) + j] for j in range(TILE // 128)]
    gt = jnp.concatenate(pieces, axis=1).astype(f32)
    grad = jnp.concatenate([gt, fill], axis=0).T
    prod = gt * oloc[...].astype(f32)
    deltas = []
    fill_queries(heads, q, q3)
    g3[...] = jnp.zeros_like(g3)
    for h in range(heads):
        rows = slice(TILE * h, TILE * (h + 1))
        head = slice(HEAD_DIM * h, HEAD_DIM * (h + 1))
        g3[head, rows] = gt[head, :].astype(bf16)
        q3n[rows, :] = jnp.where(where == h, q[...], jnp.zeros_like(q[...]))
        g3n[rows, :] = jnp.where(where == h, grad, 0.0).astype(bf16)
        deltas.append(jnp.sum(prod[HEAD_DIM * h : HEAD_DIM * (h + 1), :], axis=0, keepdims=True))
    delta = jnp.concatenate(deltas, axis=1)
    log = lse[0, 0:1, :]
    dqa[...] = jnp.zeros_like(dqa)

    def step(kt, _):
        at = pl.ds(pl.multiple_of(kt * TILE, TILE), TILE)
        rel = kt - i - away + 4
        s = dot(k[at, :], q3[...]) + bias[rel]
        p = jnp.exp(s - log)
        dp = dot(v[at, :], g3[...])
        ds = p * (dp - delta)
        tacc[rel] = tacc[rel] + ds
        low = ds.astype(bf16)
        dva[at, :] = dva[at, :] + dot(p.astype(bf16), g3n[...])
        dka[at, :] = dka[at, :] + dot(low, q3n[...])
        for h in range(heads):
            head = slice(HEAD_DIM * h, HEAD_DIM * (h + 1))
            dqa[head, :] = dqa[head, :] + dot(kt_all[head, at], low[:, TILE * h : TILE * (h + 1)])
        return 0

    lax.fori_loop(lo, hi, step, 0)
    dq[...] = jnp.concatenate([dqa[...], fill], axis=0).T.astype(bf16)

    @pl.when(i == grid - 1)
    def _():
        dk[...] = dka[...].astype(bf16)
        dv[...] = dva[...].astype(bf16)
        sum_diagonals(tacc, sums)


def attend_back(info, q, k, v, diag, oloc, lse, d0, d1, d2, d3, heads):
    rows, ext = q.shape[0], k.shape[0]
    grid = rows // TILE
    width = heads * HEAD_DIM
    tile = pl.BlockSpec((TILE, TILE), lambda i, *_: (i, 0))
    turned = pl.BlockSpec((width, TILE), lambda i, *_: (0, i))
    sums = (9, heads, 2 * TILE)
    return kernel_call(
        partial(attend_back_kernel, heads),
        (
            struct((rows, TILE), bf16),
            struct((ext, TILE), bf16),
            struct((ext, TILE), bf16),
            struct(sums, f32),
        ),
        grid=(grid,),
        prefetch=1,
        ins=[
            tile, whole(k.shape), whole(v.shape), whole(diag.shape),
            turned, pl.BlockSpec((1, 8, heads * TILE), lambda i, *_: (i, 0, 0)),
            whole(d0.shape), whole(d1.shape), whole(d2.shape), whole(d3.shape),
        ],
        out_specs=(tile, whole((ext, TILE)), whole((ext, TILE)), whole(sums)),
        scratch=[
            pltpu.VMEM((9, TILE, heads * TILE), f32),
            pltpu.VMEM((9, TILE, heads * TILE), f32),
            pltpu.VMEM((width, ext), bf16),
            pltpu.VMEM((TILE, heads * TILE), bf16),
            pltpu.VMEM((TILE, heads * TILE), bf16),
            pltpu.VMEM((heads * TILE, TILE), bf16),
            pltpu.VMEM((heads * TILE, TILE), bf16),
            pltpu.VMEM((rows // 128, width, 128), bf16),
            pltpu.VMEM((width, TILE), f32),
            pltpu.VMEM((ext, TILE), f32),
            pltpu.VMEM((ext, TILE), f32),
        ],
        flops=10 * rows * 1280 * TILE * heads,
        moved=16 * ext * TILE,
        vmem=44,
        name="attend_back",
    )(info, *in_hbm(q, k, v, diag, oloc, lse), d0, d1, d2, d3)


MERGE_ROWS = pl.BlockSpec((FORM, 144, TILE), lambda *a: (0, 4, 0), pipeline_mode=pl.Buffered(1))


def merge_rows(packed, src, part):
    span = FORM // 4
    low = 48 * part
    return packed[pl.ds(src * span, span), low : low + 48, :].reshape(48 * span, TILE)


def merge_kernel(info, a0, a1, a2, a3, packed, gb, gain, mid, nrm):
    per = a0.shape[0]
    for t in range(per):
        rows = slice(128 * t, 128 * (t + 1))
        total = [gb[rows, TILE * part : TILE * (part + 1)] for part in range(3)]
        for rel, piece in ((0, a0[t]), (2, a2[t]), (1, a1[t]), (3, a3[t])):
            flat = piece.astype(f32).T.astype(bf16)
            for part in range(3):
                total[part] = total[part] + dot(flat, merge_rows(packed, info[0] ^ rel, part))
        v = jnp.concatenate(total, axis=1)
        mid[rows, :] = v
        r = lax.rsqrt(jnp.mean(v * v, axis=1, keepdims=True) + EPS)
        nrm[rows, :] = (v * r * gain[...]).astype(bf16)


def merge(me, a0, a1, a2, a3, packed, gb, gain):
    tok, d = gb.shape
    args = (a0, a1, a2, a3, packed, gb, gain)
    specs = [MERGE_ROWS if x is packed else whole(x.shape) for x in args]
    args = in_hbm(*args)
    return kernel_call(
        merge_kernel,
        (struct((tok, d), f32), struct((tok, d), bf16)),
        prefetch=1,
        ins=specs,
        out_specs=(whole((tok, d)), whole((tok, d))),
        flops=2 * tok * d * d,
        moved=12 * tok * d,
        vmem=20,
        name="merge",
    )(me, *args)


def feed_kernel(nt, gr, wg, wu, wd, out, dn, hid, dg, du, osum, dsum):
    j = pl.program_id(0)

    @pl.when(j == 0)
    def _():
        osum[...] = jnp.zeros_like(osum)
        dsum[...] = jnp.zeros_like(dsum)

    wgt = wg[...].reshape(FORM * 48, TILE)
    wut = wu[...].reshape(FORM * 48, TILE)
    gate = dot(nt[...], wgt)
    up = dot(nt[...], wut)
    dh = None
    wds = []
    for part in range(3):
        wdt = wd[:, 64 * part : 64 * (part + 1), :].reshape(TILE, TILE)
        wds.append(wdt)
        term = dot(gr[:, TILE * part : TILE * (part + 1)], wdt, ((1,), (1,)))
        dh = term if dh is None else dh + term
    sq = gate * gate
    th = jnp.tanh(GELU_C * gate * (1.0 + GELU_A * sq))
    half = 0.5 * (1.0 + th)
    act = gate * half
    slope = half + 0.5 * gate * (1.0 - th * th) * (GELU_C * (1.0 + 3.0 * GELU_A * sq))
    h = (act * up).astype(bf16)
    g = (dh * up * slope).astype(bf16)
    u = (dh * act).astype(bf16)
    hid[...] = h
    dg[...] = g
    du[...] = u
    for part in range(3):
        cols = slice(TILE * part, TILE * (part + 1))
        osum[:, cols] = osum[:, cols] + dot(h, wds[part])
    dsum[...] = dsum[...] + dot(g, wgt, ((1,), (1,))) + dot(u, wut, ((1,), (1,)))

    @pl.when(j == pl.num_programs(0) - 1)
    def _():
        out[...] = osum[...].astype(out.dtype)
        dn[...] = dsum[...].astype(dn.dtype)


def feed(nt, gr, packed, units, kind):
    tok, d = nt.shape
    col = pl.BlockSpec((tok, TILE), lambda j: (0, j))
    full = whole((tok, d))
    return kernel_call(
        feed_kernel,
        (struct((tok, d), kind), struct((tok, d), kind)) + (struct((tok, units), bf16),) * 3,
        grid=(units // TILE,),
        ins=[
            full,
            full,
            pl.BlockSpec((FORM, 48, TILE), lambda j: (0, j, 0)),
            pl.BlockSpec((FORM, 48, TILE), lambda j: (0, 4 + j, 0)),
            pl.BlockSpec((4, 192, TILE), lambda j: (j, 2, 0)),
        ],
        out_specs=(full, full, col, col, col),
        scratch=[pltpu.VMEM((tok, d), f32), pltpu.VMEM((tok, d), f32)],
        flops=12 * tok * d * units,
        moved=2 * packed.size + 10 * tok * d + 6 * tok * units,
        vmem=24,
        name="feed",
    )(nt, gr, packed, packed, packed)


def middle_kernel(info, mid, da, db, og, gain, packed, dmid, dlow, ga, gb, gsum):
    tok, d = mid.shape
    gsum[...] = jnp.zeros_like(gsum)

    def norm(t, _):
        at = pl.ds(pl.multiple_of(t * 16, 16), 16)
        v = mid[at, :]
        e = da[at, :] + db[at, :].astype(f32)
        r = lax.rsqrt(jnp.mean(v * v, axis=1, keepdims=True) + EPS)
        ge = gain[...] * e
        m = jnp.mean(ge * v, axis=1, keepdims=True)
        out = og[at, :].astype(f32) + r * ge - v * (r * r * r * m)
        dmid[at, :] = out
        dlow[at, :] = out.astype(bf16)
        part = e * v * r
        gsum[...] = gsum[...] + part[0:8] + part[8:16]
        return 0

    lax.fori_loop(0, tok // 16, norm, 0)
    for rel in range(4):
        out = None
        for part in range(3):
            cols = slice(TILE * part, TILE * (part + 1))
            term = dot(merge_rows(packed, info[0] ^ rel, part), dlow[:, cols], ((1,), (1,)))
            out = term if out is None else out + term
        low = out.astype(bf16)
        for t in range(tok // 128):
            ref = ga if rel < 2 else gb
            ref[rel % 2, t] = low[:, 128 * t : 128 * (t + 1)]


def middle(me, mid, da, db, og, gain, packed):
    tok, d = mid.shape
    args = (mid, da, db, og, gain, packed)
    sent = (2, tok // 128, d // 4, 128)
    shapes = [((tok, d), f32), ((tok, d), bf16), (sent, bf16), (sent, bf16), ((8, d), f32)]
    return kernel_call(
        middle_kernel,
        tuple(struct(*s) for s in shapes),
        prefetch=1,
        ins=[MERGE_ROWS if x is packed else whole(x.shape) for x in args],
        out_specs=tuple(whole(s[0]) for s in shapes),
        flops=2 * tok * d * d,
        moved=30 * tok * d,
        vmem=24,
        name="middle",
    )(me, mid, da, db, *in_hbm(og, gain, packed))


def merge_grad_kernel(info, a0, a1, a2, a3, dlow, keep, send):
    per = a0.shape[0]
    width = a0.shape[1]
    me = info[0]
    for rel in range(4):
        pieces = [(a0[t], a1[t], a2[t], a3[t])[rel] for t in range(per)]
        left = jnp.concatenate(pieces, axis=1)
        rows = pl.ds(pl.multiple_of((me ^ rel) * width, 64), width)
        out = dot(left, dlow[...])
        for part in range(4):
            cols = out[:, width * part : width * (part + 1)]
            far = me ^ part

            @pl.when(far % 2 == 0)
            def _():
                keep[far // 2, rows, :] = cols

            @pl.when(far % 2 == 1)
            def _():
                send[far // 2, rows, :] = cols.astype(bf16)


def merge_grad(info, a0, a1, a2, a3, dlow):
    tok, d = dlow.shape
    args = (*in_hbm(a0, a1, a2, a3), dlow)
    shape = (2, d, d // 4)
    return kernel_call(
        merge_grad_kernel,
        (struct(shape, f32), struct(shape, bf16)),
        prefetch=1,
        ins=[whole(x.shape) for x in args],
        out_specs=(whole(shape), whole(shape)),
        flops=2 * tok * d * d,
        moved=4 * tok * d + 3 * d * d,
        vmem=20,
        name="merge_grad",
    )(info, *args)


def weight_kernel(na, nb, ga, gb, ha, dga, dua, hb, dgb, dub, out, nt):
    j = pl.program_id(0)
    tok, d = na.shape

    @pl.when(j == 0)
    def _():
        nt[:, :tok] = na[...].astype(f32).T.astype(bf16)
        nt[:, tok:] = nb[...].astype(f32).T.astype(bf16)

    for base, left, right in ((0, dga, dgb), (384, dua, dub)):
        grad = (dot(nt[:, :tok], left[...]) + dot(nt[:, tok:], right[...])).astype(bf16)
        for part in range(TILE // 128):
            at = pl.multiple_of(base + 48 * ((TILE // 128) * j + part), 16)
            out[:, pl.ds(at, 48), :] = grad[:, 128 * part : 128 * (part + 1)].reshape(FORM, 48, 128)
    grad = dot(ha[...].astype(f32).T.astype(bf16), ga[...]) + dot(hb[...].astype(f32).T.astype(bf16), gb[...])
    grad = grad.astype(bf16)
    for part in range(d // 128):
        low = 768 + 64 * part
        out[pl.ds(4 * j, 4), low : low + 64, :] = grad[:, 128 * part : 128 * (part + 1)].reshape(4, 64, 128)


def weight_grads(na, nb, ga, gb, left, right):
    tok, d = na.shape
    units = left[0].shape[1]
    args = (na, nb, ga, gb, *left, *right)
    col = pl.BlockSpec((tok, TILE), lambda j: (0, j))
    shape = (FORM, 1152, 128)
    return kernel_call(
        weight_kernel,
        struct(shape, bf16),
        grid=(units // TILE,),
        ins=[whole(x.shape) for x in args[:4]] + [col] * 6,
        out_specs=whole(shape),
        scratch=[pltpu.VMEM((d, 2 * tok), bf16)],
        flops=6 * 2 * tok * d * units,
        moved=12 * tok * units + 16 * tok * d,
        vmem=28,
        name="weight_grads",
    )(*args)


def regroup(stacked, parts, groups):
    count, _, width = stacked.shape
    if count == groups:
        return stacked
    pieces, low = [], 0
    for blocks, rows in parts:
        piece = stacked[:, low : low + blocks * rows].reshape(count, blocks, rows, width)
        low += blocks * rows
        piece = jnp.transpose(piece, (1, 0, 2, 3)).reshape(blocks, groups, count * rows // groups, width)
        pieces.append(jnp.transpose(piece, (1, 0, 2, 3)).reshape(groups, blocks * count * rows // groups, width))
    return jnp.concatenate(pieces, axis=1)


def to_blocks(mat, width):
    rows, cols = mat.shape
    return jnp.transpose(mat.reshape(rows, cols // width, width), (1, 0, 2)).reshape(-1, width)


def from_blocks(stacked, rows):
    blocks, width = stacked.shape[0] // rows, stacked.shape[1]
    return jnp.transpose(stacked.reshape(blocks, rows, width), (1, 0, 2)).reshape(rows, blocks * width)


def flip(x, bit):
    return lax.ppermute(x, ULY, [(i, i ^ bit) for i in range(4)])


def ordered(core, mine, theirs, axis):
    first = jnp.where(core == 0, mine, theirs)
    second = jnp.where(core == 0, theirs, mine)
    return jnp.concatenate([first, second], axis=axis)


def local(
    n_ctx,
    byte_embed,
    query_weight,
    key_weight,
    value_weight,
    merge_weight,
    gate_weight,
    up_weight,
    down_weight,
    conv_weight,
    score_weight,
    attn_gain,
    ffn_gain,
    bias_table,
    doc_lengths,
    rel_bucket,
    out_grad,
):
    nb, d = byte_embed.shape
    tok = out_grad.shape[0]
    n_dev = n_ctx * 4
    groups = n_ctx * 2
    rows_dev = query_weight.shape[0]
    rows_ctx = 4 * rows_dev
    down_dev = down_weight.shape[0]
    heads = HEADS // 4
    width = heads * HEAD_DIM
    group_len = tok * 4
    ext = 2 * group_len
    ff = gate_weight.shape[1]
    unit = ff // n_dev
    ctx_at = lax.axis_index("ctx")
    row_at = lax.axis_index("ux")
    core = lax.axis_index("uc")
    uly_at = lax.axis_index(ULY)
    dev_at = lax.axis_index(RING)
    me = uly_at.astype(jnp.int32).reshape(1)

    up_pairs = [(i, i + 1) for i in range(n_dev - 1)]
    down_pairs = [(i + 1, i) for i in range(n_dev - 1)]
    lo = lax.ppermute(byte_embed[nb - 8 :], RING, up_pairs)
    hi = lax.ppermute(byte_embed[:8], RING, down_pairs)

    count = doc_lengths.shape[0]
    order = lax.broadcasted_iota(jnp.int32, (count, count), 0)
    before = lax.broadcasted_iota(jnp.int32, (count, count), 1)
    starts = jnp.sum(jnp.where(before < order, doc_lengths[None, :], 0), axis=1)
    limit = jnp.sum(doc_lengths)

    shape = (nb + 16, 128)
    here = dev_at * nb - 8 + lax.broadcasted_iota(jnp.int32, shape, 0)
    there = here + lax.broadcasted_iota(jnp.int32, shape, 1) - 2
    between = jnp.sum(
        ((starts[None, None, :] <= here[:, :, None]) != (starts[None, None, :] <= there[:, :, None])).astype(jnp.int32),
        axis=2,
    )
    msk = ((between == 0) & (there >= 0) & (there < limit)).astype(f32)

    cw, sw = conv_weight, score_weight[None, :]
    gain_one, gain_two = attn_gain[None, :], ffn_gain[None, :]

    qkv_own = jnp.stack(
        [w.reshape(rows_dev, 4, width) for w in (query_weight, key_weight, value_weight)], axis=2
    ).reshape(rows_dev, 4, 3 * width)
    doubling = rows_ctx % 16 == 0
    take = lambda x, at, dim: lax.dynamic_index_in_dim(x, at, dim, keepdims=False)
    if doubling:
        cols = jnp.transpose(qkv_own, (1, 0, 2)).reshape(2, 2, rows_dev, 3 * width)
        got = flip(take(cols, 1 - core, 1), 1)
        cols = ordered(core, take(cols, core, 1), got, 1)
        got = flip(take(cols, 1 - row_at, 0), 2)
        qkv_w = ordered(row_at, take(cols, row_at, 0), got, 0)[None]
    else:
        qkv_send = jnp.broadcast_to(
            jnp.transpose(qkv_own, (1, 0, 2))[None], (n_ctx, 4, rows_dev, 3 * width)
        ).reshape(n_dev, rows_dev, 3 * width)
        qkv_w = lax.all_to_all(qkv_send, RING, 0, 0, tiled=True).reshape(8, d // 8, 3 * width)

    codes = [0]
    if doubling:
        bits_left = [1 << i for i in range(n_ctx.bit_length() - 1)][::-1]

        def double(qkv_w, bit):
            got = lax.ppermute(qkv_w, "ctx", [(i, i ^ bit) for i in range(n_ctx)])
            return jnp.concatenate([qkv_w, got], axis=0)

        qkv_w, lo, hi = lax.optimization_barrier((qkv_w, lo, hi))
        gbst, normed, conv, aw = gbst_forward(lo, byte_embed, hi, msk, cw, sw, gain_one)
        gate_in, up_in, merge_in = gate_weight, up_weight, merge_weight
        for i, bit in enumerate(bits_left):
            qkv_w = double(qkv_w, bit)
            codes = codes + [c ^ bit for c in codes]
            if i == 0:
                gate_in, up_in, merge_in, qkv_w, normed = lax.optimization_barrier(
                    (gate_in, up_in, merge_in, qkv_w, normed)
                )
        places = ctx_at ^ jnp.array(codes, jnp.int32)
    else:
        gbst, normed, conv, aw = gbst_forward(lo, byte_embed, hi, msk, cw, sw, gain_one)
        gate_in, up_in, merge_in = gate_weight, up_weight, merge_weight
        places = jnp.arange(8, dtype=jnp.int32)
    weight_info = jnp.concatenate([me, places.astype(jnp.int32)])
    chunk = jnp.concatenate([gate_in, up_in, merge_in], axis=1)
    chip = ordered(core, chunk, flip(chunk, 1), 0)

    def split(at):
        halves = [
            lax.dynamic_index_in_dim(
                chip[:, low : low + ff].reshape(2 * rows_dev, n_ctx, 2, 2 * unit), at, 2, keepdims=False
            ).reshape(2 * rows_dev, ff // 2)
            for low in (0, ff)
        ]
        return jnp.concatenate(halves + [chip[:, 2 * ff :]], axis=1)

    both = jnp.where(row_at == core, split(row_at), flip(split(1 - row_at), 2))
    packed_own = jnp.concatenate(
        [
            to_blocks(both[:, : ff // 2], TILE),
            to_blocks(both[:, ff // 2 : ff], TILE),
            to_blocks(down_weight, TILE),
            to_blocks(both[:, ff:], TILE),
        ],
        axis=0,
    )
    starts, limit, _ = lax.optimization_barrier((starts, limit, aw))

    tok_at = ctx_at * group_len - group_len // 2 + jnp.arange(ext, dtype=jnp.int32)
    tok_doc = jnp.sum((starts[None, :] <= 2 * tok_at[:, None]).astype(jnp.int32), axis=1) - 1
    tok_doc = jnp.where((tok_at >= 0) & (2 * tok_at < limit), tok_doc, -1)
    bits = count.bit_length()
    lane = jnp.arange(TILE, dtype=jnp.int32) - width

    def coded(docs, code, agree, value):
        bit_on = ((docs >> jnp.clip(code // 2, 0, 31)) & 1) == 1
        used = (code >= 0) & (code < 2 * bits)
        return jnp.where(used & ((bit_on == (code % 2 == 1)) == agree), value, 0.0).astype(bf16)

    code_k = coded(tok_doc[:, None], lane[None, :], True, 1.0)
    own_doc = tok_doc[group_len // 2 : group_len // 2 + group_len]
    code_q = coded(own_doc[:, None], lane[None, :], False, -BIG)
    tiles = group_len // TILE
    first = ctx_at * group_len + TILE * jnp.arange(tiles, dtype=jnp.int32)
    begin = jnp.max(jnp.where(starts[None, :] <= 2 * first[:, None], starts[None, :], 0), axis=1)
    last = 2 * (first + TILE - 1)
    end = jnp.min(jnp.where(starts[None, :] > last[:, None], starts[None, :], limit), axis=1)
    shift = group_len // 2 - ctx_at * group_len
    tile_lo = jnp.clip(((begin + 1) // 2 + shift) // TILE, 0, ext // TILE)
    tile_hi = jnp.clip(((end - 1) // 2 + shift) // TILE + 1, 0, ext // TILE)
    info = jnp.concatenate([tile_lo, tile_hi, me]).astype(jnp.int32)

    rel_count = rel_bucket.shape[0]
    diag_len = 2 * DOC_TOK + 2 * TILE
    bucket = jnp.pad(rel_bucket[::-1], (diag_len - TILE - rel_count, TILE), constant_values=-1)
    onehot = (bucket[None, :] == jnp.arange(NBUCK, dtype=jnp.int32)[:, None]).astype(f32)
    table_here = lax.dynamic_slice_in_dim(bias_table, uly_at * heads, heads, 1)
    diag = lax.dot_general(table_here, onehot, (((0,), (0,)), ((), ())), precision=highest)

    near = [(4 * c + u, 4 * (c + s) + u) for c in range(n_ctx) for u, s in ((0, -1), (1, -1), (2, 1), (3, 1)) if 0 <= c + s < n_ctx]
    far0 = lax.ppermute(normed, RING, near)
    own2 = flip(normed, 2)
    packed_own, qkv_w, far0, own2 = lax.optimization_barrier((packed_own, qkv_w, far0, own2))
    packed = lax.all_gather(packed_own, ("ctx", "uc"), axis=0, tiled=False)
    packed = packed.reshape(groups, packed_own.shape[0], TILE)
    packed = regroup(
        packed,
        ((4, 2 * rows_dev), (4, 2 * rows_dev), (3, down_dev), (3, 2 * rows_dev)),
        FORM,
    )


    own1 = flip(normed, 1)
    own3 = flip(own2, 1)
    far2 = flip(far0, 2)
    far1 = flip(far0, 1)
    far3 = flip(far2, 1)
    grad_in, far3 = lax.optimization_barrier((out_grad, far3))
    grad_other = flip(grad_in, 2)
    own = (normed, own1, own2, own3)
    far = (far0, far1, far2, far3)
    q, k, v, vt, wp = project(weight_info, own, far, qkv_w, code_q, code_k, heads)

    oa, ob, oloc, lse = attend(info, q, k, vt, diag, heads, tok)
    got2 = flip(ob, 2)
    got2, grad_other = lax.optimization_barrier((got2, grad_other))
    att = (oa[0], flip(oa[1], 1), got2[0], flip(got2[1], 1))
    mid, normed_two = merge(me, *att, packed, gbst, gain_two)

    normed_other = flip(normed_two, 2)
    out_a, dn_a, *left = feed(normed_two, out_grad, packed, ff // 2, f32)
    normed_other, dn_a = lax.optimization_barrier((normed_other, dn_a))
    out_b, dn_b, *right = feed(normed_other, grad_other, packed, ff // 2, bf16)
    dn_got = flip(dn_b, 2)
    grads = weight_grads(normed_two, normed_other, out_grad, grad_other, left, right)
    dn_got, grads = lax.optimization_barrier((dn_got, grads))
    parts16 = ((8, 48), (8, 48), (6, 64))
    grads = regroup(grads, parts16, groups)
    summed = lax.psum_scatter(grads, ("ctx", "uc"), scatter_dimension=0, tiled=False)
    dmid, dlow, ga, gb2, ffn_sum = middle(me, mid, dn_a, dn_got, out_grad, gain_two, packed)
    back2 = flip(gb2, 2)
    back1 = flip(ga[1], 1)
    back1, dlow = lax.optimization_barrier((back1, dlow))
    keep_m, send_m = merge_grad(me, *att, dlow)
    recv_m = flip(send_m, 1)
    back = (ga[0], back1, back2[0], flip(back2[1], 1))
    mid_m = (keep_m[1] + recv_m[1].astype(f32)).astype(bf16)

    out_b, mid_m, *back = lax.optimization_barrier((out_b, mid_m, *back))
    got_m = flip(mid_m, 2)
    out_got = flip(out_b, 2)
    dq, dk, dv, sums = attend_back(info, q, k, v, diag, oloc, lse, *back, heads)
    out_got, got_m, dk = lax.optimization_barrier((out_got, got_m, dk))
    layer_out = (mid + out_a + out_got.astype(f32)).astype(bf16)
    grad_info = jnp.concatenate([me, jnp.arange(8, dtype=jnp.int32)])
    hk0, hk2, hs1, hs3 = project_back(True, me, dq, dk, dv, wp)
    h_mid = (hk2 + flip(hs3, 1).astype(f32)).astype(bf16)
    h_mid, dq_g = lax.optimization_barrier((h_mid, dq))
    h_got2 = flip(h_mid, 2)
    part = project_grad(grad_info, own, far, dq_g, dk, dv, keep_m, recv_m, got_m, 8)
    dq_p, part, h_got2 = lax.optimization_barrier((dq_g, part, h_got2))
    ok0, ok2, os1, os3 = project_back(False, me, dq_p, dk, dv, wp)
    part = lax.psum_scatter(part.reshape(n_ctx, rows_ctx, 4 * width), "ctx", scatter_dimension=0, tiled=False)
    got = lax.all_to_all(part.reshape(4, rows_dev, 4 * width), ULY, 0, 0, tiled=True).astype(f32)
    h_got1 = flip(hs1, 1)
    o_got1 = flip(os1, 1)
    o_mid = (ok2 + flip(os3, 1).astype(f32)).astype(bf16)
    h_sum = (hk0 + h_got1.astype(f32) + h_got2.astype(f32)).astype(bf16)
    h_sum, o_mid = lax.optimization_barrier((h_sum, o_mid))
    h_back = lax.ppermute(h_sum, RING, [(b, a) for a, b in near])
    o_got2 = flip(o_mid, 2)
    o_sum = ok0 + o_got1.astype(f32) + o_got2.astype(f32)
    got = jnp.transpose(got.reshape(4, rows_dev, 4, width), (2, 1, 0, 3))
    query_grad, key_grad, value_grad, merge_g = (got[j].reshape(rows_dev, d) for j in range(4))

    sums, _ = lax.optimization_barrier((sums, h_sum))
    diag_parts = jnp.transpose(sums, (1, 0, 2))
    count_t = diag_parts.shape[1]
    low = diag_parts[:, :, :TILE].reshape(heads, count_t * TILE)
    high = diag_parts[:, :, TILE:].reshape(heads, count_t * TILE)
    diag_grad = jnp.pad(low, ((0, 0), (0, TILE))) + jnp.pad(high, ((0, 0), (TILE, 0)))
    table_local = lax.dot_general(onehot, diag_grad, (((1,), (1,)), ((), ())), precision=highest)
    table_grad = lax.dynamic_update_slice(jnp.zeros((NBUCK, HEADS), f32), table_local, (0, uly_at * heads))

    eg, small = gbst_backward(
        o_sum, h_back, gbst, dmid, gain_one, conv, aw, lo, byte_embed, hi, msk, cw, sw
    )
    from_prev = lax.ppermute(eg[nb + 8 :], RING, up_pairs)
    from_next = lax.ppermute(eg[:8], RING, down_pairs)
    main = eg[8 : nb + 8]
    embed_grad = jnp.concatenate(
        [main[:8] + from_prev, main[8 : nb - 8], main[nb - 8 :] + from_next], axis=0
    )

    rest = jnp.concatenate(
        [jnp.sum(ffn_sum, axis=0, keepdims=True), jnp.pad(table_grad.reshape(1, -1), ((0, 0), (0, d - NBUCK * HEADS)))],
        axis=0,
    )
    total = jnp.concatenate([small, jnp.pad(rest, ((0, 6), (0, 0)))], axis=0)
    for bit in (1, 2):
        total = total + flip(total, bit)
    bit = 1
    while bit < n_ctx:
        total = total + lax.ppermute(total, "ctx", [(i, i ^ bit) for i in range(n_ctx)])
        bit *= 2

    rows2 = 2 * rows_dev
    down_grad = from_blocks(summed[16 * rows2 :], down_dev).astype(f32)
    mine = jnp.concatenate(
        [from_blocks(summed[: 8 * rows2], rows2), from_blocks(summed[8 * rows2 : 16 * rows2], rows2)], axis=1
    )
    theirs = flip(mine, 2)
    sets = [jnp.where(row_at == at, mine, theirs).reshape(rows2, 2, n_ctx, 1, 2 * unit) for at in (0, 1)]
    full = jnp.concatenate(sets, axis=3).reshape(2, rows_dev, 2 * ff)
    given = flip(lax.dynamic_index_in_dim(full, 1 - core, 0, keepdims=False), 1)
    kept = lax.dynamic_index_in_dim(full, core, 0, keepdims=False)
    final = jnp.where(row_at == core, kept, given).astype(f32)
    return (
        layer_out,
        embed_grad,
        query_grad,
        key_grad,
        value_grad,
        merge_g,
        final[:, :ff],
        final[:, ff:],
        down_grad,
        total[:CONV],
        total[5],
        total[6],
        total[8],
        total[9, : NBUCK * HEADS].reshape(NBUCK, HEADS),
    )


def solution(mesh):
    n_ctx = mesh.shape["ctx"]
    inner = Mesh(mesh.devices.reshape(n_ctx, 2, 2), RING)
    row = P(RING, None)
    return jax.shard_map(
        partial(local, n_ctx),
        mesh=inner,
        in_specs=(row,) * 8 + (P(),) * 7 + (row,),
        out_specs=(row,) * 9 + (P(),) * 5,
        check_vma=False,
    )
```

```python
from functools import partial

import jax
import jax.numpy as jnp
from jax import lax
from jax.experimental import pallas as pl
from jax.experimental.pallas import tpu as pltpu
from jax.sharding import Mesh, PartitionSpec as P

HEADS = 12
HEAD_DIM = 64
NBUCK = 32
CONV = 5
DOC_TOK = 1024
TILE = 256
FORM = 16
PHASES = 12
EPS = 1e-06
BIG = 1e30
GELU_C = 0.7978845608028654
GELU_A = 0.044715

bf16 = jnp.bfloat16
f32 = jnp.float32
RING = ("ctx", "ux", "uc")
ULY = ("ux", "uc")
highest = lax.Precision.HIGHEST


def dot(left, right, dims=((1,), (0,))):
    return lax.dot_general(left, right, (dims, ((), ())), preferred_element_type=f32)


def kernel_call(body, outs, *, grid=(1,), ins, scratch=(), prefetch=0, out_specs=None, flops=0, moved=0, vmem=40, name=None):
    params = pltpu.CompilerParams(
        dimension_semantics=("arbitrary",) * len(grid), vmem_limit_bytes=vmem << 20
    )
    return pl.pallas_call(
        body,
        out_shape=outs,
        grid_spec=pltpu.PrefetchScalarGridSpec(
            num_scalar_prefetch=prefetch,
            grid=grid,
            in_specs=ins,
            out_specs=out_specs,
            scratch_shapes=list(scratch),
        ),
        compiler_params=params,
        cost_estimate=pl.CostEstimate(flops=int(flops) // 8, bytes_accessed=int(moved) // 8, transcendentals=0),
        name=name,
    )


def whole(shape, once=True):
    zeros = (0,) * len(shape)
    if once:
        return pl.BlockSpec(shape, lambda *a: zeros, pipeline_mode=pl.Buffered(1))
    return pl.BlockSpec(shape, lambda *a: zeros)


def in_hbm(*arrays):
    return tuple(pltpu.with_memory_space_constraint(x, pltpu.HBM) for x in arrays)


def struct(shape, dtype):
    return jax.ShapeDtypeStruct(shape, dtype)


def block_of(size, at):
    first = size * (at // size)
    return range(first, first + size)


def token_pairs(tok):
    found = set()
    for byte in (2 * tok, 2 * tok + 1):
        for size in range(1, 5):
            found |= set(block_of(size, byte))
    return sorted(found)


def mix_coefs(weights):
    coefs = {}
    for tok in range(PHASES // 2):
        for at in token_pairs(tok):
            total = None
            for byte in (2 * tok, 2 * tok + 1):
                for size in range(1, 5):
                    if at in block_of(size, byte):
                        term = weights[size - 1][byte] * (0.5 / size)
                        total = term if total is None else total + term
            coefs[tok, at] = total
    return coefs


def lane_chunks(feats):
    return [slice(128 * c, 128 * (c + 1)) for c in range(feats // 128)]


def fill_bytes(pad, lo, emb, hi):
    byte_count, feats = emb.shape
    chunks = lane_chunks(feats)
    for c, cols in enumerate(chunks):
        pad[c, 0:8, :] = lo[:, cols].astype(f32)
        pad[c, 8 + byte_count : 16 + byte_count, :] = hi[:, cols].astype(f32)

    def fill(t, _):
        at = pl.multiple_of(t * 32, 32)
        for c, cols in enumerate(chunks):
            pad[c, pl.ds(at + 8, 32), :] = emb[pl.ds(at, 32), cols].astype(f32)
        return 0

    lax.fori_loop(0, byte_count // 32, fill, 0)


def gbst_forward_kernel(lo, emb, hi, msk, cw, sw, gain, gb, nrm, conv, aw, pad, mix):
    byte_count, feats = emb.shape
    chunks = lane_chunks(feats)
    fill_bytes(pad, lo, emb, hi)
    lanes = lax.broadcasted_iota(jnp.int32, (8, 128), 1)

    def step(g, _):
        base = g * 8 * PHASES + 8
        rows = pl.ds(pl.multiple_of(8 * g, 8), 8)
        first = []
        for p in range(PHASES):
            mask = msk[pl.ds(base + p, 8, stride=PHASES), :]
            same = {k: jnp.broadcast_to(mask[:, k : k + 1], (8, 128)) for k in (0, 1, 3, 4)}
            dots = None
            for c, cols in enumerate(chunks):
                x = pad[c, pl.ds(base + p, 8, stride=PHASES), :] * cw[2:3, cols]
                for k in (0, 1, 3, 4):
                    x = x + pad[c, pl.ds(base + p + k - 2, 8, stride=PHASES), :] * same[k] * cw[k : k + 1, cols]
                conv[p, rows, cols] = x
                term = x * sw[:, cols]
                dots = term if dots is None else dots + term
            first.append(jnp.broadcast_to(jnp.sum(dots, axis=1, keepdims=True), (8, 128)))
        weights = [[None] * PHASES for _ in range(4)]
        packed = jnp.zeros((8, 128), f32)
        for p in range(PHASES):
            scores = []
            for size in range(1, 5):
                total = None
                for at in block_of(size, p):
                    total = first[at] if total is None else total + first[at]
                scores.append(total * (1.0 / size))
            top = jnp.maximum(jnp.maximum(scores[0], scores[1]), jnp.maximum(scores[2], scores[3]))
            exps = [jnp.exp(s - top) for s in scores]
            inv = 1.0 / (exps[0] + exps[1] + exps[2] + exps[3])
            for size in range(4):
                weights[size][p] = exps[size] * inv
                packed = jnp.where(lanes == 4 * p + size, weights[size][p], packed)
        aw[rows, :] = packed
        coefs = mix_coefs(weights)
        for tok in range(PHASES // 2):
            for c, cols in enumerate(chunks):
                out = None
                for at in token_pairs(tok):
                    term = coefs[tok, at] * conv[at, rows, cols]
                    out = term if out is None else out + term
                mix[c, pl.ds(g * 4 * PHASES + tok, 8, stride=PHASES // 2), :] = out
        return 0

    lax.fori_loop(0, byte_count // (8 * PHASES), step, 0)

    def norm(t, _):
        at = pl.multiple_of(t * 16, 16)
        v = jnp.concatenate([mix[c, pl.ds(at, 16), :] for c in range(len(chunks))], axis=1)
        r = lax.rsqrt(jnp.mean(v * v, axis=1, keepdims=True) + EPS)
        gb[pl.ds(at, 16), :] = v
        nrm[pl.ds(at, 16), :] = (v * r * gain[...]).astype(bf16)
        return 0

    lax.fori_loop(0, byte_count // 32, norm, 0)


def gbst_forward(lo, emb, hi, msk, cw, sw, gain):
    nb, d = emb.shape
    return kernel_call(
        gbst_forward_kernel,
        (
            struct((nb // 2, d), f32),
            struct((nb // 2, d), bf16),
            struct((PHASES, nb // PHASES, d), f32),
            struct((nb // PHASES, 128), f32),
        ),
        ins=[whole(x.shape) for x in (lo, emb, hi, msk, cw, sw, gain)],
        out_specs=(
            whole((nb // 2, d)),
            whole((nb // 2, d)),
            whole((PHASES, nb // PHASES, d)),
            whole((nb // PHASES, 128)),
        ),
        scratch=[pltpu.VMEM((d // 128, nb + 16, 128), f32), pltpu.VMEM((d // 128, nb // 2, 128), f32)],
        flops=60 * nb * d,
        moved=20 * nb * d,
        vmem=20,
        name="gbst_forward",
    )(lo, emb, hi, msk, cw, sw, gain)


def gbst_backward_kernel(keep, recv, gb, dmid, gain, conv, aw, lo, emb, hi, msk, cw, sw, eg, small, dtok, dconv, pad, acc):
    byte_count, feats = emb.shape
    chunks = lane_chunks(feats)
    acc[...] = jnp.zeros_like(acc)
    fill_bytes(pad, lo, emb, hi)
    for c in range(len(chunks)):
        dconv[c, 0:16, :] = jnp.zeros((16, 128), f32)
        dconv[c, 16 + byte_count : 32 + byte_count, :] = jnp.zeros((16, 128), f32)

    def norm(t, _):
        at = pl.multiple_of(t * 16, 16)
        e = keep[pl.ds(at, 16), :] + recv[pl.ds(at, 16), :].astype(f32)
        v = gb[pl.ds(at, 16), :]
        r = lax.rsqrt(jnp.mean(v * v, axis=1, keepdims=True) + EPS)
        ge = gain[...] * e
        m = jnp.mean(ge * v, axis=1, keepdims=True)
        out = dmid[pl.ds(at, 16), :] + r * ge - v * (r * r * r * m)
        for c, cols in enumerate(chunks):
            dtok[c, pl.ds(at, 16), :] = out[:, cols]
        part = e * v * r
        acc[48:56, :] = acc[48:56, :] + part[0:8] + part[8:16]
        return 0

    lax.fori_loop(0, byte_count // 32, norm, 0)

    def step(g, _):
        rows = pl.ds(pl.multiple_of(8 * g, 8), 8)
        half = PHASES // 2

        def tok_rows(tok, c):
            return dtok[c, pl.ds(g * 8 * half + tok, 8, stride=half), :]

        inner = {}
        for tok in range(half):
            toks = [tok_rows(tok, c) for c in range(len(chunks))]
            for at in token_pairs(tok):
                dots = None
                for c, cols in enumerate(chunks):
                    term = toks[c] * conv[at, rows, cols]
                    dots = term if dots is None else dots + term
                inner[tok, at] = jnp.broadcast_to(jnp.sum(dots, axis=1, keepdims=True), (8, 128))
        tile = aw[rows, :]
        weights = [
            [jnp.broadcast_to(tile[:, 4 * p + size : 4 * p + size + 1], (8, 128)) for p in range(PHASES)]
            for size in range(4)
        ]
        coefs = mix_coefs(weights)
        dsize = [[None] * PHASES for _ in range(4)]
        for p in range(PHASES):
            cs = []
            for size in range(1, 5):
                total = None
                for at in block_of(size, p):
                    total = inner[p // 2, at] if total is None else total + inner[p // 2, at]
                cs.append(total * (0.5 / size))
            mean = sum(weights[s][p] * cs[s] for s in range(4))
            for s in range(4):
                dsize[s][p] = weights[s][p] * (cs[s] - mean)
        slopes = []
        for at in range(PHASES):
            e = None
            for size in range(1, 5):
                for p in block_of(size, at):
                    term = dsize[size - 1][p] * (1.0 / size)
                    e = term if e is None else e + term
            slopes.append(e)
        for c, cols in enumerate(chunks):
            toks = [tok_rows(tok, c) for tok in range(half)]
            score = acc[40:48, cols]
            for at in range(PHASES):
                out = slopes[at] * sw[:, cols]
                for tok in range(half):
                    if (tok, at) in coefs:
                        out = out + coefs[tok, at] * toks[tok]
                dconv[c, pl.ds(g * 8 * PHASES + 16 + at, 8, stride=PHASES), :] = out
                score = score + slopes[at] * conv[at, rows, cols]
            acc[40:48, cols] = score
        return 0

    lax.fori_loop(0, byte_count // (8 * PHASES), step, 0)

    def taps(t, _):
        masks = []
        for u in range(2):
            mask = msk[pl.ds(pl.multiple_of(t * 16 + 8 * u, 8), 8), :]
            masks.append({k: jnp.broadcast_to(mask[:, 4 - k : 5 - k], (8, 128)) for k in (0, 1, 3, 4)})
        for c, cols in enumerate(chunks):
            sums = [None] * CONV
            for u in range(2):
                at = pl.multiple_of(t * 16 + 8 * u, 8)
                x = pad[c, pl.ds(at, 8), :]
                out = None
                for k in range(CONV):
                    z = dconv[c, pl.ds(at + 8 + 2 - k, 8), :]
                    if k != 2:
                        z = z * masks[u][k]
                    term = z * cw[k : k + 1, cols]
                    out = term if out is None else out + term
                    sums[k] = z * x if sums[k] is None else sums[k] + z * x
                eg[pl.ds(at, 8), cols] = out
            for k in range(CONV):
                acc[8 * k : 8 * k + 8, cols] = acc[8 * k : 8 * k + 8, cols] + sums[k]
        return 0

    lax.fori_loop(0, (byte_count + 16) // 16, taps, 0)
    small[...] = jnp.zeros_like(small)
    for k in range(7):
        small[k : k + 1, :] = jnp.sum(acc[8 * k : 8 * k + 8, :], axis=0, keepdims=True)


def gbst_backward(keep, recv, gb, dmid, gain, conv, aw, lo, emb, hi, msk, cw, sw):
    nb, d = emb.shape
    args = (keep, recv, *in_hbm(gb, dmid, gain, conv, aw, lo, emb, hi, msk, cw, sw))
    return kernel_call(
        gbst_backward_kernel,
        (struct((nb + 16, d), f32), struct((8, d), f32)),
        ins=[whole(x.shape) for x in args],
        out_specs=(whole((nb + 16, d)), whole((8, d))),
        scratch=[
            pltpu.VMEM((d // 128, nb // 2, 128), f32),
            pltpu.VMEM((d // 128, nb + 32, 128), f32),
            pltpu.VMEM((d // 128, nb + 16, 128), f32),
            pltpu.VMEM((56, d), f32),
        ],
        flops=120 * nb * d,
        moved=24 * nb * d,
        vmem=28,
        name="gbst_backward",
    )(*args)


def halo_row(who, tok_dev, ext):
    return jnp.where(who >= 2, (who - 2) * tok_dev, ext - 2 * tok_dev + who * tok_dev)


def project_kernel(n_heads, info, *refs):
    own, far, w, cq, ck, (q, k, v, vt, wp) = refs[:4], refs[4:8], refs[8], refs[9], refs[10], refs[11:16]
    tok, _ = own[0].shape
    me = info[0]
    part = w.shape[2] // 3
    rows = w.shape[1]
    wp[...] = jnp.zeros_like(wp)
    for b in range(w.shape[0]):
        at = pl.ds(pl.multiple_of(info[1 + b] * rows, 16), rows)
        block = w[b]
        for j in range(3):
            wp[at, TILE * j : TILE * j + part] = block[:, part * j : part * (j + 1)]
    ext = k.shape[0]
    left = (ext - q.shape[0]) // 2
    for rel in range(4):
        who = me ^ rel
        out = dot(own[rel][...], wp[...])
        at = pl.ds(pl.multiple_of(who * tok, 128), tok)
        q[at, :] = out[:, :TILE].astype(bf16) + cq[at, :]
        edge = dot(far[rel][...], wp[:, TILE:])
        for at, ks, vs in (
            (left + who * tok, out[:, TILE : 2 * TILE], out[:, 2 * TILE :]),
            (halo_row(who, tok, ext), edge[:, :TILE], edge[:, TILE:]),
        ):
            at = pl.ds(pl.multiple_of(at, 128), tok)
            k[at, :] = ks.astype(bf16) + ck[at, :]
            v[at, :] = vs.astype(bf16)
            vt[:, at] = vs.T.astype(bf16)


def project(info, own, far, w, cq, ck, n_heads):
    tok, d = own[0].shape
    rows, ext = 4 * tok, 8 * tok
    args = (*own, *far, w, cq, ck)
    shapes = [(rows, TILE), (ext, TILE), (ext, TILE), (TILE, ext), (d, 3 * TILE)]
    return kernel_call(
        partial(project_kernel, n_heads),
        tuple(struct(x, bf16) for x in shapes),
        prefetch=1,
        ins=[whole(x.shape) for x in args],
        out_specs=tuple(whole(x) for x in shapes),
        flops=2 * ext * d * 3 * TILE,
        moved=2 * (ext * d + 2 * ext * TILE + d * d),
        vmem=30,
        name="project",
    )(info, *args)


def project_back_kernel(is_halo, me, dq, dk, dv, wp, keep0, keep2, send1, send3):
    tok = keep0.shape[0]
    ext = dk.shape[0]
    left = (ext - dq.shape[0]) // 2
    for rel, ref in ((3, send3), (1, send1), (2, keep2), (0, keep0)):
        who = me[0] ^ rel
        if is_halo:
            at = pl.multiple_of(halo_row(who, tok, ext), 128)
            out = dot(dk[pl.ds(at, tok), :], wp[:, TILE : 2 * TILE], ((1,), (1,)))
        else:
            at = pl.multiple_of(left + who * tok, 128)
            out = dot(dk[pl.ds(at, tok), :], wp[:, TILE : 2 * TILE], ((1,), (1,)))
            mine = pl.multiple_of(who * tok, 128)
            out = out + dot(dq[pl.ds(mine, tok), :], wp[:, :TILE], ((1,), (1,)))
        out = out + dot(dv[pl.ds(at, tok), :], wp[:, 2 * TILE :], ((1,), (1,)))
        ref[...] = out.astype(ref.dtype)


def project_back(is_halo, me, dq, dk, dv, wp):
    ext, d = dk.shape[0], wp.shape[0]
    tok = ext // 8
    args = (dq, dk, dv, wp)
    kinds = (f32, f32, bf16, bf16)
    return kernel_call(
        partial(project_back_kernel, is_halo),
        tuple(struct((tok, d), kind) for kind in kinds),
        prefetch=1,
        ins=[whole(x.shape) for x in args],
        out_specs=tuple(whole((tok, d)) for _ in kinds),
        flops=2 * ext // 2 * d * 3 * TILE,
        moved=4 * ext * d,
        vmem=20,
        name="project_back",
    )(me, *args)


def project_grad_kernel(info, *refs):
    own, far, (dq, dk, dv, mkeep, mrecv, mgot), out, flat = refs[:4], refs[4:8], refs[8:14], refs[14], refs[15]
    tok = own[0].shape[0]
    ext = dk.shape[0]
    me = info[0]
    left = (ext - dq.shape[0]) // 2
    part = mgot.shape[1]
    totals = [None] * 3

    def turned(ref, at):
        return ref[pl.ds(pl.multiple_of(at, 128), tok), :].astype(f32).T[:part].astype(bf16)

    for rel in range(4):
        who = me ^ rel
        at = left + who * tok
        edge = halo_row(who, tok, ext)
        terms = [
            dot(turned(dq, who * tok), own[rel][...]),
            dot(turned(dk, at), own[rel][...]) + dot(turned(dk, edge), far[rel][...]),
            dot(turned(dv, at), own[rel][...]) + dot(turned(dv, edge), far[rel][...]),
        ]
        totals = [t if x is None else x + t for x, t in zip(totals, terms)]
    for j in range(3):
        flat[:, part * j : part * (j + 1)] = totals[j].T.astype(bf16)
    merged = mkeep[0] + mrecv[0].astype(f32) + mgot[...].astype(f32)
    flat[:, 3 * part :] = merged.astype(bf16)
    rows = out.shape[1]
    for b in range(out.shape[0]):
        out[b] = flat[pl.ds(pl.multiple_of(info[1 + b] * rows, 16), rows), :]


def project_grad(info, own, far, dq, dk, dv, mkeep, mrecv, mgot, blocks):
    tok, d = own[0].shape
    args = (*in_hbm(*own, *far), dq, dk, dv, *in_hbm(mkeep, mrecv, mgot))
    shape = (blocks, d // blocks, 4 * mgot.shape[1])
    return kernel_call(
        project_grad_kernel,
        struct(shape, bf16),
        prefetch=1,
        ins=[whole(x.shape) for x in args],
        out_specs=whole(shape),
        scratch=[pltpu.VMEM((d, shape[2]), bf16)],
        flops=2 * 8 * tok * d * 3 * mgot.shape[1],
        moved=2 * 12 * tok * d,
        vmem=28,
        name="project_grad",
    )(info, *args)


def spread_kernel(got, *outs):
    width = got.shape[2] // 4
    for j, out in enumerate(outs):
        for u in range(4):
            out[:, width * u : width * (u + 1)] = got[u, :, width * j : width * (j + 1)].astype(f32)


def spread(got):
    _, rows, d = got.shape
    return kernel_call(
        spread_kernel,
        (struct((rows, d), f32),) * 4,
        ins=[whole(got.shape)],
        out_specs=(whole((rows, d)),) * 4,
        flops=8 * 10**11,
        moved=24 * rows * d,
        vmem=8,
        name="spread",
    )(got)


def fill_bias(diag, bias):
    count = bias.shape[0]
    heads = diag.shape[0]

    def tile(t, _):
        seg = diag[:, pl.ds(pl.multiple_of((count - 1 - t) * TILE, TILE), 2 * TILE)]
        for h in range(heads):
            rows = jnp.broadcast_to(seg[h : h + 1, :], (TILE, 2 * TILE))
            turned = pltpu.roll(rows, TILE, axis=1, stride=1, stride_axis=0)
            bias[t, :, TILE * h : TILE * (h + 1)] = turned[:, :TILE]
        return 0

    lax.fori_loop(0, count, tile, 0)


def sum_diagonals(tiles, out):
    count, heads, _, _ = out.shape

    def tile(t, _):
        for h in range(heads):
            part = tiles[t, :, TILE * h : TILE * (h + 1)]
            cur = jnp.concatenate([part, jnp.zeros_like(part)], axis=1)
            rows = TILE
            while rows > 8:
                rows //= 2
                cur = cur[:rows] + pltpu.roll(cur[rows:], 2 * TILE - rows, axis=1)
            out[count - 1 - t, h] = cur
        return 0

    lax.fori_loop(0, count, tile, 0)


def lane_head(shape):
    return lax.broadcasted_iota(jnp.int32, shape, 1) // HEAD_DIM


def fill_queries(heads, q, q3):
    turned = q[...].astype(f32).T
    row = lax.broadcasted_iota(jnp.int32, (TILE, TILE), 0) // HEAD_DIM
    for h in range(heads):
        q3[:, TILE * h : TILE * (h + 1)] = jnp.where((row == h) | (row >= heads), turned, 0.0).astype(bf16)


def attend_kernel(heads, info, q, k, vt, diag, oa, ob, oloc, lse, bias, q3, sc, ac):
    i = pl.program_id(0)
    grid = pl.num_programs(0)
    me = info[2 * grid]
    ext = k.shape[0]
    wide = heads * TILE

    @pl.when(i == 0)
    def _():
        fill_bias(diag, bias)

    lo, hi = info[i], info[grid + i]
    away = (ext // TILE - grid) // 2
    fill_queries(heads, q, q3)
    ac[...] = jnp.zeros_like(ac)

    def scores(kt, top):
        at = pl.multiple_of(kt * TILE, TILE)
        s = dot(k[pl.ds(at, TILE), :], q3[...]) + bias[kt - i - away + 4]
        sc[kt - lo] = s
        return jnp.maximum(top, jnp.max(s.reshape(TILE // 8, 8, wide), axis=0))

    top = lax.fori_loop(lo, hi, scores, jnp.full((8, wide), -jnp.inf, f32))
    top = jnp.max(top, axis=0, keepdims=True)

    def gather(kt, total):
        at = pl.multiple_of(kt * TILE, TILE)
        p = jnp.exp(sc[kt - lo] - top)
        low = p.astype(bf16)
        for h in range(heads):
            cols = slice(TILE * h, TILE * (h + 1))
            head = slice(HEAD_DIM * h, HEAD_DIM * (h + 1))
            ac[head, :] = ac[head, :] + dot(vt[head, pl.ds(at, TILE)], low[:, cols])
        return total + jnp.sum(p.reshape(TILE // 8, 8, wide), axis=0)

    total = lax.fori_loop(lo, hi, gather, jnp.zeros((8, wide), f32))
    total = jnp.sum(total, axis=0, keepdims=True)
    inv = 1.0 / total
    lse[0] = jnp.broadcast_to(top + jnp.log(total), (8, wide))
    parts = []
    for h in range(heads):
        parts.append(ac[HEAD_DIM * h : HEAD_DIM * (h + 1), :] * inv[:, TILE * h : TILE * (h + 1)])
    turned = jnp.concatenate(parts, axis=0).astype(bf16)
    oloc[...] = turned
    per = oa.shape[1]
    for j in range(TILE // 128):
        chunk = i * (TILE // 128) + j
        rel = (chunk // per) ^ me
        piece = turned[:, 128 * j : 128 * (j + 1)]

        @pl.when(rel < 2)
        def _():
            oa[rel, chunk % per] = piece

        @pl.when(rel >= 2)
        def _():
            ob[rel - 2, chunk % per] = piece


def attend(info, q, k, vt, diag, heads, tok):
    rows, ext = q.shape[0], k.shape[0]
    grid = rows // TILE
    width = heads * HEAD_DIM
    sent = (2, tok // 128, width, 128)
    tile = pl.BlockSpec((TILE, TILE), lambda i, *_: (i, 0))
    return kernel_call(
        partial(attend_kernel, heads),
        (
            struct(sent, bf16),
            struct(sent, bf16),
            struct((width, rows), bf16),
            struct((grid, 8, heads * TILE), f32),
        ),
        grid=(grid,),
        prefetch=1,
        ins=[tile, whole(k.shape), whole(vt.shape), whole(diag.shape)],
        out_specs=(
            whole(sent),
            whole(sent),
            pl.BlockSpec((width, TILE), lambda i, *_: (0, i)),
            pl.BlockSpec((1, 8, heads * TILE), lambda i, *_: (i, 0, 0)),
        ),
        scratch=[
            pltpu.VMEM((9, TILE, heads * TILE), f32),
            pltpu.VMEM((TILE, heads * TILE), bf16),
            pltpu.VMEM((9, TILE, heads * TILE), f32),
            pltpu.VMEM((width, TILE), f32),
        ],
        flops=4 * rows * 1280 * TILE * heads,
        moved=8 * ext * TILE,
        vmem=30,
        name="attend",
    )(info, q, k, vt, diag)


def attend_back_kernel(
    heads, info, q, k, v, diag, oloc, lse, d0, d1, d2, d3,
    dq, dk, dv, sums,
    bias, tacc, kt_all, q3, g3, q3n, g3n, gall, dqa, dka, dva,
):
    i = pl.program_id(0)
    grid = pl.num_programs(0)
    me = info[2 * grid]
    ext = k.shape[0]
    per = d0.shape[0]
    width = heads * HEAD_DIM

    @pl.when(i == 0)
    def _():
        fill_bias(diag, bias)

        def turn(t, _):
            at = pl.ds(pl.multiple_of(t * TILE, TILE), TILE)
            kt_all[:, at] = k[at, :].astype(f32).T[:width].astype(bf16)
            return 0

        lax.fori_loop(0, ext // TILE, turn, 0)
        dka[...] = jnp.zeros_like(dka)
        dva[...] = jnp.zeros_like(dva)
        tacc[...] = jnp.zeros_like(tacc)
        for rel, piece in ((0, d0[...]), (2, d2[...]), (1, d1[...]), (3, d3[...])):
            gall[pl.ds((me ^ rel) * per, per)] = piece

    lo, hi = info[i], info[grid + i]
    away = (ext // TILE - grid) // 2
    where = lane_head((TILE, TILE))
    fill = jnp.zeros((TILE - width, TILE), f32)
    pieces = [gall[i * (TILE // 128) + j] for j in range(TILE // 128)]
    gt = jnp.concatenate(pieces, axis=1).astype(f32)
    grad = jnp.concatenate([gt, fill], axis=0).T
    prod = gt * oloc[...].astype(f32)
    deltas = []
    fill_queries(heads, q, q3)
    g3[...] = jnp.zeros_like(g3)
    for h in range(heads):
        rows = slice(TILE * h, TILE * (h + 1))
        head = slice(HEAD_DIM * h, HEAD_DIM * (h + 1))
        g3[head, rows] = gt[head, :].astype(bf16)
        q3n[rows, :] = jnp.where(where == h, q[...], jnp.zeros_like(q[...]))
        g3n[rows, :] = jnp.where(where == h, grad, 0.0).astype(bf16)
        deltas.append(jnp.sum(prod[HEAD_DIM * h : HEAD_DIM * (h + 1), :], axis=0, keepdims=True))
    delta = jnp.concatenate(deltas, axis=1)
    log = lse[0, 0:1, :]
    dqa[...] = jnp.zeros_like(dqa)

    def step(kt, _):
        at = pl.ds(pl.multiple_of(kt * TILE, TILE), TILE)
        rel = kt - i - away + 4
        s = dot(k[at, :], q3[...]) + bias[rel]
        p = jnp.exp(s - log)
        dp = dot(v[at, :], g3[...])
        ds = p * (dp - delta)
        tacc[rel] = tacc[rel] + ds
        low = ds.astype(bf16)
        dva[at, :] = dva[at, :] + dot(p.astype(bf16), g3n[...])
        dka[at, :] = dka[at, :] + dot(low, q3n[...])
        for h in range(heads):
            head = slice(HEAD_DIM * h, HEAD_DIM * (h + 1))
            dqa[head, :] = dqa[head, :] + dot(kt_all[head, at], low[:, TILE * h : TILE * (h + 1)])
        return 0

    lax.fori_loop(lo, hi, step, 0)
    dq[...] = jnp.concatenate([dqa[...], fill], axis=0).T.astype(bf16)

    @pl.when(i == grid - 1)
    def _():
        dk[...] = dka[...].astype(bf16)
        dv[...] = dva[...].astype(bf16)
        sum_diagonals(tacc, sums)


def attend_back(info, q, k, v, diag, oloc, lse, d0, d1, d2, d3, heads):
    rows, ext = q.shape[0], k.shape[0]
    grid = rows // TILE
    width = heads * HEAD_DIM
    tile = pl.BlockSpec((TILE, TILE), lambda i, *_: (i, 0))
    turned = pl.BlockSpec((width, TILE), lambda i, *_: (0, i))
    sums = (9, heads, 8, 2 * TILE)
    return kernel_call(
        partial(attend_back_kernel, heads),
        (
            struct((rows, TILE), bf16),
            struct((ext, TILE), bf16),
            struct((ext, TILE), bf16),
            struct(sums, f32),
        ),
        grid=(grid,),
        prefetch=1,
        ins=[
            tile, whole(k.shape), whole(v.shape), whole(diag.shape),
            turned, pl.BlockSpec((1, 8, heads * TILE), lambda i, *_: (i, 0, 0)),
            whole(d0.shape), whole(d1.shape), whole(d2.shape), whole(d3.shape),
        ],
        out_specs=(tile, whole((ext, TILE)), whole((ext, TILE)), whole(sums)),
        scratch=[
            pltpu.VMEM((9, TILE, heads * TILE), f32),
            pltpu.VMEM((9, TILE, heads * TILE), f32),
            pltpu.VMEM((width, ext), bf16),
            pltpu.VMEM((TILE, heads * TILE), bf16),
            pltpu.VMEM((TILE, heads * TILE), bf16),
            pltpu.VMEM((heads * TILE, TILE), bf16),
            pltpu.VMEM((heads * TILE, TILE), bf16),
            pltpu.VMEM((rows // 128, width, 128), bf16),
            pltpu.VMEM((width, TILE), f32),
            pltpu.VMEM((ext, TILE), f32),
            pltpu.VMEM((ext, TILE), f32),
        ],
        flops=10 * rows * 1280 * TILE * heads,
        moved=16 * ext * TILE,
        vmem=44,
        name="attend_back",
    )(info, *in_hbm(q, k, v, diag, oloc, lse), d0, d1, d2, d3)


MERGE_ROWS = pl.BlockSpec((FORM, 144, TILE), lambda *a: (0, 4, 0), pipeline_mode=pl.Buffered(1))


def merge_rows(packed, src, part):
    span = FORM // 4
    low = 48 * part
    return packed[pl.ds(src * span, span), low : low + 48, :].reshape(48 * span, TILE)


def merge_kernel(info, a0, a1, a2, a3, packed, gb, gain, mid, nrm):
    per = a0.shape[0]
    for t in range(per):
        rows = slice(128 * t, 128 * (t + 1))
        total = [gb[rows, TILE * part : TILE * (part + 1)] for part in range(3)]
        for rel, piece in ((0, a0[t]), (2, a2[t]), (1, a1[t]), (3, a3[t])):
            flat = piece.astype(f32).T.astype(bf16)
            for part in range(3):
                total[part] = total[part] + dot(flat, merge_rows(packed, info[0] ^ rel, part))
        v = jnp.concatenate(total, axis=1)
        mid[rows, :] = v
        r = lax.rsqrt(jnp.mean(v * v, axis=1, keepdims=True) + EPS)
        nrm[rows, :] = (v * r * gain[...]).astype(bf16)


def merge(me, a0, a1, a2, a3, packed, gb, gain):
    tok, d = gb.shape
    args = (a0, a1, a2, a3, packed, gb, gain)
    specs = [MERGE_ROWS if x is packed else whole(x.shape) for x in args]
    args = in_hbm(*args)
    return kernel_call(
        merge_kernel,
        (struct((tok, d), f32), struct((tok, d), bf16)),
        prefetch=1,
        ins=specs,
        out_specs=(whole((tok, d)), whole((tok, d))),
        flops=2 * tok * d * d,
        moved=12 * tok * d,
        vmem=20,
        name="merge",
    )(me, *args)


def feed_kernel(nt, gr, wg, wu, wd, out, dn, hid, dg, du, osum, dsum):
    j = pl.program_id(0)

    @pl.when(j == 0)
    def _():
        osum[...] = jnp.zeros_like(osum)
        dsum[...] = jnp.zeros_like(dsum)

    wgt = wg[...].reshape(FORM * 48, TILE)
    wut = wu[...].reshape(FORM * 48, TILE)
    gate = dot(nt[...], wgt)
    up = dot(nt[...], wut)
    dh = None
    wds = []
    for part in range(3):
        wdt = wd[:, 64 * part : 64 * (part + 1), :].reshape(TILE, TILE)
        wds.append(wdt)
        term = dot(gr[:, TILE * part : TILE * (part + 1)], wdt, ((1,), (1,)))
        dh = term if dh is None else dh + term
    sq = gate * gate
    th = jnp.tanh(GELU_C * gate * (1.0 + GELU_A * sq))
    half = 0.5 * (1.0 + th)
    act = gate * half
    slope = half + 0.5 * gate * (1.0 - th * th) * (GELU_C * (1.0 + 3.0 * GELU_A * sq))
    h = (act * up).astype(bf16)
    g = (dh * up * slope).astype(bf16)
    u = (dh * act).astype(bf16)
    hid[...] = h
    dg[...] = g
    du[...] = u
    for part in range(3):
        cols = slice(TILE * part, TILE * (part + 1))
        osum[:, cols] = osum[:, cols] + dot(h, wds[part])
    dsum[...] = dsum[...] + dot(g, wgt, ((1,), (1,))) + dot(u, wut, ((1,), (1,)))

    @pl.when(j == pl.num_programs(0) - 1)
    def _():
        out[...] = osum[...].astype(out.dtype)
        dn[...] = dsum[...].astype(dn.dtype)


def feed(nt, gr, packed, units, kind):
    tok, d = nt.shape
    col = pl.BlockSpec((tok, TILE), lambda j: (0, j))
    full = whole((tok, d))
    return kernel_call(
        feed_kernel,
        (struct((tok, d), kind), struct((tok, d), kind)) + (struct((tok, units), bf16),) * 3,
        grid=(units // TILE,),
        ins=[
            full,
            full,
            pl.BlockSpec((FORM, 48, TILE), lambda j: (0, j, 0)),
            pl.BlockSpec((FORM, 48, TILE), lambda j: (0, 4 + j, 0)),
            pl.BlockSpec((4, 192, TILE), lambda j: (j, 2, 0)),
        ],
        out_specs=(full, full, col, col, col),
        scratch=[pltpu.VMEM((tok, d), f32), pltpu.VMEM((tok, d), f32)],
        flops=12 * tok * d * units,
        moved=2 * packed.size + 10 * tok * d + 6 * tok * units,
        vmem=24,
        name="feed",
    )(nt, gr, packed, packed, packed)


def middle_kernel(info, mid, da, db, og, gain, packed, dmid, dlow, ga, gb, gsum):
    tok, d = mid.shape
    gsum[...] = jnp.zeros_like(gsum)

    def norm(t, _):
        at = pl.ds(pl.multiple_of(t * 16, 16), 16)
        v = mid[at, :]
        e = da[at, :] + db[at, :].astype(f32)
        r = lax.rsqrt(jnp.mean(v * v, axis=1, keepdims=True) + EPS)
        ge = gain[...] * e
        m = jnp.mean(ge * v, axis=1, keepdims=True)
        out = og[at, :].astype(f32) + r * ge - v * (r * r * r * m)
        dmid[at, :] = out
        dlow[at, :] = out.astype(bf16)
        part = e * v * r
        gsum[...] = gsum[...] + part[0:8] + part[8:16]
        return 0

    lax.fori_loop(0, tok // 16, norm, 0)
    for rel in range(4):
        out = None
        for part in range(3):
            cols = slice(TILE * part, TILE * (part + 1))
            term = dot(merge_rows(packed, info[0] ^ rel, part), dlow[:, cols], ((1,), (1,)))
            out = term if out is None else out + term
        low = out.astype(bf16)
        for t in range(tok // 128):
            ref = ga if rel < 2 else gb
            ref[rel % 2, t] = low[:, 128 * t : 128 * (t + 1)]


def middle(me, mid, da, db, og, gain, packed):
    tok, d = mid.shape
    args = (mid, da, db, og, gain, packed)
    sent = (2, tok // 128, d // 4, 128)
    shapes = [((tok, d), f32), ((tok, d), bf16), (sent, bf16), (sent, bf16), ((8, d), f32)]
    return kernel_call(
        middle_kernel,
        tuple(struct(*s) for s in shapes),
        prefetch=1,
        ins=[MERGE_ROWS if x is packed else whole(x.shape) for x in args],
        out_specs=tuple(whole(s[0]) for s in shapes),
        flops=2 * tok * d * d,
        moved=30 * tok * d,
        vmem=24,
        name="middle",
    )(me, mid, da, db, *in_hbm(og, gain, packed))


def merge_grad_kernel(info, a0, a1, a2, a3, dlow, keep, send):
    per = a0.shape[0]
    width = a0.shape[1]
    me = info[0]
    for rel in range(4):
        pieces = [(a0[t], a1[t], a2[t], a3[t])[rel] for t in range(per)]
        left = jnp.concatenate(pieces, axis=1)
        rows = pl.ds(pl.multiple_of((me ^ rel) * width, 64), width)
        out = dot(left, dlow[...])
        for part in range(4):
            cols = out[:, width * part : width * (part + 1)]
            far = me ^ part

            @pl.when(far % 2 == 0)
            def _():
                keep[far // 2, rows, :] = cols

            @pl.when(far % 2 == 1)
            def _():
                send[far // 2, rows, :] = cols.astype(bf16)


def merge_grad(info, a0, a1, a2, a3, dlow):
    tok, d = dlow.shape
    args = (*in_hbm(a0, a1, a2, a3), dlow)
    shape = (2, d, d // 4)
    return kernel_call(
        merge_grad_kernel,
        (struct(shape, f32), struct(shape, bf16)),
        prefetch=1,
        ins=[whole(x.shape) for x in args],
        out_specs=(whole(shape), whole(shape)),
        flops=2 * tok * d * d,
        moved=4 * tok * d + 3 * d * d,
        vmem=20,
        name="merge_grad",
    )(info, *args)


def weight_kernel(na, nb, ga, gb, ha, dga, dua, hb, dgb, dub, out, nt):
    j = pl.program_id(0)
    tok, d = na.shape

    @pl.when(j == 0)
    def _():
        nt[:, :tok] = na[...].astype(f32).T.astype(bf16)
        nt[:, tok:] = nb[...].astype(f32).T.astype(bf16)

    for base, left, right in ((0, dga, dgb), (384, dua, dub)):
        grad = (dot(nt[:, :tok], left[...]) + dot(nt[:, tok:], right[...])).astype(bf16)
        for part in range(TILE // 128):
            at = pl.multiple_of(base + 48 * ((TILE // 128) * j + part), 16)
            out[:, pl.ds(at, 48), :] = grad[:, 128 * part : 128 * (part + 1)].reshape(FORM, 48, 128)
    grad = dot(ha[...].astype(f32).T.astype(bf16), ga[...]) + dot(hb[...].astype(f32).T.astype(bf16), gb[...])
    grad = grad.astype(bf16)
    for part in range(d // 128):
        low = 768 + 64 * part
        out[pl.ds(4 * j, 4), low : low + 64, :] = grad[:, 128 * part : 128 * (part + 1)].reshape(4, 64, 128)


def weight_grads(na, nb, ga, gb, left, right):
    tok, d = na.shape
    units = left[0].shape[1]
    args = (na, nb, ga, gb, *left, *right)
    col = pl.BlockSpec((tok, TILE), lambda j: (0, j))
    shape = (FORM, 1152, 128)
    return kernel_call(
        weight_kernel,
        struct(shape, bf16),
        grid=(units // TILE,),
        ins=[whole(x.shape) for x in args[:4]] + [col] * 6,
        out_specs=whole(shape),
        scratch=[pltpu.VMEM((d, 2 * tok), bf16)],
        flops=6 * 2 * tok * d * units,
        moved=12 * tok * units + 16 * tok * d,
        vmem=28,
        name="weight_grads",
    )(*args)


def regroup(stacked, parts, groups):
    count, _, width = stacked.shape
    if count == groups:
        return stacked
    pieces, low = [], 0
    for blocks, rows in parts:
        piece = stacked[:, low : low + blocks * rows].reshape(count, blocks, rows, width)
        low += blocks * rows
        piece = jnp.transpose(piece, (1, 0, 2, 3)).reshape(blocks, groups, count * rows // groups, width)
        pieces.append(jnp.transpose(piece, (1, 0, 2, 3)).reshape(groups, blocks * count * rows // groups, width))
    return jnp.concatenate(pieces, axis=1)


def to_blocks(mat, width):
    rows, cols = mat.shape
    return jnp.transpose(mat.reshape(rows, cols // width, width), (1, 0, 2)).reshape(-1, width)


def from_blocks(stacked, rows):
    blocks, width = stacked.shape[0] // rows, stacked.shape[1]
    return jnp.transpose(stacked.reshape(blocks, rows, width), (1, 0, 2)).reshape(rows, blocks * width)


def flip(x, bit):
    return lax.ppermute(x, ULY, [(i, i ^ bit) for i in range(4)])


def ordered(core, mine, theirs, axis):
    first = jnp.where(core == 0, mine, theirs)
    second = jnp.where(core == 0, theirs, mine)
    return jnp.concatenate([first, second], axis=axis)


def local(
    n_ctx,
    byte_embed,
    query_weight,
    key_weight,
    value_weight,
    merge_weight,
    gate_weight,
    up_weight,
    down_weight,
    conv_weight,
    score_weight,
    attn_gain,
    ffn_gain,
    bias_table,
    doc_lengths,
    rel_bucket,
    out_grad,
):
    nb, d = byte_embed.shape
    tok = out_grad.shape[0]
    n_dev = n_ctx * 4
    groups = n_ctx * 2
    rows_dev = query_weight.shape[0]
    rows_ctx = 4 * rows_dev
    down_dev = down_weight.shape[0]
    heads = HEADS // 4
    width = heads * HEAD_DIM
    group_len = tok * 4
    ext = 2 * group_len
    ff = gate_weight.shape[1]
    unit = ff // n_dev
    ctx_at = lax.axis_index("ctx")
    row_at = lax.axis_index("ux")
    core = lax.axis_index("uc")
    uly_at = lax.axis_index(ULY)
    dev_at = lax.axis_index(RING)
    me = uly_at.astype(jnp.int32).reshape(1)

    up_pairs = [(i, i + 1) for i in range(n_dev - 1)]
    down_pairs = [(i + 1, i) for i in range(n_dev - 1)]
    lo = lax.ppermute(byte_embed[nb - 8 :], RING, up_pairs)
    hi = lax.ppermute(byte_embed[:8], RING, down_pairs)

    count = doc_lengths.shape[0]
    order = lax.broadcasted_iota(jnp.int32, (count, count), 0)
    before = lax.broadcasted_iota(jnp.int32, (count, count), 1)
    starts = jnp.sum(jnp.where(before < order, doc_lengths[None, :], 0), axis=1)
    limit = jnp.sum(doc_lengths)

    shape = (nb + 16, 128)
    here = dev_at * nb - 8 + lax.broadcasted_iota(jnp.int32, shape, 0)
    there = here + lax.broadcasted_iota(jnp.int32, shape, 1) - 2
    between = jnp.sum(
        ((starts[None, None, :] <= here[:, :, None]) != (starts[None, None, :] <= there[:, :, None])).astype(jnp.int32),
        axis=2,
    )
    msk = ((between == 0) & (there >= 0) & (there < limit)).astype(f32)

    cw, sw = conv_weight, score_weight[None, :]
    gain_one, gain_two = attn_gain[None, :], ffn_gain[None, :]

    qkv_own = jnp.stack(
        [w.reshape(rows_dev, 4, width) for w in (query_weight, key_weight, value_weight)], axis=2
    ).reshape(rows_dev, 4, 3 * width)
    doubling = rows_ctx % 16 == 0
    take = lambda x, at, dim: lax.dynamic_index_in_dim(x, at, dim, keepdims=False)
    if doubling:
        cols = jnp.transpose(qkv_own, (1, 0, 2)).reshape(2, 2, rows_dev, 3 * width)
        got = flip(take(cols, 1 - core, 1), 1)
        cols = ordered(core, take(cols, core, 1), got, 1)
        got = flip(take(cols, 1 - row_at, 0), 2)
        qkv_w = ordered(row_at, take(cols, row_at, 0), got, 0)[None]
    else:
        qkv_send = jnp.broadcast_to(
            jnp.transpose(qkv_own, (1, 0, 2))[None], (n_ctx, 4, rows_dev, 3 * width)
        ).reshape(n_dev, rows_dev, 3 * width)
        qkv_w = lax.all_to_all(qkv_send, RING, 0, 0, tiled=True).reshape(8, d // 8, 3 * width)

    codes = [0]
    if doubling:
        bits_left = [1 << i for i in range(n_ctx.bit_length() - 1)][::-1]

        def double(qkv_w, bit):
            got = lax.ppermute(qkv_w, "ctx", [(i, i ^ bit) for i in range(n_ctx)])
            return jnp.concatenate([qkv_w, got], axis=0)

        gbst, normed, conv, aw = gbst_forward(lo, byte_embed, hi, msk, cw, sw, gain_one)
        gate_in, up_in, merge_in = gate_weight, up_weight, merge_weight
        for i, bit in enumerate(bits_left):
            if i < len(bits_left) - 1:
                qkv_w = double(qkv_w, bit)
            codes = codes + [c ^ bit for c in codes]
            if i == 0:
                gate_in, up_in, merge_in, qkv_w, normed = lax.optimization_barrier(
                    (gate_in, up_in, merge_in, qkv_w, normed)
                )
        places = ctx_at ^ jnp.array(codes, jnp.int32)
    else:
        gbst, normed, conv, aw = gbst_forward(lo, byte_embed, hi, msk, cw, sw, gain_one)
        gate_in, up_in, merge_in = gate_weight, up_weight, merge_weight
        places = jnp.arange(8, dtype=jnp.int32)
    weight_info = jnp.concatenate([me, places.astype(jnp.int32)])
    chunk = jnp.concatenate([gate_in, up_in, merge_in], axis=1)
    chip = ordered(core, chunk, flip(chunk, 1), 0)

    def split(at):
        halves = [
            lax.dynamic_index_in_dim(
                chip[:, low : low + ff].reshape(2 * rows_dev, n_ctx, 2, 2 * unit), at, 2, keepdims=False
            ).reshape(2 * rows_dev, ff // 2)
            for low in (0, ff)
        ]
        return jnp.concatenate(halves + [chip[:, 2 * ff :]], axis=1)

    both = jnp.where(row_at == core, split(row_at), flip(split(1 - row_at), 2))
    packed_own = jnp.concatenate(
        [
            to_blocks(both[:, : ff // 2], TILE),
            to_blocks(both[:, ff // 2 : ff], TILE),
            to_blocks(down_weight, TILE),
            to_blocks(both[:, ff:], TILE),
        ],
        axis=0,
    )
    starts, limit, _ = lax.optimization_barrier((starts, limit, aw))

    tok_at = ctx_at * group_len - group_len // 2 + jnp.arange(ext, dtype=jnp.int32)
    tok_doc = jnp.sum((starts[None, :] <= 2 * tok_at[:, None]).astype(jnp.int32), axis=1) - 1
    tok_doc = jnp.where((tok_at >= 0) & (2 * tok_at < limit), tok_doc, -1)
    bits = count.bit_length()
    lane = jnp.arange(TILE, dtype=jnp.int32) - width

    def coded(docs, code, agree, value):
        bit_on = ((docs >> jnp.clip(code // 2, 0, 31)) & 1) == 1
        used = (code >= 0) & (code < 2 * bits)
        return jnp.where(used & ((bit_on == (code % 2 == 1)) == agree), value, 0.0).astype(bf16)

    code_k = coded(tok_doc[:, None], lane[None, :], True, 1.0)
    own_doc = tok_doc[group_len // 2 : group_len // 2 + group_len]
    code_q = coded(own_doc[:, None], lane[None, :], False, -BIG)
    tiles = group_len // TILE
    first = ctx_at * group_len + TILE * jnp.arange(tiles, dtype=jnp.int32)
    begin = jnp.max(jnp.where(starts[None, :] <= 2 * first[:, None], starts[None, :], 0), axis=1)
    last = 2 * (first + TILE - 1)
    end = jnp.min(jnp.where(starts[None, :] > last[:, None], starts[None, :], limit), axis=1)
    shift = group_len // 2 - ctx_at * group_len
    tile_lo = jnp.clip(((begin + 1) // 2 + shift) // TILE, 0, ext // TILE)
    tile_hi = jnp.clip(((end - 1) // 2 + shift) // TILE + 1, 0, ext // TILE)
    info = jnp.concatenate([tile_lo, tile_hi, me]).astype(jnp.int32)

    rel_count = rel_bucket.shape[0]
    diag_len = 2 * DOC_TOK + 2 * TILE
    bucket = jnp.pad(rel_bucket[::-1], (diag_len - TILE - rel_count, TILE), constant_values=-1)
    onehot = (bucket[None, :] == jnp.arange(NBUCK, dtype=jnp.int32)[:, None]).astype(f32)
    table_here = lax.dynamic_slice_in_dim(bias_table, uly_at * heads, heads, 1)
    diag = lax.dot_general(table_here, onehot, (((0,), (0,)), ((), ())), precision=highest)

    near = [(4 * c + u, 4 * (c + s) + u) for c in range(n_ctx) for u, s in ((0, -1), (1, -1), (2, 1), (3, 1)) if 0 <= c + s < n_ctx]
    far0 = lax.ppermute(normed, RING, near)
    own2 = flip(normed, 2)
    packed_own, far0, own2, qkv_w = lax.optimization_barrier((packed_own, far0, own2, qkv_w))
    packed = lax.all_gather(packed_own, ("ctx", "uc"), axis=0, tiled=False)
    packed = packed.reshape(groups, packed_own.shape[0], TILE)
    packed = regroup(
        packed,
        ((4, 2 * rows_dev), (4, 2 * rows_dev), (3, down_dev), (3, 2 * rows_dev)),
        FORM,
    )


    own1 = flip(normed, 1)
    own3 = flip(own2, 1)
    far2 = flip(far0, 2)
    far1 = flip(far0, 1)
    far3 = flip(far2, 1)
    grad_in, far3 = lax.optimization_barrier((out_grad, far3))
    grad_other = flip(grad_in, 2)
    if doubling:
        qkv_got = lax.ppermute(qkv_w, "ctx", [(i, i ^ bits_left[-1]) for i in range(n_ctx)])
        qkv_got, far2 = lax.optimization_barrier((qkv_got, far2))
        qkv_w = jnp.concatenate([qkv_w, qkv_got], axis=0)
    own = (normed, own1, own2, own3)
    far = (far0, far1, far2, far3)
    q, k, v, vt, wp = project(weight_info, own, far, qkv_w, code_q, code_k, heads)

    oa, ob, oloc, lse = attend(info, q, k, vt, diag, heads, tok)
    got2 = flip(ob, 2)
    got2, grad_other = lax.optimization_barrier((got2, grad_other))
    att = (oa[0], flip(oa[1], 1), got2[0], flip(got2[1], 1))
    mid, normed_two = merge(me, *att, packed, gbst, gain_two)

    normed_other = flip(normed_two, 2)
    out_a, dn_a, *left = feed(normed_two, out_grad, packed, ff // 2, f32)
    normed_other, dn_a = lax.optimization_barrier((normed_other, dn_a))
    out_b, dn_b, *right = feed(normed_other, grad_other, packed, ff // 2, bf16)
    dn_got = flip(dn_b, 2)
    grads = weight_grads(normed_two, normed_other, out_grad, grad_other, left, right)
    dn_got, grads = lax.optimization_barrier((dn_got, grads))
    parts16 = ((8, 48), (8, 48), (6, 64))
    grads = regroup(grads, parts16, groups)
    summed = lax.psum_scatter(grads, ("ctx", "uc"), scatter_dimension=0, tiled=False)
    dmid, dlow, ga, gb2, ffn_sum = middle(me, mid, dn_a, dn_got, out_grad, gain_two, packed)
    back2 = flip(gb2, 2)
    back1 = flip(ga[1], 1)
    back1, dlow = lax.optimization_barrier((back1, dlow))
    keep_m, send_m = merge_grad(me, *att, dlow)
    recv_m = flip(send_m, 1)
    back = (ga[0], back1, back2[0], flip(back2[1], 1))
    mid_m = (keep_m[1] + recv_m[1].astype(f32)).astype(bf16)

    out_b, mid_m, *back = lax.optimization_barrier((out_b, mid_m, *back))
    got_m = flip(mid_m, 2)
    out_got = flip(out_b, 2)
    dq, dk, dv, sums = attend_back(info, q, k, v, diag, oloc, lse, *back, heads)
    out_got, got_m, dk = lax.optimization_barrier((out_got, got_m, dk))
    layer_out = (mid + out_a + out_got.astype(f32)).astype(bf16)
    grad_info = jnp.concatenate([me, jnp.arange(8, dtype=jnp.int32)])
    hk0, hk2, hs1, hs3 = project_back(True, me, dq, dk, dv, wp)
    h_mid = (hk2 + flip(hs3, 1).astype(f32)).astype(bf16)
    h_mid, dq_g = lax.optimization_barrier((h_mid, dq))
    h_got2 = flip(h_mid, 2)
    part = project_grad(grad_info, own, far, dq_g, dk, dv, keep_m, recv_m, got_m, 8)
    dq_p, part, h_got2, summed = lax.optimization_barrier((dq_g, part, h_got2, summed))
    ok0, ok2, os1, os3 = project_back(False, me, dq_p, dk, dv, wp)
    part = lax.psum_scatter(part.reshape(n_ctx, rows_ctx, 4 * width), "ctx", scatter_dimension=0, tiled=False)
    got = lax.all_to_all(part.reshape(4, rows_dev, 4 * width), ULY, 0, 0, tiled=True)
    h_got1 = flip(hs1, 1)
    o_got1 = flip(os1, 1)
    o_mid = (ok2 + flip(os3, 1).astype(f32)).astype(bf16)
    h_sum = (hk0 + h_got1.astype(f32) + h_got2.astype(f32)).astype(bf16)
    h_sum, o_mid = lax.optimization_barrier((h_sum, o_mid))
    h_back = lax.ppermute(h_sum, RING, [(b, a) for a, b in near])
    o_got2 = flip(o_mid, 2)
    o_sum = ok0 + o_got1.astype(f32) + o_got2.astype(f32)

    sums, _ = lax.optimization_barrier((sums, h_sum))
    twice = jnp.concatenate([sums, sums], axis=3)
    moved = sum(twice[:, :, r, r + TILE : r + 3 * TILE] for r in range(8))
    diag_parts = jnp.transpose(moved, (1, 0, 2))
    count_t = diag_parts.shape[1]
    low = diag_parts[:, :, :TILE].reshape(heads, count_t * TILE)
    high = diag_parts[:, :, TILE:].reshape(heads, count_t * TILE)
    diag_grad = jnp.pad(low, ((0, 0), (0, TILE))) + jnp.pad(high, ((0, 0), (TILE, 0)))
    table_local = lax.dot_general(onehot, diag_grad, (((1,), (1,)), ((), ())), precision=highest)
    table_grad = lax.dynamic_update_slice(jnp.zeros((NBUCK, HEADS), f32), table_local, (0, uly_at * heads))

    eg, small = gbst_backward(
        o_sum, h_back, gbst, dmid, gain_one, conv, aw, lo, byte_embed, hi, msk, cw, sw
    )
    from_prev = lax.ppermute(eg[nb + 8 :], RING, up_pairs)
    from_next = lax.ppermute(eg[:8], RING, down_pairs)
    main = eg[8 : nb + 8]
    embed_grad = jnp.concatenate(
        [main[:8] + from_prev, main[8 : nb - 8], main[nb - 8 :] + from_next], axis=0
    )

    rest = jnp.concatenate(
        [jnp.sum(ffn_sum, axis=0, keepdims=True), jnp.pad(table_grad.reshape(1, -1), ((0, 0), (0, d - NBUCK * HEADS)))],
        axis=0,
    )
    total = jnp.concatenate([small, jnp.pad(rest, ((0, 6), (0, 0)))], axis=0)
    for bit in (1, 2):
        total = total + flip(total, bit)
    bit = 1
    while bit < n_ctx:
        total = total + lax.ppermute(total, "ctx", [(i, i ^ bit) for i in range(n_ctx)])
        bit *= 2

    got, total = lax.optimization_barrier((got, total))
    query_grad, key_grad, value_grad, merge_g = spread(got)

    rows2 = 2 * rows_dev
    down_grad = from_blocks(summed[16 * rows2 :], down_dev).astype(f32)
    mine = jnp.concatenate(
        [from_blocks(summed[: 8 * rows2], rows2), from_blocks(summed[8 * rows2 : 16 * rows2], rows2)], axis=1
    )
    theirs = flip(mine, 2)
    sets = [jnp.where(row_at == at, mine, theirs).reshape(rows2, 2, n_ctx, 1, 2 * unit) for at in (0, 1)]
    full = jnp.concatenate(sets, axis=3).reshape(2, rows_dev, 2 * ff)
    given = flip(lax.dynamic_index_in_dim(full, 1 - core, 0, keepdims=False), 1)
    kept = lax.dynamic_index_in_dim(full, core, 0, keepdims=False)
    final = jnp.where(row_at == core, kept, given).astype(f32)
    return (
        layer_out,
        embed_grad,
        query_grad,
        key_grad,
        value_grad,
        merge_g,
        final[:, :ff],
        final[:, ff:],
        down_grad,
        total[:CONV],
        total[5],
        total[6],
        total[8],
        total[9, : NBUCK * HEADS].reshape(NBUCK, HEADS),
    )


def solution(mesh):
    n_ctx = mesh.shape["ctx"]
    inner = Mesh(mesh.devices.reshape(n_ctx, 2, 2), RING)
    row = P(RING, None)
    return jax.shard_map(
        partial(local, n_ctx),
        mesh=inner,
        in_specs=(row,) * 8 + (P(),) * 7 + (row,),
        out_specs=(row,) * 9 + (P(),) * 5,
        check_vma=False,
    )
```

```python
from functools import partial

import jax
import jax.numpy as jnp
from jax import lax
from jax.experimental import pallas as pl
from jax.experimental.pallas import tpu as pltpu
from jax.sharding import Mesh, PartitionSpec as P

HEADS = 12
HEAD_DIM = 64
NBUCK = 32
CONV = 5
DOC_TOK = 1024
TILE = 256
FORM = 16
PHASES = 12
EPS = 1e-06
BIG = 1e30
GELU_C = 0.7978845608028654
GELU_A = 0.044715

bf16 = jnp.bfloat16
f32 = jnp.float32
RING = ("ctx", "ux", "uc")
ULY = ("ux", "uc")
highest = lax.Precision.HIGHEST


def dot(left, right, dims=((1,), (0,))):
    return lax.dot_general(left, right, (dims, ((), ())), preferred_element_type=f32)


def kernel_call(body, outs, *, grid=(1,), ins, scratch=(), prefetch=0, out_specs=None, flops=0, moved=0, vmem=40, name=None):
    params = pltpu.CompilerParams(
        dimension_semantics=("arbitrary",) * len(grid), vmem_limit_bytes=vmem << 20
    )
    return pl.pallas_call(
        body,
        out_shape=outs,
        grid_spec=pltpu.PrefetchScalarGridSpec(
            num_scalar_prefetch=prefetch,
            grid=grid,
            in_specs=ins,
            out_specs=out_specs,
            scratch_shapes=list(scratch),
        ),
        compiler_params=params,
        cost_estimate=pl.CostEstimate(flops=int(flops) // 8, bytes_accessed=int(moved) // 8, transcendentals=0),
        name=name,
    )


def whole(shape, once=True):
    zeros = (0,) * len(shape)
    if once:
        return pl.BlockSpec(shape, lambda *a: zeros, pipeline_mode=pl.Buffered(1))
    return pl.BlockSpec(shape, lambda *a: zeros)


def in_hbm(*arrays):
    return tuple(pltpu.with_memory_space_constraint(x, pltpu.HBM) for x in arrays)


def struct(shape, dtype):
    return jax.ShapeDtypeStruct(shape, dtype)


def block_of(size, at):
    first = size * (at // size)
    return range(first, first + size)


def token_pairs(tok):
    found = set()
    for byte in (2 * tok, 2 * tok + 1):
        for size in range(1, 5):
            found |= set(block_of(size, byte))
    return sorted(found)


def mix_coefs(weights):
    coefs = {}
    for tok in range(PHASES // 2):
        for at in token_pairs(tok):
            total = None
            for byte in (2 * tok, 2 * tok + 1):
                for size in range(1, 5):
                    if at in block_of(size, byte):
                        term = weights[size - 1][byte] * (0.5 / size)
                        total = term if total is None else total + term
            coefs[tok, at] = total
    return coefs


def lane_chunks(feats):
    return [slice(128 * c, 128 * (c + 1)) for c in range(feats // 128)]


def fill_bytes(pad, lo, emb, hi):
    byte_count, feats = emb.shape
    chunks = lane_chunks(feats)
    for c, cols in enumerate(chunks):
        pad[c, 0:8, :] = lo[:, cols].astype(f32)
        pad[c, 8 + byte_count : 16 + byte_count, :] = hi[:, cols].astype(f32)

    def fill(t, _):
        at = pl.multiple_of(t * 32, 32)
        for c, cols in enumerate(chunks):
            pad[c, pl.ds(at + 8, 32), :] = emb[pl.ds(at, 32), cols].astype(f32)
        return 0

    lax.fori_loop(0, byte_count // 32, fill, 0)


def gbst_forward_kernel(lo, emb, hi, msk, cw, sw, gain, gb, nrm, conv, aw, pad, mix):
    byte_count, feats = emb.shape
    chunks = lane_chunks(feats)
    fill_bytes(pad, lo, emb, hi)
    lanes = lax.broadcasted_iota(jnp.int32, (8, 128), 1)

    def step(g, _):
        base = g * 8 * PHASES + 8
        rows = pl.ds(pl.multiple_of(8 * g, 8), 8)
        first = []
        for p in range(PHASES):
            mask = msk[pl.ds(base + p, 8, stride=PHASES), :]
            same = {k: jnp.broadcast_to(mask[:, k : k + 1], (8, 128)) for k in (0, 1, 3, 4)}
            dots = None
            for c, cols in enumerate(chunks):
                x = pad[c, pl.ds(base + p, 8, stride=PHASES), :] * cw[2:3, cols]
                for k in (0, 1, 3, 4):
                    x = x + pad[c, pl.ds(base + p + k - 2, 8, stride=PHASES), :] * same[k] * cw[k : k + 1, cols]
                conv[p, rows, cols] = x
                term = x * sw[:, cols]
                dots = term if dots is None else dots + term
            first.append(jnp.broadcast_to(jnp.sum(dots, axis=1, keepdims=True), (8, 128)))
        weights = [[None] * PHASES for _ in range(4)]
        packed = jnp.zeros((8, 128), f32)
        for p in range(PHASES):
            scores = []
            for size in range(1, 5):
                total = None
                for at in block_of(size, p):
                    total = first[at] if total is None else total + first[at]
                scores.append(total * (1.0 / size))
            top = jnp.maximum(jnp.maximum(scores[0], scores[1]), jnp.maximum(scores[2], scores[3]))
            exps = [jnp.exp(s - top) for s in scores]
            inv = 1.0 / (exps[0] + exps[1] + exps[2] + exps[3])
            for size in range(4):
                weights[size][p] = exps[size] * inv
                packed = jnp.where(lanes == 4 * p + size, weights[size][p], packed)
        aw[rows, :] = packed
        coefs = mix_coefs(weights)
        for tok in range(PHASES // 2):
            for c, cols in enumerate(chunks):
                out = None
                for at in token_pairs(tok):
                    term = coefs[tok, at] * conv[at, rows, cols]
                    out = term if out is None else out + term
                mix[c, pl.ds(g * 4 * PHASES + tok, 8, stride=PHASES // 2), :] = out
        return 0

    lax.fori_loop(0, byte_count // (8 * PHASES), step, 0)

    def norm(t, _):
        at = pl.multiple_of(t * 16, 16)
        v = jnp.concatenate([mix[c, pl.ds(at, 16), :] for c in range(len(chunks))], axis=1)
        r = lax.rsqrt(jnp.mean(v * v, axis=1, keepdims=True) + EPS)
        gb[pl.ds(at, 16), :] = v
        nrm[pl.ds(at, 16), :] = (v * r * gain[...]).astype(bf16)
        return 0

    lax.fori_loop(0, byte_count // 32, norm, 0)


def gbst_forward(lo, emb, hi, msk, cw, sw, gain):
    nb, d = emb.shape
    return kernel_call(
        gbst_forward_kernel,
        (
            struct((nb // 2, d), f32),
            struct((nb // 2, d), bf16),
            struct((PHASES, nb // PHASES, d), f32),
            struct((nb // PHASES, 128), f32),
        ),
        ins=[whole(x.shape) for x in (lo, emb, hi, msk, cw, sw, gain)],
        out_specs=(
            whole((nb // 2, d)),
            whole((nb // 2, d)),
            whole((PHASES, nb // PHASES, d)),
            whole((nb // PHASES, 128)),
        ),
        scratch=[pltpu.VMEM((d // 128, nb + 16, 128), f32), pltpu.VMEM((d // 128, nb // 2, 128), f32)],
        flops=60 * nb * d,
        moved=20 * nb * d,
        vmem=20,
        name="gbst_forward",
    )(lo, emb, hi, msk, cw, sw, gain)


def gbst_backward_kernel(keep, recv, gb, dmid, gain, conv, aw, lo, emb, hi, msk, cw, sw, eg, small, dtok, dconv, pad, acc):
    byte_count, feats = emb.shape
    chunks = lane_chunks(feats)
    acc[...] = jnp.zeros_like(acc)
    fill_bytes(pad, lo, emb, hi)
    for c in range(len(chunks)):
        dconv[c, 0:16, :] = jnp.zeros((16, 128), f32)
        dconv[c, 16 + byte_count : 32 + byte_count, :] = jnp.zeros((16, 128), f32)

    def norm(t, _):
        at = pl.multiple_of(t * 16, 16)
        e = keep[pl.ds(at, 16), :] + recv[pl.ds(at, 16), :].astype(f32)
        v = gb[pl.ds(at, 16), :]
        r = lax.rsqrt(jnp.mean(v * v, axis=1, keepdims=True) + EPS)
        ge = gain[...] * e
        m = jnp.mean(ge * v, axis=1, keepdims=True)
        out = dmid[pl.ds(at, 16), :] + r * ge - v * (r * r * r * m)
        for c, cols in enumerate(chunks):
            dtok[c, pl.ds(at, 16), :] = out[:, cols]
        part = e * v * r
        acc[48:56, :] = acc[48:56, :] + part[0:8] + part[8:16]
        return 0

    lax.fori_loop(0, byte_count // 32, norm, 0)

    def step(g, _):
        rows = pl.ds(pl.multiple_of(8 * g, 8), 8)
        half = PHASES // 2

        def tok_rows(tok, c):
            return dtok[c, pl.ds(g * 8 * half + tok, 8, stride=half), :]

        inner = {}
        for tok in range(half):
            toks = [tok_rows(tok, c) for c in range(len(chunks))]
            for at in token_pairs(tok):
                dots = None
                for c, cols in enumerate(chunks):
                    term = toks[c] * conv[at, rows, cols]
                    dots = term if dots is None else dots + term
                inner[tok, at] = jnp.broadcast_to(jnp.sum(dots, axis=1, keepdims=True), (8, 128))
        tile = aw[rows, :]
        weights = [
            [jnp.broadcast_to(tile[:, 4 * p + size : 4 * p + size + 1], (8, 128)) for p in range(PHASES)]
            for size in range(4)
        ]
        coefs = mix_coefs(weights)
        dsize = [[None] * PHASES for _ in range(4)]
        for p in range(PHASES):
            cs = []
            for size in range(1, 5):
                total = None
                for at in block_of(size, p):
                    total = inner[p // 2, at] if total is None else total + inner[p // 2, at]
                cs.append(total * (0.5 / size))
            mean = sum(weights[s][p] * cs[s] for s in range(4))
            for s in range(4):
                dsize[s][p] = weights[s][p] * (cs[s] - mean)
        slopes = []
        for at in range(PHASES):
            e = None
            for size in range(1, 5):
                for p in block_of(size, at):
                    term = dsize[size - 1][p] * (1.0 / size)
                    e = term if e is None else e + term
            slopes.append(e)
        for c, cols in enumerate(chunks):
            toks = [tok_rows(tok, c) for tok in range(half)]
            score = acc[40:48, cols]
            for at in range(PHASES):
                out = slopes[at] * sw[:, cols]
                for tok in range(half):
                    if (tok, at) in coefs:
                        out = out + coefs[tok, at] * toks[tok]
                dconv[c, pl.ds(g * 8 * PHASES + 16 + at, 8, stride=PHASES), :] = out
                score = score + slopes[at] * conv[at, rows, cols]
            acc[40:48, cols] = score
        return 0

    lax.fori_loop(0, byte_count // (8 * PHASES), step, 0)

    def taps(t, _):
        masks = []
        for u in range(2):
            mask = msk[pl.ds(pl.multiple_of(t * 16 + 8 * u, 8), 8), :]
            masks.append({k: jnp.broadcast_to(mask[:, 4 - k : 5 - k], (8, 128)) for k in (0, 1, 3, 4)})
        for c, cols in enumerate(chunks):
            sums = [None] * CONV
            for u in range(2):
                at = pl.multiple_of(t * 16 + 8 * u, 8)
                x = pad[c, pl.ds(at, 8), :]
                out = None
                for k in range(CONV):
                    z = dconv[c, pl.ds(at + 8 + 2 - k, 8), :]
                    if k != 2:
                        z = z * masks[u][k]
                    term = z * cw[k : k + 1, cols]
                    out = term if out is None else out + term
                    sums[k] = z * x if sums[k] is None else sums[k] + z * x
                eg[pl.ds(at, 8), cols] = out
            for k in range(CONV):
                acc[8 * k : 8 * k + 8, cols] = acc[8 * k : 8 * k + 8, cols] + sums[k]
        return 0

    lax.fori_loop(0, (byte_count + 16) // 16, taps, 0)
    small[...] = jnp.zeros_like(small)
    for k in range(7):
        small[k : k + 1, :] = jnp.sum(acc[8 * k : 8 * k + 8, :], axis=0, keepdims=True)


def gbst_backward(keep, recv, gb, dmid, gain, conv, aw, lo, emb, hi, msk, cw, sw):
    nb, d = emb.shape
    args = (keep, recv, *in_hbm(gb, dmid, gain, conv, aw, lo, emb, hi, msk, cw, sw))
    return kernel_call(
        gbst_backward_kernel,
        (struct((nb + 16, d), f32), struct((8, d), f32)),
        ins=[whole(x.shape) for x in args],
        out_specs=(whole((nb + 16, d)), whole((8, d))),
        scratch=[
            pltpu.VMEM((d // 128, nb // 2, 128), f32),
            pltpu.VMEM((d // 128, nb + 32, 128), f32),
            pltpu.VMEM((d // 128, nb + 16, 128), f32),
            pltpu.VMEM((56, d), f32),
        ],
        flops=4 * 10**11,
        moved=24 * nb * d,
        vmem=28,
        name="gbst_backward",
    )(*args)


def halo_row(who, tok_dev, ext):
    return jnp.where(who >= 2, (who - 2) * tok_dev, ext - 2 * tok_dev + who * tok_dev)


def project_kernel(n_heads, info, *refs):
    own, far, w, cq, ck, (q, k, v, vt, wp) = refs[:4], refs[4:8], refs[8], refs[9], refs[10], refs[11:16]
    tok, _ = own[0].shape
    me = info[0]
    part = w.shape[2] // 3
    rows = w.shape[1]
    wp[...] = jnp.zeros_like(wp)
    for b in range(w.shape[0]):
        at = pl.ds(pl.multiple_of(info[1 + b] * rows, 16), rows)
        block = w[b]
        for j in range(3):
            wp[at, TILE * j : TILE * j + part] = block[:, part * j : part * (j + 1)]
    ext = k.shape[0]
    left = (ext - q.shape[0]) // 2
    for rel in range(4):
        who = me ^ rel
        out = dot(own[rel][...], wp[...])
        at = pl.ds(pl.multiple_of(who * tok, 128), tok)
        q[at, :] = out[:, :TILE].astype(bf16) + cq[at, :]
        edge = dot(far[rel][...], wp[:, TILE:])
        for at, ks, vs in (
            (left + who * tok, out[:, TILE : 2 * TILE], out[:, 2 * TILE :]),
            (halo_row(who, tok, ext), edge[:, :TILE], edge[:, TILE:]),
        ):
            at = pl.ds(pl.multiple_of(at, 128), tok)
            k[at, :] = ks.astype(bf16) + ck[at, :]
            v[at, :] = vs.astype(bf16)
            vt[:, at] = vs.T.astype(bf16)


def project(info, own, far, w, cq, ck, n_heads):
    tok, d = own[0].shape
    rows, ext = 4 * tok, 8 * tok
    args = (*own, *far, w, cq, ck)
    shapes = [(rows, TILE), (ext, TILE), (ext, TILE), (TILE, ext), (d, 3 * TILE)]
    return kernel_call(
        partial(project_kernel, n_heads),
        tuple(struct(x, bf16) for x in shapes),
        prefetch=1,
        ins=[whole(x.shape) for x in args],
        out_specs=tuple(whole(x) for x in shapes),
        flops=4 * 10**11,
        moved=2 * (ext * d + 2 * ext * TILE + d * d),
        vmem=30,
        name="project",
    )(info, *args)


def project_back_kernel(is_halo, me, dq, dk, dv, wp, keep0, keep2, send1, send3):
    tok = keep0.shape[0]
    ext = dk.shape[0]
    left = (ext - dq.shape[0]) // 2
    for rel, ref in ((3, send3), (1, send1), (2, keep2), (0, keep0)):
        who = me[0] ^ rel
        if is_halo:
            at = pl.multiple_of(halo_row(who, tok, ext), 128)
            out = dot(dk[pl.ds(at, tok), :], wp[:, TILE : 2 * TILE], ((1,), (1,)))
        else:
            at = pl.multiple_of(left + who * tok, 128)
            out = dot(dk[pl.ds(at, tok), :], wp[:, TILE : 2 * TILE], ((1,), (1,)))
            mine = pl.multiple_of(who * tok, 128)
            out = out + dot(dq[pl.ds(mine, tok), :], wp[:, :TILE], ((1,), (1,)))
        out = out + dot(dv[pl.ds(at, tok), :], wp[:, 2 * TILE :], ((1,), (1,)))
        ref[...] = out.astype(ref.dtype)


def project_back(is_halo, me, dq, dk, dv, wp):
    ext, d = dk.shape[0], wp.shape[0]
    tok = ext // 8
    args = (dq, dk, dv, wp)
    kinds = (f32, f32, bf16, bf16)
    return kernel_call(
        partial(project_back_kernel, is_halo),
        tuple(struct((tok, d), kind) for kind in kinds),
        prefetch=1,
        ins=[whole(x.shape) for x in args],
        out_specs=tuple(whole((tok, d)) for _ in kinds),
        flops=2 * ext // 2 * d * 3 * TILE,
        moved=4 * ext * d,
        vmem=20,
        name="project_back",
    )(me, *args)


def project_grad_kernel(info, *refs):
    own, far, (dq, dk, dv, mkeep, mrecv, mgot), out, flat = refs[:4], refs[4:8], refs[8:14], refs[14], refs[15]
    tok = own[0].shape[0]
    ext = dk.shape[0]
    me = info[0]
    left = (ext - dq.shape[0]) // 2
    part = mgot.shape[1]
    totals = [None] * 3

    def turned(ref, at):
        return ref[pl.ds(pl.multiple_of(at, 128), tok), :].astype(f32).T[:part].astype(bf16)

    for rel in range(4):
        who = me ^ rel
        at = left + who * tok
        edge = halo_row(who, tok, ext)
        terms = [
            dot(turned(dq, who * tok), own[rel][...]),
            dot(turned(dk, at), own[rel][...]) + dot(turned(dk, edge), far[rel][...]),
            dot(turned(dv, at), own[rel][...]) + dot(turned(dv, edge), far[rel][...]),
        ]
        totals = [t if x is None else x + t for x, t in zip(totals, terms)]
    for j in range(3):
        flat[:, part * j : part * (j + 1)] = totals[j].T.astype(bf16)
    merged = mkeep[0] + mrecv[0].astype(f32) + mgot[...].astype(f32)
    flat[:, 3 * part :] = merged.astype(bf16)
    rows = out.shape[1]
    for b in range(out.shape[0]):
        out[b] = flat[pl.ds(pl.multiple_of(info[1 + b] * rows, 16), rows), :]


def project_grad(info, own, far, dq, dk, dv, mkeep, mrecv, mgot, blocks):
    tok, d = own[0].shape
    args = (*in_hbm(*own, *far), dq, dk, dv, *in_hbm(mkeep, mrecv, mgot))
    shape = (blocks, d // blocks, 4 * mgot.shape[1])
    return kernel_call(
        project_grad_kernel,
        struct(shape, bf16),
        prefetch=1,
        ins=[whole(x.shape) for x in args],
        out_specs=whole(shape),
        scratch=[pltpu.VMEM((d, shape[2]), bf16)],
        flops=2 * 8 * tok * d * 3 * mgot.shape[1],
        moved=2 * 12 * tok * d,
        vmem=28,
        name="project_grad",
    )(info, *args)


def spread_kernel(got, *outs):
    width = got.shape[2] // 4
    for j, out in enumerate(outs):
        for u in range(4):
            out[:, width * u : width * (u + 1)] = got[u, :, width * j : width * (j + 1)].astype(f32)


def spread(got):
    _, rows, d = got.shape
    return kernel_call(
        spread_kernel,
        (struct((rows, d), f32),) * 4,
        ins=[whole(got.shape)],
        out_specs=(whole((rows, d)),) * 4,
        flops=8 * 10**11,
        moved=24 * rows * d,
        vmem=8,
        name="spread",
    )(got)


def fill_bias(diag, bias):
    count = bias.shape[0]
    heads = diag.shape[0]

    def tile(t, _):
        seg = diag[:, pl.ds(pl.multiple_of((count - 1 - t) * TILE, TILE), 2 * TILE)]
        for h in range(heads):
            rows = jnp.broadcast_to(seg[h : h + 1, :], (TILE, 2 * TILE))
            turned = pltpu.roll(rows, TILE, axis=1, stride=1, stride_axis=0)
            bias[t, :, TILE * h : TILE * (h + 1)] = turned[:, :TILE]
        return 0

    lax.fori_loop(0, count, tile, 0)


def sum_diagonals(tiles, out):
    count, heads, _, _ = out.shape

    def tile(t, _):
        for h in range(heads):
            part = tiles[t, :, TILE * h : TILE * (h + 1)]
            cur = jnp.concatenate([part, jnp.zeros_like(part)], axis=1)
            rows = TILE
            while rows > 8:
                rows //= 2
                cur = cur[:rows] + pltpu.roll(cur[rows:], 2 * TILE - rows, axis=1)
            out[count - 1 - t, h] = cur
        return 0

    lax.fori_loop(0, count, tile, 0)


def lane_head(shape):
    return lax.broadcasted_iota(jnp.int32, shape, 1) // HEAD_DIM


def fill_queries(heads, q, q3):
    turned = q[...].astype(f32).T
    row = lax.broadcasted_iota(jnp.int32, (TILE, TILE), 0) // HEAD_DIM
    for h in range(heads):
        q3[:, TILE * h : TILE * (h + 1)] = jnp.where((row == h) | (row >= heads), turned, 0.0).astype(bf16)


def attend_kernel(heads, info, q, k, vt, diag, oa, ob, oloc, lse, bias, q3, sc, ac):
    i = pl.program_id(0)
    grid = pl.num_programs(0)
    me = info[2 * grid]
    ext = k.shape[0]
    wide = heads * TILE

    @pl.when(i == 0)
    def _():
        fill_bias(diag, bias)

    lo, hi = info[i], info[grid + i]
    away = (ext // TILE - grid) // 2
    fill_queries(heads, q, q3)
    ac[...] = jnp.zeros_like(ac)

    def scores(kt, top):
        at = pl.multiple_of(kt * TILE, TILE)
        s = dot(k[pl.ds(at, TILE), :], q3[...]) + bias[kt - i - away + 4]
        sc[kt - lo] = s
        return jnp.maximum(top, jnp.max(s.reshape(TILE // 8, 8, wide), axis=0))

    top = lax.fori_loop(lo, hi, scores, jnp.full((8, wide), -jnp.inf, f32))
    top = jnp.max(top, axis=0, keepdims=True)

    def gather(kt, total):
        at = pl.multiple_of(kt * TILE, TILE)
        p = jnp.exp(sc[kt - lo] - top)
        low = p.astype(bf16)
        for h in range(heads):
            cols = slice(TILE * h, TILE * (h + 1))
            head = slice(HEAD_DIM * h, HEAD_DIM * (h + 1))
            ac[head, :] = ac[head, :] + dot(vt[head, pl.ds(at, TILE)], low[:, cols])
        return total + jnp.sum(p.reshape(TILE // 8, 8, wide), axis=0)

    total = lax.fori_loop(lo, hi, gather, jnp.zeros((8, wide), f32))
    total = jnp.sum(total, axis=0, keepdims=True)
    inv = 1.0 / total
    lse[0] = jnp.broadcast_to(top + jnp.log(total), (8, wide))
    parts = []
    for h in range(heads):
        parts.append(ac[HEAD_DIM * h : HEAD_DIM * (h + 1), :] * inv[:, TILE * h : TILE * (h + 1)])
    turned = jnp.concatenate(parts, axis=0).astype(bf16)
    oloc[...] = turned
    per = oa.shape[1]
    for j in range(TILE // 128):
        chunk = i * (TILE // 128) + j
        rel = (chunk // per) ^ me
        piece = turned[:, 128 * j : 128 * (j + 1)]

        @pl.when(rel < 2)
        def _():
            oa[rel, chunk % per] = piece

        @pl.when(rel >= 2)
        def _():
            ob[rel - 2, chunk % per] = piece


def attend(info, q, k, vt, diag, heads, tok):
    rows, ext = q.shape[0], k.shape[0]
    grid = rows // TILE
    width = heads * HEAD_DIM
    sent = (2, tok // 128, width, 128)
    tile = pl.BlockSpec((TILE, TILE), lambda i, *_: (i, 0))
    return kernel_call(
        partial(attend_kernel, heads),
        (
            struct(sent, bf16),
            struct(sent, bf16),
            struct((width, rows), bf16),
            struct((grid, 8, heads * TILE), f32),
        ),
        grid=(grid,),
        prefetch=1,
        ins=[tile, whole(k.shape), whole(vt.shape), whole(diag.shape)],
        out_specs=(
            whole(sent),
            whole(sent),
            pl.BlockSpec((width, TILE), lambda i, *_: (0, i)),
            pl.BlockSpec((1, 8, heads * TILE), lambda i, *_: (i, 0, 0)),
        ),
        scratch=[
            pltpu.VMEM((9, TILE, heads * TILE), f32),
            pltpu.VMEM((TILE, heads * TILE), bf16),
            pltpu.VMEM((9, TILE, heads * TILE), f32),
            pltpu.VMEM((width, TILE), f32),
        ],
        flops=4 * rows * 1280 * TILE * heads,
        moved=8 * ext * TILE,
        vmem=30,
        name="attend",
    )(info, q, k, vt, diag)


def attend_back_kernel(
    heads, info, q, k, v, diag, oloc, lse, d0, d1, d2, d3,
    dq, dk, dv, sums,
    bias, tacc, kt_all, q3, g3, q3n, g3n, gall, dqa, dka, dva,
):
    i = pl.program_id(0)
    grid = pl.num_programs(0)
    me = info[2 * grid]
    ext = k.shape[0]
    per = d0.shape[0]
    width = heads * HEAD_DIM

    @pl.when(i == 0)
    def _():
        fill_bias(diag, bias)

        def turn(t, _):
            at = pl.ds(pl.multiple_of(t * TILE, TILE), TILE)
            kt_all[:, at] = k[at, :].astype(f32).T[:width].astype(bf16)
            return 0

        lax.fori_loop(0, ext // TILE, turn, 0)
        dka[...] = jnp.zeros_like(dka)
        dva[...] = jnp.zeros_like(dva)
        tacc[...] = jnp.zeros_like(tacc)
        for rel, piece in ((0, d0[...]), (2, d2[...]), (1, d1[...]), (3, d3[...])):
            gall[pl.ds((me ^ rel) * per, per)] = piece

    lo, hi = info[i], info[grid + i]
    away = (ext // TILE - grid) // 2
    where = lane_head((TILE, TILE))
    fill = jnp.zeros((TILE - width, TILE), f32)
    pieces = [gall[i * (TILE // 128) + j] for j in range(TILE // 128)]
    gt = jnp.concatenate(pieces, axis=1).astype(f32)
    grad = jnp.concatenate([gt, fill], axis=0).T
    prod = gt * oloc[...].astype(f32)
    deltas = []
    fill_queries(heads, q, q3)
    g3[...] = jnp.zeros_like(g3)
    for h in range(heads):
        rows = slice(TILE * h, TILE * (h + 1))
        head = slice(HEAD_DIM * h, HEAD_DIM * (h + 1))
        g3[head, rows] = gt[head, :].astype(bf16)
        q3n[rows, :] = jnp.where(where == h, q[...], jnp.zeros_like(q[...]))
        g3n[rows, :] = jnp.where(where == h, grad, 0.0).astype(bf16)
        deltas.append(jnp.sum(prod[HEAD_DIM * h : HEAD_DIM * (h + 1), :], axis=0, keepdims=True))
    delta = jnp.concatenate(deltas, axis=1)
    log = lse[0, 0:1, :]
    dqa[...] = jnp.zeros_like(dqa)

    def step(kt, _):
        at = pl.ds(pl.multiple_of(kt * TILE, TILE), TILE)
        rel = kt - i - away + 4
        s = dot(k[at, :], q3[...]) + bias[rel]
        p = jnp.exp(s - log)
        dp = dot(v[at, :], g3[...])
        ds = p * (dp - delta)
        tacc[rel] = tacc[rel] + ds
        low = ds.astype(bf16)
        dva[at, :] = dva[at, :] + dot(p.astype(bf16), g3n[...])
        dka[at, :] = dka[at, :] + dot(low, q3n[...])
        for h in range(heads):
            head = slice(HEAD_DIM * h, HEAD_DIM * (h + 1))
            dqa[head, :] = dqa[head, :] + dot(kt_all[head, at], low[:, TILE * h : TILE * (h + 1)])
        return 0

    lax.fori_loop(lo, hi, step, 0)
    dq[...] = jnp.concatenate([dqa[...], fill], axis=0).T.astype(bf16)

    @pl.when(i == grid - 1)
    def _():
        dk[...] = dka[...].astype(bf16)
        dv[...] = dva[...].astype(bf16)
        sum_diagonals(tacc, sums)


def attend_back(info, q, k, v, diag, oloc, lse, d0, d1, d2, d3, heads):
    rows, ext = q.shape[0], k.shape[0]
    grid = rows // TILE
    width = heads * HEAD_DIM
    tile = pl.BlockSpec((TILE, TILE), lambda i, *_: (i, 0))
    turned = pl.BlockSpec((width, TILE), lambda i, *_: (0, i))
    sums = (9, heads, 8, 2 * TILE)
    return kernel_call(
        partial(attend_back_kernel, heads),
        (
            struct((rows, TILE), bf16),
            struct((ext, TILE), bf16),
            struct((ext, TILE), bf16),
            struct(sums, f32),
        ),
        grid=(grid,),
        prefetch=1,
        ins=[
            tile, whole(k.shape), whole(v.shape), whole(diag.shape),
            turned, pl.BlockSpec((1, 8, heads * TILE), lambda i, *_: (i, 0, 0)),
            whole(d0.shape), whole(d1.shape), whole(d2.shape), whole(d3.shape),
        ],
        out_specs=(tile, whole((ext, TILE)), whole((ext, TILE)), whole(sums)),
        scratch=[
            pltpu.VMEM((9, TILE, heads * TILE), f32),
            pltpu.VMEM((9, TILE, heads * TILE), f32),
            pltpu.VMEM((width, ext), bf16),
            pltpu.VMEM((TILE, heads * TILE), bf16),
            pltpu.VMEM((TILE, heads * TILE), bf16),
            pltpu.VMEM((heads * TILE, TILE), bf16),
            pltpu.VMEM((heads * TILE, TILE), bf16),
            pltpu.VMEM((rows // 128, width, 128), bf16),
            pltpu.VMEM((width, TILE), f32),
            pltpu.VMEM((ext, TILE), f32),
            pltpu.VMEM((ext, TILE), f32),
        ],
        flops=10 * rows * 1280 * TILE * heads,
        moved=16 * ext * TILE,
        vmem=44,
        name="attend_back",
    )(info, *in_hbm(q, k, v, diag, oloc, lse), d0, d1, d2, d3)


MERGE_ROWS = pl.BlockSpec((FORM, 144, TILE), lambda *a: (0, 4, 0), pipeline_mode=pl.Buffered(1))


def merge_rows(packed, src, part):
    span = FORM // 4
    low = 48 * part
    return packed[pl.ds(src * span, span), low : low + 48, :].reshape(48 * span, TILE)


def merge_kernel(info, a0, a1, a2, a3, packed, gb, gain, mid, nrm):
    per = a0.shape[0]
    for t in range(per):
        rows = slice(128 * t, 128 * (t + 1))
        total = [gb[rows, TILE * part : TILE * (part + 1)] for part in range(3)]
        for rel, piece in ((0, a0[t]), (2, a2[t]), (1, a1[t]), (3, a3[t])):
            flat = piece.astype(f32).T.astype(bf16)
            for part in range(3):
                total[part] = total[part] + dot(flat, merge_rows(packed, info[0] ^ rel, part))
        v = jnp.concatenate(total, axis=1)
        mid[rows, :] = v
        r = lax.rsqrt(jnp.mean(v * v, axis=1, keepdims=True) + EPS)
        nrm[rows, :] = (v * r * gain[...]).astype(bf16)


def merge(me, a0, a1, a2, a3, packed, gb, gain):
    tok, d = gb.shape
    args = (a0, a1, a2, a3, packed, gb, gain)
    specs = [MERGE_ROWS if x is packed else whole(x.shape) for x in args]
    args = in_hbm(*args)
    return kernel_call(
        merge_kernel,
        (struct((tok, d), f32), struct((tok, d), bf16)),
        prefetch=1,
        ins=specs,
        out_specs=(whole((tok, d)), whole((tok, d))),
        flops=2 * tok * d * d,
        moved=12 * tok * d,
        vmem=20,
        name="merge",
    )(me, *args)


def feed_kernel(nt, gr, wg, wu, wd, out, dn, hid, dg, du, osum, dsum):
    j = pl.program_id(0)

    @pl.when(j == 0)
    def _():
        osum[...] = jnp.zeros_like(osum)
        dsum[...] = jnp.zeros_like(dsum)

    wgt = wg[...].reshape(FORM * 48, TILE)
    wut = wu[...].reshape(FORM * 48, TILE)
    gate = dot(nt[...], wgt)
    up = dot(nt[...], wut)
    dh = None
    wds = []
    for part in range(3):
        wdt = wd[:, 64 * part : 64 * (part + 1), :].reshape(TILE, TILE)
        wds.append(wdt)
        term = dot(gr[:, TILE * part : TILE * (part + 1)], wdt, ((1,), (1,)))
        dh = term if dh is None else dh + term
    sq = gate * gate
    th = jnp.tanh(GELU_C * gate * (1.0 + GELU_A * sq))
    half = 0.5 * (1.0 + th)
    act = gate * half
    slope = half + 0.5 * gate * (1.0 - th * th) * (GELU_C * (1.0 + 3.0 * GELU_A * sq))
    h = (act * up).astype(bf16)
    g = (dh * up * slope).astype(bf16)
    u = (dh * act).astype(bf16)
    hid[...] = h
    dg[...] = g
    du[...] = u
    for part in range(3):
        cols = slice(TILE * part, TILE * (part + 1))
        osum[:, cols] = osum[:, cols] + dot(h, wds[part])
    dsum[...] = dsum[...] + dot(g, wgt, ((1,), (1,))) + dot(u, wut, ((1,), (1,)))

    @pl.when(j == pl.num_programs(0) - 1)
    def _():
        out[...] = osum[...].astype(out.dtype)
        dn[...] = dsum[...].astype(dn.dtype)


def feed(nt, gr, packed, units, kind):
    tok, d = nt.shape
    col = pl.BlockSpec((tok, TILE), lambda j: (0, j))
    full = whole((tok, d))
    return kernel_call(
        feed_kernel,
        (struct((tok, d), kind), struct((tok, d), kind)) + (struct((tok, units), bf16),) * 3,
        grid=(units // TILE,),
        ins=[
            full,
            full,
            pl.BlockSpec((FORM, 48, TILE), lambda j: (0, j, 0)),
            pl.BlockSpec((FORM, 48, TILE), lambda j: (0, 4 + j, 0)),
            pl.BlockSpec((4, 192, TILE), lambda j: (j, 2, 0)),
        ],
        out_specs=(full, full, col, col, col),
        scratch=[pltpu.VMEM((tok, d), f32), pltpu.VMEM((tok, d), f32)],
        flops=12 * tok * d * units,
        moved=2 * packed.size + 10 * tok * d + 6 * tok * units,
        vmem=24,
        name="feed",
    )(nt, gr, packed, packed, packed)


def middle_kernel(info, mid, da, db, og, gain, packed, dmid, dlow, ga, gb, gsum):
    tok, d = mid.shape
    gsum[...] = jnp.zeros_like(gsum)

    def norm(t, _):
        at = pl.ds(pl.multiple_of(t * 16, 16), 16)
        v = mid[at, :]
        e = da[at, :] + db[at, :].astype(f32)
        r = lax.rsqrt(jnp.mean(v * v, axis=1, keepdims=True) + EPS)
        ge = gain[...] * e
        m = jnp.mean(ge * v, axis=1, keepdims=True)
        out = og[at, :].astype(f32) + r * ge - v * (r * r * r * m)
        dmid[at, :] = out
        dlow[at, :] = out.astype(bf16)
        part = e * v * r
        gsum[...] = gsum[...] + part[0:8] + part[8:16]
        return 0

    lax.fori_loop(0, tok // 16, norm, 0)
    for rel in range(4):
        out = None
        for part in range(3):
            cols = slice(TILE * part, TILE * (part + 1))
            term = dot(merge_rows(packed, info[0] ^ rel, part), dlow[:, cols], ((1,), (1,)))
            out = term if out is None else out + term
        low = out.astype(bf16)
        for t in range(tok // 128):
            ref = ga if rel < 2 else gb
            ref[rel % 2, t] = low[:, 128 * t : 128 * (t + 1)]


def middle(me, mid, da, db, og, gain, packed):
    tok, d = mid.shape
    args = (mid, da, db, og, gain, packed)
    sent = (2, tok // 128, d // 4, 128)
    shapes = [((tok, d), f32), ((tok, d), bf16), (sent, bf16), (sent, bf16), ((8, d), f32)]
    return kernel_call(
        middle_kernel,
        tuple(struct(*s) for s in shapes),
        prefetch=1,
        ins=[MERGE_ROWS if x is packed else whole(x.shape) for x in args],
        out_specs=tuple(whole(s[0]) for s in shapes),
        flops=2 * tok * d * d,
        moved=30 * tok * d,
        vmem=24,
        name="middle",
    )(me, mid, da, db, *in_hbm(og, gain, packed))


def merge_grad_kernel(info, a0, a1, a2, a3, dlow, keep, send):
    per = a0.shape[0]
    width = a0.shape[1]
    me = info[0]
    for rel in range(4):
        pieces = [(a0[t], a1[t], a2[t], a3[t])[rel] for t in range(per)]
        left = jnp.concatenate(pieces, axis=1)
        rows = pl.ds(pl.multiple_of((me ^ rel) * width, 64), width)
        out = dot(left, dlow[...])
        for part in range(4):
            cols = out[:, width * part : width * (part + 1)]
            far = me ^ part

            @pl.when(far % 2 == 0)
            def _():
                keep[far // 2, rows, :] = cols

            @pl.when(far % 2 == 1)
            def _():
                send[far // 2, rows, :] = cols.astype(bf16)


def merge_grad(info, a0, a1, a2, a3, dlow):
    tok, d = dlow.shape
    args = (*in_hbm(a0, a1, a2, a3), dlow)
    shape = (2, d, d // 4)
    return kernel_call(
        merge_grad_kernel,
        (struct(shape, f32), struct(shape, bf16)),
        prefetch=1,
        ins=[whole(x.shape) for x in args],
        out_specs=(whole(shape), whole(shape)),
        flops=2 * tok * d * d,
        moved=4 * tok * d + 3 * d * d,
        vmem=20,
        name="merge_grad",
    )(info, *args)


def weight_kernel(na, nb, ga, gb, ha, dga, dua, hb, dgb, dub, out, nt):
    j = pl.program_id(0)
    tok, d = na.shape

    @pl.when(j == 0)
    def _():
        nt[:, :tok] = na[...].astype(f32).T.astype(bf16)
        nt[:, tok:] = nb[...].astype(f32).T.astype(bf16)

    for base, left, right in ((0, dga, dgb), (384, dua, dub)):
        grad = (dot(nt[:, :tok], left[...]) + dot(nt[:, tok:], right[...])).astype(bf16)
        for part in range(TILE // 128):
            at = pl.multiple_of(base + 48 * ((TILE // 128) * j + part), 16)
            out[:, pl.ds(at, 48), :] = grad[:, 128 * part : 128 * (part + 1)].reshape(FORM, 48, 128)
    grad = dot(ha[...].astype(f32).T.astype(bf16), ga[...]) + dot(hb[...].astype(f32).T.astype(bf16), gb[...])
    grad = grad.astype(bf16)
    for part in range(d // 128):
        low = 768 + 64 * part
        out[pl.ds(4 * j, 4), low : low + 64, :] = grad[:, 128 * part : 128 * (part + 1)].reshape(4, 64, 128)


def weight_grads(na, nb, ga, gb, left, right):
    tok, d = na.shape
    units = left[0].shape[1]
    args = (na, nb, ga, gb, *left, *right)
    col = pl.BlockSpec((tok, TILE), lambda j: (0, j))
    shape = (FORM, 1152, 128)
    return kernel_call(
        weight_kernel,
        struct(shape, bf16),
        grid=(units // TILE,),
        ins=[whole(x.shape) for x in args[:4]] + [col] * 6,
        out_specs=whole(shape),
        scratch=[pltpu.VMEM((d, 2 * tok), bf16)],
        flops=6 * 2 * tok * d * units,
        moved=12 * tok * units + 16 * tok * d,
        vmem=28,
        name="weight_grads",
    )(*args)


def regroup(stacked, parts, groups):
    count, _, width = stacked.shape
    if count == groups:
        return stacked
    pieces, low = [], 0
    for blocks, rows in parts:
        piece = stacked[:, low : low + blocks * rows].reshape(count, blocks, rows, width)
        low += blocks * rows
        piece = jnp.transpose(piece, (1, 0, 2, 3)).reshape(blocks, groups, count * rows // groups, width)
        pieces.append(jnp.transpose(piece, (1, 0, 2, 3)).reshape(groups, blocks * count * rows // groups, width))
    return jnp.concatenate(pieces, axis=1)


def to_blocks(mat, width):
    rows, cols = mat.shape
    return jnp.transpose(mat.reshape(rows, cols // width, width), (1, 0, 2)).reshape(-1, width)


def from_blocks(stacked, rows):
    blocks, width = stacked.shape[0] // rows, stacked.shape[1]
    return jnp.transpose(stacked.reshape(blocks, rows, width), (1, 0, 2)).reshape(rows, blocks * width)


def flip(x, bit):
    return lax.ppermute(x, ULY, [(i, i ^ bit) for i in range(4)])


def ordered(core, mine, theirs, axis):
    first = jnp.where(core == 0, mine, theirs)
    second = jnp.where(core == 0, theirs, mine)
    return jnp.concatenate([first, second], axis=axis)


def local(
    n_ctx,
    byte_embed,
    query_weight,
    key_weight,
    value_weight,
    merge_weight,
    gate_weight,
    up_weight,
    down_weight,
    conv_weight,
    score_weight,
    attn_gain,
    ffn_gain,
    bias_table,
    doc_lengths,
    rel_bucket,
    out_grad,
):
    nb, d = byte_embed.shape
    tok = out_grad.shape[0]
    n_dev = n_ctx * 4
    groups = n_ctx * 2
    rows_dev = query_weight.shape[0]
    rows_ctx = 4 * rows_dev
    down_dev = down_weight.shape[0]
    heads = HEADS // 4
    width = heads * HEAD_DIM
    group_len = tok * 4
    ext = 2 * group_len
    ff = gate_weight.shape[1]
    unit = ff // n_dev
    ctx_at = lax.axis_index("ctx")
    row_at = lax.axis_index("ux")
    core = lax.axis_index("uc")
    uly_at = lax.axis_index(ULY)
    dev_at = lax.axis_index(RING)
    me = uly_at.astype(jnp.int32).reshape(1)

    up_pairs = [(i, i + 1) for i in range(n_dev - 1)]
    down_pairs = [(i + 1, i) for i in range(n_dev - 1)]
    lo = lax.ppermute(byte_embed[nb - 8 :], RING, up_pairs)
    hi = lax.ppermute(byte_embed[:8], RING, down_pairs)

    count = doc_lengths.shape[0]
    order = lax.broadcasted_iota(jnp.int32, (count, count), 0)
    before = lax.broadcasted_iota(jnp.int32, (count, count), 1)
    starts = jnp.sum(jnp.where(before < order, doc_lengths[None, :], 0), axis=1)
    limit = jnp.sum(doc_lengths)

    shape = (nb + 16, 128)
    here = dev_at * nb - 8 + lax.broadcasted_iota(jnp.int32, shape, 0)
    there = here + lax.broadcasted_iota(jnp.int32, shape, 1) - 2
    between = jnp.sum(
        ((starts[None, None, :] <= here[:, :, None]) != (starts[None, None, :] <= there[:, :, None])).astype(jnp.int32),
        axis=2,
    )
    msk = ((between == 0) & (there >= 0) & (there < limit)).astype(f32)

    cw, sw = conv_weight, score_weight[None, :]
    gain_one, gain_two = attn_gain[None, :], ffn_gain[None, :]

    qkv_own = jnp.stack(
        [w.reshape(rows_dev, 4, width) for w in (query_weight, key_weight, value_weight)], axis=2
    ).reshape(rows_dev, 4, 3 * width)
    doubling = rows_ctx % 16 == 0
    take = lambda x, at, dim: lax.dynamic_index_in_dim(x, at, dim, keepdims=False)
    if doubling:
        cols = jnp.transpose(qkv_own, (1, 0, 2)).reshape(2, 2, rows_dev, 3 * width)
        got = flip(take(cols, 1 - core, 1), 1)
        cols = ordered(core, take(cols, core, 1), got, 1)
        got = flip(take(cols, 1 - row_at, 0), 2)
        qkv_w = ordered(row_at, take(cols, row_at, 0), got, 0)[None]
    else:
        qkv_send = jnp.broadcast_to(
            jnp.transpose(qkv_own, (1, 0, 2))[None], (n_ctx, 4, rows_dev, 3 * width)
        ).reshape(n_dev, rows_dev, 3 * width)
        qkv_w = lax.all_to_all(qkv_send, RING, 0, 0, tiled=True).reshape(8, d // 8, 3 * width)

    codes = [0]
    if doubling:
        bits_left = [1 << i for i in range(n_ctx.bit_length() - 1)][::-1]

        def double(qkv_w, bit):
            got = lax.ppermute(qkv_w, "ctx", [(i, i ^ bit) for i in range(n_ctx)])
            return jnp.concatenate([qkv_w, got], axis=0)

        gbst, normed, conv, aw = gbst_forward(lo, byte_embed, hi, msk, cw, sw, gain_one)
        gate_in, up_in, merge_in = gate_weight, up_weight, merge_weight
        for i, bit in enumerate(bits_left):
            if i < len(bits_left) - 1:
                qkv_w = double(qkv_w, bit)
            codes = codes + [c ^ bit for c in codes]
            if i == 0:
                gate_in, up_in, merge_in, qkv_w, normed = lax.optimization_barrier(
                    (gate_in, up_in, merge_in, qkv_w, normed)
                )
        places = ctx_at ^ jnp.array(codes, jnp.int32)
    else:
        gbst, normed, conv, aw = gbst_forward(lo, byte_embed, hi, msk, cw, sw, gain_one)
        gate_in, up_in, merge_in = gate_weight, up_weight, merge_weight
        places = jnp.arange(8, dtype=jnp.int32)
    weight_info = jnp.concatenate([me, places.astype(jnp.int32)])
    chunk = jnp.concatenate([gate_in, up_in, merge_in], axis=1)
    chip = ordered(core, chunk, flip(chunk, 1), 0)

    def split(at):
        halves = [
            lax.dynamic_index_in_dim(
                chip[:, low : low + ff].reshape(2 * rows_dev, n_ctx, 2, 2 * unit), at, 2, keepdims=False
            ).reshape(2 * rows_dev, ff // 2)
            for low in (0, ff)
        ]
        return jnp.concatenate(halves + [chip[:, 2 * ff :]], axis=1)

    both = jnp.where(row_at == core, split(row_at), flip(split(1 - row_at), 2))
    packed_own = jnp.concatenate(
        [
            to_blocks(both[:, : ff // 2], TILE),
            to_blocks(both[:, ff // 2 : ff], TILE),
            to_blocks(down_weight, TILE),
            to_blocks(both[:, ff:], TILE),
        ],
        axis=0,
    )
    starts, limit, _ = lax.optimization_barrier((starts, limit, aw))

    tok_at = ctx_at * group_len - group_len // 2 + jnp.arange(ext, dtype=jnp.int32)
    tok_doc = jnp.sum((starts[None, :] <= 2 * tok_at[:, None]).astype(jnp.int32), axis=1) - 1
    tok_doc = jnp.where((tok_at >= 0) & (2 * tok_at < limit), tok_doc, -1)
    bits = count.bit_length()
    lane = jnp.arange(TILE, dtype=jnp.int32) - width

    def coded(docs, code, agree, value):
        bit_on = ((docs >> jnp.clip(code // 2, 0, 31)) & 1) == 1
        used = (code >= 0) & (code < 2 * bits)
        return jnp.where(used & ((bit_on == (code % 2 == 1)) == agree), value, 0.0).astype(bf16)

    code_k = coded(tok_doc[:, None], lane[None, :], True, 1.0)
    own_doc = tok_doc[group_len // 2 : group_len // 2 + group_len]
    code_q = coded(own_doc[:, None], lane[None, :], False, -BIG)
    tiles = group_len // TILE
    first = ctx_at * group_len + TILE * jnp.arange(tiles, dtype=jnp.int32)
    begin = jnp.max(jnp.where(starts[None, :] <= 2 * first[:, None], starts[None, :], 0), axis=1)
    last = 2 * (first + TILE - 1)
    end = jnp.min(jnp.where(starts[None, :] > last[:, None], starts[None, :], limit), axis=1)
    shift = group_len // 2 - ctx_at * group_len
    tile_lo = jnp.clip(((begin + 1) // 2 + shift) // TILE, 0, ext // TILE)
    tile_hi = jnp.clip(((end - 1) // 2 + shift) // TILE + 1, 0, ext // TILE)
    info = jnp.concatenate([tile_lo, tile_hi, me]).astype(jnp.int32)

    rel_count = rel_bucket.shape[0]
    diag_len = 2 * DOC_TOK + 2 * TILE
    bucket = jnp.pad(rel_bucket[::-1], (diag_len - TILE - rel_count, TILE), constant_values=-1)
    onehot = (bucket[None, :] == jnp.arange(NBUCK, dtype=jnp.int32)[:, None]).astype(f32)
    table_here = lax.dynamic_slice_in_dim(bias_table, uly_at * heads, heads, 1)
    diag = lax.dot_general(table_here, onehot, (((0,), (0,)), ((), ())), precision=highest)

    near = [(4 * c + u, 4 * (c + s) + u) for c in range(n_ctx) for u, s in ((0, -1), (1, -1), (2, 1), (3, 1)) if 0 <= c + s < n_ctx]
    far0 = lax.ppermute(normed, RING, near)
    own2 = flip(normed, 2)
    packed_own, far0, own2, qkv_w = lax.optimization_barrier((packed_own, far0, own2, qkv_w))
    packed = lax.all_gather(packed_own, ("ctx", "uc"), axis=0, tiled=False)
    packed = packed.reshape(groups, packed_own.shape[0], TILE)
    packed = regroup(
        packed,
        ((4, 2 * rows_dev), (4, 2 * rows_dev), (3, down_dev), (3, 2 * rows_dev)),
        FORM,
    )


    own1 = flip(normed, 1)
    own3 = flip(own2, 1)
    far2 = flip(far0, 2)
    far1 = flip(far0, 1)
    far3 = flip(far2, 1)
    grad_in, far3 = lax.optimization_barrier((out_grad, far3))
    grad_other = flip(grad_in, 2)
    if doubling:
        qkv_got = lax.ppermute(qkv_w, "ctx", [(i, i ^ bits_left[-1]) for i in range(n_ctx)])
        qkv_got, far2 = lax.optimization_barrier((qkv_got, far2))
        qkv_w = jnp.concatenate([qkv_w, qkv_got], axis=0)
    own = (normed, own1, own2, own3)
    far = (far0, far1, far2, far3)
    q, k, v, vt, wp = project(weight_info, own, far, qkv_w, code_q, code_k, heads)

    oa, ob, oloc, lse = attend(info, q, k, vt, diag, heads, tok)
    got2 = flip(ob, 2)
    got2, grad_other = lax.optimization_barrier((got2, grad_other))
    att = (oa[0], flip(oa[1], 1), got2[0], flip(got2[1], 1))
    mid, normed_two = merge(me, *att, packed, gbst, gain_two)

    normed_other = flip(normed_two, 2)
    out_a, dn_a, *left = feed(normed_two, out_grad, packed, ff // 2, f32)
    normed_other, dn_a = lax.optimization_barrier((normed_other, dn_a))
    out_b, dn_b, *right = feed(normed_other, grad_other, packed, ff // 2, bf16)
    dn_got = flip(dn_b, 2)
    grads = weight_grads(normed_two, normed_other, out_grad, grad_other, left, right)
    dn_got, grads = lax.optimization_barrier((dn_got, grads))
    parts16 = ((8, 48), (8, 48), (6, 64))
    grads = regroup(grads, parts16, groups)
    summed = lax.psum_scatter(grads, ("ctx", "uc"), scatter_dimension=0, tiled=False)
    dmid, dlow, ga, gb2, ffn_sum = middle(me, mid, dn_a, dn_got, out_grad, gain_two, packed)
    back2 = flip(gb2, 2)
    back1 = flip(ga[1], 1)
    back1, dlow = lax.optimization_barrier((back1, dlow))
    keep_m, send_m = merge_grad(me, *att, dlow)
    recv_m = flip(send_m, 1)
    back = (ga[0], back1, back2[0], flip(back2[1], 1))
    mid_m = (keep_m[1] + recv_m[1].astype(f32)).astype(bf16)

    out_b, *back = lax.optimization_barrier((out_b, *back))
    got_m = flip(mid_m, 2)
    out_got = flip(out_b, 2)
    dq, dk, dv, sums = attend_back(info, q, k, v, diag, oloc, lse, *back, heads)
    out_got, got_m, dk = lax.optimization_barrier((out_got, got_m, dk))
    layer_out = (mid + out_a + out_got.astype(f32)).astype(bf16)
    grad_info = jnp.concatenate([me, jnp.arange(8, dtype=jnp.int32)])
    hk0, hk2, hs1, hs3 = project_back(True, me, dq, dk, dv, wp)
    h_mid = (hk2 + flip(hs3, 1).astype(f32)).astype(bf16)
    h_mid, dq_g = lax.optimization_barrier((h_mid, dq))
    h_got2 = flip(h_mid, 2)
    part = project_grad(grad_info, own, far, dq_g, dk, dv, keep_m, recv_m, got_m, 8)
    dq_p, part, h_got2, summed = lax.optimization_barrier((dq_g, part, h_got2, summed))
    ok0, ok2, os1, os3 = project_back(False, me, dq_p, dk, dv, wp)
    part = lax.psum_scatter(part.reshape(n_ctx, rows_ctx, 4 * width), "ctx", scatter_dimension=0, tiled=False)
    got = lax.all_to_all(part.reshape(4, rows_dev, 4 * width), ULY, 0, 0, tiled=True)
    h_got1 = flip(hs1, 1)
    o_got1 = flip(os1, 1)
    o_mid = (ok2 + flip(os3, 1).astype(f32)).astype(bf16)
    h_sum = (hk0 + h_got1.astype(f32) + h_got2.astype(f32)).astype(bf16)
    h_sum, o_mid = lax.optimization_barrier((h_sum, o_mid))
    h_back = lax.ppermute(h_sum, RING, [(b, a) for a, b in near])
    o_got2 = flip(o_mid, 2)
    o_sum = ok0 + o_got1.astype(f32) + o_got2.astype(f32)

    sums, _ = lax.optimization_barrier((sums, h_sum))
    twice = jnp.concatenate([sums, sums], axis=3)
    moved = sum(twice[:, :, r, r + TILE : r + 3 * TILE] for r in range(8))
    diag_parts = jnp.transpose(moved, (1, 0, 2))
    count_t = diag_parts.shape[1]
    low = diag_parts[:, :, :TILE].reshape(heads, count_t * TILE)
    high = diag_parts[:, :, TILE:].reshape(heads, count_t * TILE)
    diag_grad = jnp.pad(low, ((0, 0), (0, TILE))) + jnp.pad(high, ((0, 0), (TILE, 0)))
    table_local = lax.dot_general(onehot, diag_grad, (((1,), (1,)), ((), ())), precision=highest)
    table_grad = lax.dynamic_update_slice(jnp.zeros((NBUCK, HEADS), f32), table_local, (0, uly_at * heads))

    eg, small = gbst_backward(
        o_sum, h_back, gbst, dmid, gain_one, conv, aw, lo, byte_embed, hi, msk, cw, sw
    )
    from_prev = lax.ppermute(eg[nb + 8 :], RING, up_pairs)
    from_next = lax.ppermute(eg[:8], RING, down_pairs)
    main = eg[8 : nb + 8]
    embed_grad = jnp.concatenate(
        [main[:8] + from_prev, main[8 : nb - 8], main[nb - 8 :] + from_next], axis=0
    )

    rest = jnp.concatenate(
        [jnp.sum(ffn_sum, axis=0, keepdims=True), jnp.pad(table_grad.reshape(1, -1), ((0, 0), (0, d - NBUCK * HEADS)))],
        axis=0,
    )
    total = jnp.concatenate([small, jnp.pad(rest, ((0, 6), (0, 0)))], axis=0)
    for bit in (1, 2):
        total = total + flip(total, bit)
    bit = 1
    while bit < n_ctx:
        total = total + lax.ppermute(total, "ctx", [(i, i ^ bit) for i in range(n_ctx)])
        bit *= 2

    got, total = lax.optimization_barrier((got, total))
    query_grad, key_grad, value_grad, merge_g = spread(got)

    rows2 = 2 * rows_dev
    down_grad = from_blocks(summed[16 * rows2 :], down_dev).astype(f32)
    mine = jnp.concatenate(
        [from_blocks(summed[: 8 * rows2], rows2), from_blocks(summed[8 * rows2 : 16 * rows2], rows2)], axis=1
    )
    theirs = flip(mine, 2)
    sets = [jnp.where(row_at == at, mine, theirs).reshape(rows2, 2, n_ctx, 1, 2 * unit) for at in (0, 1)]
    full = jnp.concatenate(sets, axis=3).reshape(2, rows_dev, 2 * ff)
    given = flip(lax.dynamic_index_in_dim(full, 1 - core, 0, keepdims=False), 1)
    kept = lax.dynamic_index_in_dim(full, core, 0, keepdims=False)
    final = jnp.where(row_at == core, kept, given).astype(f32)
    return (
        layer_out,
        embed_grad,
        query_grad,
        key_grad,
        value_grad,
        merge_g,
        final[:, :ff],
        final[:, ff:],
        down_grad,
        total[:CONV],
        total[5],
        total[6],
        total[8],
        total[9, : NBUCK * HEADS].reshape(NBUCK, HEADS),
    )


def solution(mesh):
    n_ctx = mesh.shape["ctx"]
    inner = Mesh(mesh.devices.reshape(n_ctx, 2, 2), RING)
    row = P(RING, None)
    return jax.shard_map(
        partial(local, n_ctx),
        mesh=inner,
        in_specs=(row,) * 8 + (P(),) * 7 + (row,),
        out_specs=(row,) * 9 + (P(),) * 5,
        check_vma=False,
    )
```
